32 devices in a mesh: dp: 4 (over z), context: 8 (over y, x, core).
Axes of the slice: x: 2, y: 2, z: 4, core: 2. Of those that a mesh axis runs over, the one named last changes fastest.
Arguments:
- inputs: float32 [4096, 2560], P(('dp', 'context')), may hold values from -6 to 6
- segment_ids: int32 [4, 1024], P('dp'), may hold values from 0 to 5, never falling along the last dimension, each value on 1 to 512 neighbouring positions
- first_gain: bfloat16 [2560], P(('dp', 'context')), may hold values from 0.5 to 1.5
- gelu_in_w: bfloat16 [2560, 2560], P(('dp', 'context')), may hold values from -0.125 to 0.125
- linear_in_w: bfloat16 [2560, 2560], P(('dp', 'context')), may hold values from -0.125 to 0.125
- conv_weight: bfloat16 [4, 2560], P(None, ('dp', 'context')), may hold values from -3 to 3
- conv_bias: bfloat16 [2560], P(('dp', 'context')), may hold values from -3 to 3
- recur_gate_w: bfloat16 [2560, 256], P(('dp', 'context')), may hold values from -0.375 to 0.375
- recur_gate_b: bfloat16 [2560], P(('dp', 'context')), may hold values from -4 to 4
- input_gate_w: bfloat16 [2560, 256], P(('dp', 'context')), may hold values from -0.375 to 0.375
- input_gate_b: bfloat16 [2560], P(('dp', 'context')), may hold values from -4 to 4
- decay_param: bfloat16 [2560], P(('dp', 'context')), may hold values from -13 to -4
- out_proj_w: bfloat16 [2560, 2560], P(('dp', 'context')), may hold values from -0.5 to 0.5
- second_gain: bfloat16 [2560], P(('dp', 'context')), may hold values from 0.5 to 1.5
- mlp_gate_w: bfloat16 [2560, 7680], P(('dp', 'context')), may hold values from -0.125 to 0.125
- mlp_up_w: bfloat16 [2560, 7680], P(('dp', 'context')), may hold values from -0.125 to 0.125
- mlp_down_w: bfloat16 [7680, 2560], P(('dp', 'context')), may hold values from -0.0625 to 0.0625
- out_grad: float32 [4096, 2560], P(('dp', 'context')), may hold values from -6 to 6
Outputs:
- output: float32 [4096, 2560], P(('dp', 'context'))
- input_grad: float32 [4096, 2560], P(('dp', 'context'))
- grad_first_gain: float32 [2560], P(('dp', 'context'))
- grad_gelu_in_w: float32 [2560, 2560], P('dp', 'context')
- grad_linear_in_w: float32 [2560, 2560], P('dp', 'context')
- grad_conv_weight: float32 [4, 2560], P(None, ('dp', 'context'))
- grad_conv_bias: float32 [2560], P(('dp', 'context'))
- grad_recur_gate_w: float32 [2560, 256], P(('dp', 'context'))
- grad_recur_gate_b: float32 [2560], P(('dp', 'context'))
- grad_input_gate_w: float32 [2560, 256], P(('dp', 'context'))
- grad_input_gate_b: float32 [2560], P(('dp', 'context'))
- grad_decay_param: float32 [2560], P(('dp', 'context'))
- grad_out_proj_w: float32 [2560, 2560], P('dp', 'context')
- grad_second_gain: float32 [2560], P(('dp', 'context'))
- grad_mlp_gate_w: float32 [2560, 7680], P('dp', 'context')
- grad_mlp_up_w: float32 [2560, 7680], P('dp', 'context')
- grad_mlp_down_w: float32 [7680, 2560], P('context', 'dp')
The draws below stay inside these ranges and needn't reach their ends.
Inputs may be any that keep to these rules, and one draw needn't show every extreme that they name: `segment_ids`: within each sequence the ids never fall; each of the 6 ids names 1 to 512 positions, and one names exactly 512.
All inputs are finite; a program needn't handle non-finite values.
Results may differ from the reference program's by a relative error of at most 0.013.
Values may be sent and summed in bfloat16 or wider, within the bound.
A program may use at most 512 MiB of HBM per device.

```python
import math
import jax
import jax.numpy as jnp
import numpy as np
from jax import lax

D = 2560
R = 2560
FF = 7680
HEADS = 10
CONV = 4
BW = 256
LEN = 1024
SEQS = 4
TOKENS = 4096
DOCS = 6


def level_of(stream_key, dims, split, smallest, largest):
    level, own = 1.0, jax.random.fold_in(stream_key, 6)
    for axis_at, shards_of in split:
        steps = jnp.exp(jax.random.uniform(jax.random.fold_in(own, axis_at), (shards_of,), jnp.float32, smallest / len(split), largest / len(split)))
        level = level * jnp.repeat(steps, dims[axis_at] // shards_of).reshape([-1 if axis == axis_at else 1 for axis in range(len(dims))])
    return level


def split_up(amount, total, reach, slope):
    weights = [(1 << 20) // math.isqrt(rank ** slope) + 1 for rank in range(2, amount + 1)]
    surplus, given = total - reach - (amount - 1), [1] * (amount - 1)
    while surplus > 0:
        movable = [i for i in range(amount - 1) if given[i] < reach]
        whole, budget = sum([weights[i] for i in movable]), surplus
        for i in movable:
            more = min(reach - given[i], max(1, budget * weights[i] // whole), surplus)
            given[i] = given[i] + more
            surplus = surplus - more
    return np.array([reach] + given)


def uneven(rng, number_of, total, most, lean):
    if number_of == 2:
        one = jax.random.randint(rng, (), max(1, total - most), min(most, total - 1) + 1)
        return jnp.stack([one, total - one])
    tallies = jnp.asarray(split_up(number_of, total, most, lean), jnp.int32)
    pairs = (number_of - 1) // 2
    giver, taker = tallies[1:1 + 2 * pairs:2], tallies[2:2 + 2 * pairs:2]
    room = jnp.minimum(giver - 1, most - taker)
    moved = jax.random.randint(jax.random.fold_in(rng, 1), (pairs,), 0, 1 << 20) % (room + 1)
    tallies = tallies.at[1:1 + 2 * pairs:2].set(giver - moved).at[2:2 + 2 * pairs:2].set(taker + moved)
    return tallies[jax.random.permutation(jax.random.fold_in(rng, 2), number_of)]


def bell_draw(rng, shape, scale, bound, shards=(), held_as=jnp.bfloat16):
    drawn = scale * jax.random.normal(rng, shape, jnp.float32)
    if shards:
        drawn = drawn * level_of(rng, shape, shards, -0.22, 0.18)
    return jnp.clip(drawn, -bound, bound).astype(held_as)


def setup_inputs(seed: int = 0) -> dict:
    key_list = jax.random.split(jax.random.key(seed), 19)
    inputs = bell_draw(key_list[0], (TOKENS, D), 1.0, 6.0, ((0, 32),), jnp.float32)
    segment_ids = jax.vmap(lambda own: jnp.searchsorted(jnp.cumsum(uneven(own, DOCS, LEN, LEN // 2, 2)), jnp.arange(LEN), side="right"))(jax.random.split(key_list[1], SEQS)).reshape((SEQS, LEN)).astype(jnp.int32)
    first_gain = jnp.clip(1.0 + 0.1 * jax.random.normal(key_list[2], (D,), jnp.float32), 0.5, 1.5).astype(jnp.bfloat16)
    gelu_in_w = bell_draw(key_list[3], (D, R), D ** -0.5, 0.125, ((0, 32),))
    linear_in_w = bell_draw(key_list[4], (D, R), D ** -0.5, 0.125, ((0, 32),))
    conv_weight = bell_draw(key_list[5], (CONV, R), CONV ** -0.5, 3.0, ((1, 32),))
    conv_bias = bell_draw(key_list[6], (R,), 0.5, 3.0, ((0, 32),))
    recur_gate_w = bell_draw(key_list[7], (R, BW), BW ** -0.5, 0.375, ((0, 32),))
    recur_gate_b = bell_draw(key_list[8], (R,), 1.0, 4.0, ((0, 32),))
    input_gate_w = bell_draw(key_list[9], (R, BW), BW ** -0.5, 0.375, ((0, 32),))
    input_gate_b = bell_draw(key_list[10], (R,), 1.0, 4.0, ((0, 32),))
    decay_param = jnp.clip(-13.0 + 9.0 * jax.random.uniform(key_list[11], (R,), jnp.float32) ** level_of(key_list[11], (R,), ((0, 32),), -0.2, 0.2), -13.0, -4.0).astype(jnp.bfloat16)
    out_proj_w = bell_draw(key_list[12], (R, D), (R // 16) ** -0.5, 0.5, ((0, 32),))
    second_gain = jnp.clip(1.0 + 0.1 * jax.random.normal(key_list[13], (D,), jnp.float32), 0.5, 1.5).astype(jnp.bfloat16)
    mlp_gate_w = bell_draw(key_list[14], (D, FF), D ** -0.5, 0.125, ((0, 32),))
    mlp_up_w = bell_draw(key_list[15], (D, FF), D ** -0.5, 0.125, ((0, 32),))
    mlp_down_w = bell_draw(key_list[16], (FF, D), FF ** -0.5, 0.0625, ((0, 32),))
    out_grad = bell_draw(key_list[17], (TOKENS, D), 1.0, 6.0, ((0, 32),), jnp.float32)
    return {"inputs": inputs, "segment_ids": segment_ids, "first_gain": first_gain, "gelu_in_w": gelu_in_w, "linear_in_w": linear_in_w, "conv_weight": conv_weight, "conv_bias": conv_bias, "recur_gate_w": recur_gate_w, "recur_gate_b": recur_gate_b, "input_gate_w": input_gate_w, "input_gate_b": input_gate_b, "decay_param": decay_param, "out_proj_w": out_proj_w, "second_gain": second_gain, "mlp_gate_w": mlp_gate_w, "mlp_up_w": mlp_up_w, "mlp_down_w": mlp_down_w, "out_grad": out_grad}


@jax.custom_vjp
def low(v):
    return lax.optimization_barrier(v.astype(jnp.bfloat16)).astype(jnp.float32)

@jax.custom_vjp
def low_back(v):
    return v

def low_keep(v):
    return (low(v), None)

def low_pass(kept, grad):
    return (grad,)

def back_keep(v):
    return (v, None)

def back_low(kept, grad):
    return (low(grad),)
low.defvjp(low_keep, low_pass)
low_back.defvjp(back_keep, back_low)

def rms_scale(values, gain_vec):
    return values * lax.rsqrt(lax.optimization_barrier(jnp.mean(values * values, axis=-1, keepdims=True)) + 1e-06) * gain_vec

def exact_dot(lhs_rows, rhs_rows):
    return jnp.dot(lhs_rows, rhs_rows, precision=lax.Precision.HIGHEST)

def block_dot(values, weight):
    row_count = values.shape[0]
    result = jnp.einsum('thi,hio->tho', values.reshape(row_count, HEADS, BW), weight.reshape(HEADS, BW, BW), precision=lax.Precision.HIGHEST)
    return result.reshape(row_count, HEADS * BW)

def conv_mix(x_rows, seg_line, conv_w, conv_b):
    channels = x_rows.shape[1]
    summed = conv_b[None, :] + conv_w[0][None, :] * x_rows
    for offset in range(1, CONV):
        shifted = jnp.concatenate([jnp.zeros((offset, channels), jnp.float32), x_rows[:-offset]], axis=0)
        earlier_ids = jnp.concatenate([jnp.full((offset,), -1, jnp.int32), seg_line[:-offset]])
        same_doc = (earlier_ids == seg_line).astype(jnp.float32)
        summed = summed + conv_w[offset][None, :] * shifted * same_doc[:, None]
    return summed

def gate_values(recur_in, input_in, conv_out, decay_vals, is_reset):
    rec_gate = jax.nn.sigmoid(recur_in)
    in_gate = jax.nn.sigmoid(input_in)
    log_decay = -8.0 * jax.nn.softplus(decay_vals) * rec_gate
    decays = jnp.where(is_reset, 0.0, jnp.exp(log_decay))
    in_scale = jnp.where(is_reset, 1.0, jnp.sqrt(-jnp.expm1(2.0 * log_decay)))
    return (decays, in_scale * in_gate * conv_out)

def combine_pair(earlier, latter):
    return (earlier[0] * latter[0], latter[0] * earlier[1] + latter[1])

def block_forward(x_rows, seg_line, params):
    first_gain, gelu_in_w, linear_in_w, conv_weight, conv_bias, recur_gate_w, recur_gate_b, input_gate_w, input_gate_b, decay_param, out_proj_w, second_gain, mlp_gate_w, mlp_up_w, mlp_down_w = params
    normed = low(rms_scale(x_rows, first_gain))
    gelu_pre = low_back(exact_dot(normed, gelu_in_w))
    linear_out = low(low_back(exact_dot(normed, linear_in_w)))
    conv_out = conv_mix(linear_out, seg_line, conv_weight, conv_bias)
    conv_low = low(conv_out)
    recur_in = low_back(block_dot(conv_low, recur_gate_w)) + recur_gate_b
    input_in = low_back(block_dot(conv_low, input_gate_w)) + input_gate_b
    starts = jnp.concatenate([jnp.ones((1,), jnp.int32), (seg_line[1:] != seg_line[:-1]).astype(jnp.int32)])
    is_reset = starts[:, None] > 0
    decays, driven = gate_values(recur_in, input_in, conv_out, decay_param, is_reset)
    scanned = lax.associative_scan(combine_pair, (decays, driven), axis=0)
    states = scanned[1]
    mixed_rows = low(jax.nn.gelu(gelu_pre) * states)
    hidden = x_rows + low_back(exact_dot(mixed_rows, out_proj_w))
    second_normed = low(rms_scale(hidden, second_gain))
    gate_pre = low_back(exact_dot(second_normed, mlp_gate_w))
    up_pre = low_back(exact_dot(second_normed, mlp_up_w))
    activation = low(jax.nn.gelu(gate_pre) * up_pre)
    return hidden + low_back(exact_dot(activation, mlp_down_w))

def reference(inputs, segment_ids, first_gain, gelu_in_w, linear_in_w, conv_weight, conv_bias, recur_gate_w, recur_gate_b, input_gate_w, input_gate_b, decay_param, out_proj_w, second_gain, mlp_gate_w, mlp_up_w, mlp_down_w, out_grad):
    params = tuple((weight_arr.astype(jnp.float32) for weight_arr in (first_gain, gelu_in_w, linear_in_w, conv_weight, conv_bias, recur_gate_w, recur_gate_b, input_gate_w, input_gate_b, decay_param, out_proj_w, second_gain, mlp_gate_w, mlp_up_w, mlp_down_w)))
    x_seqs = inputs.astype(jnp.float32).reshape(SEQS, LEN, D)
    cot_seqs = out_grad.astype(jnp.float32).reshape(SEQS, LEN, D)

    def total_forward(x_all, weights):
        return lax.map(lambda seq_pair: block_forward(seq_pair[0], seq_pair[1], weights), (x_all, segment_ids))
    outputs, pull_back = jax.vjp(total_forward, x_seqs, params)
    x_grad, weight_grads = pull_back(cot_seqs)
    return (outputs.reshape(TOKENS, D), x_grad.reshape(TOKENS, D), weight_grads[0], weight_grads[1], weight_grads[2], weight_grads[3], weight_grads[4], weight_grads[5], weight_grads[6], weight_grads[7], weight_grads[8], weight_grads[9], weight_grads[10], weight_grads[11], weight_grads[12], weight_grads[13], weight_grads[14])
```

```python
import functools

import jax
import jax.numpy as jnp
from jax import lax
from jax.experimental import pallas as pl
from jax.experimental.pallas import tpu as pltpu
from jax.sharding import Mesh
from jax.sharding import PartitionSpec as P

HEADS = 10
CONV = 4
CHUNK = 256
BF = jnp.bfloat16
F32 = jnp.float32
DP = ("hi", "lo")
CTX = ("cxy", "core")
CUBE = ("lo", "cxy", "core")
EVERY = ("hi", "lo", "cxy", "core")
SWAP = [(0, 1), (1, 0)]


def dot(a, b, ca, cb):
    return lax.dot_general(a, b, (((ca,), (cb,)), ((), ())), preferred_element_type=F32)


def rms_back(values, gain, grad):
    r = lax.rsqrt(jnp.mean(values * values, axis=-1, keepdims=True) + 1e-06)
    q = grad * gain
    gain_grad = jnp.sum(grad * values * r, axis=0)
    value_grad = r * q - r * r * r * values * jnp.mean(q * values, axis=-1, keepdims=True)
    return value_grad, gain_grad


def gelu_parts(x):
    c0 = 0.7978845608028654
    c1 = 0.044715
    x2 = x * x
    th = jnp.tanh(c0 * x * (1.0 + c1 * x2))
    half = 0.5 * (1.0 + th)
    slope = half + 0.5 * x * (1.0 - th * th) * c0 * (1.0 + 3.0 * c1 * x2)
    return x * half, slope


def minus_expm1(x):
    series = 1.0 + x * (1.0 / 8.0)
    for n in range(7, 1, -1):
        series = 1.0 + x * (1.0 / n) * series
    return jnp.where(x > -0.5, -x * series, 1.0 - jnp.exp(x))


def forward_kernel(
    lin_ref, gpre_ref, meta_ref, vec_ref, rw_ref, iw_ref,
    mixed_ref, prev_ref, conv_ref, rec_ref, inp_ref,
    xbuf, dec_s, drv_s, st_s, carry,
):
    rows = lin_ref.shape[0]
    first = pl.program_id(1) == 0

    @pl.when(first)
    def _():
        xbuf[0:8, :] = jnp.zeros((8, xbuf.shape[1]), F32)
        carry[...] = jnp.zeros_like(carry)

    x = lin_ref[...].astype(F32)
    xbuf[8 : 8 + rows, :] = x
    conv = vec_ref[4:5, :] + vec_ref[0:1, :] * x
    for k in range(1, CONV):
        conv = conv + vec_ref[k : k + 1, :] * (xbuf[8 - k : 8 - k + rows, :] * meta_ref[:, k : k + 1])
    xbuf[0:8, :] = x[rows - 8 : rows, :]
    low = conv.astype(BF)
    rec = jax.nn.sigmoid(jnp.dot(low, rw_ref[...], preferred_element_type=F32) + vec_ref[5:6, :])
    inp = jax.nn.sigmoid(jnp.dot(low, iw_ref[...], preferred_element_type=F32) + vec_ref[6:7, :])
    reset = meta_ref[:, 0:1] > 0.5
    log_decay = vec_ref[7:8, :] * rec
    scale = jnp.where(reset, 1.0, jnp.sqrt(minus_expm1(2.0 * log_decay)))
    dec_s[...] = jnp.where(reset, 0.0, jnp.exp(log_decay))
    drv_s[...] = scale * inp * conv
    conv_ref[...] = conv
    rec_ref[...] = rec
    inp_ref[...] = inp
    width = carry.shape[1]
    row = lax.broadcasted_iota(jnp.int32, (8, width), 0)

    def step(i, held):
        at = pl.multiple_of(i * 8, 8)
        a = dec_s[pl.ds(at, 8), :]
        b = drv_s[pl.ds(at, 8), :]
        for s in (1, 2, 4):
            keep = row >= s
            b = a * jnp.where(keep, pltpu.roll(b, s, 0), 0.0) + b
            a = a * jnp.where(keep, pltpu.roll(a, s, 0), 1.0)
        h = a * held + b
        st_s[pl.ds(at, 8), :] = h
        prev_ref[pl.ds(at, 8), :] = jnp.where(row == 0, held, pltpu.roll(h, 1, 0))
        return jnp.broadcast_to(h[7:8, :], (8, width))

    carry[...] = lax.fori_loop(0, rows // 8, step, carry[...], unroll=4)
    gel, _ = gelu_parts(gpre_ref[...])
    mixed_ref[...] = (gel * st_s[...] * vec_ref[8:9, :]).astype(BF)


def backward_kernel(
    mg_ref, gpre_ref, conv_ref, rec_ref, inp_ref, prev_ref, lin_ref, meta_ref, vec_ref, rw_ref, iw_ref,
    glow_ref, llow_ref, rwg_ref, iwg_ref, sum_ref,
    dec_s, sg_s, lam_s, gbuf, carry,
):
    rows = lin_ref.shape[0]
    first = pl.program_id(1) == 0

    @pl.when(first)
    def _():
        carry[...] = jnp.zeros_like(carry)
        for k in range(CONV - 1):
            gbuf[k, rows : rows + 8, :] = jnp.zeros((8, gbuf.shape[2]), F32)
        rwg_ref[...] = jnp.zeros_like(rwg_ref)
        iwg_ref[...] = jnp.zeros_like(iwg_ref)
        sum_ref[...] = jnp.zeros_like(sum_ref)

    mg = mg_ref[...]
    conv = conv_ref[...]
    rec = rec_ref[...]
    inp = inp_ref[...]
    prev = prev_ref[...]
    own = vec_ref[8:9, :]
    gel, slope = gelu_parts(gpre_ref[...])
    reset = meta_ref[:, 0:1] > 0.5
    log_decay = vec_ref[7:8, :] * rec
    scale = jnp.where(reset, 1.0, jnp.sqrt(minus_expm1(2.0 * log_decay)))
    dec = jnp.where(reset, 0.0, jnp.exp(log_decay))
    gated = scale * inp
    states = dec * prev + gated * conv
    glow_ref[...] = (mg * states * slope * own).astype(BF)
    dec_s[...] = dec
    sg_s[...] = mg * gel
    width = carry.shape[1]
    row = lax.broadcasted_iota(jnp.int32, (8, width), 0)
    blocks = rows // 8

    def step(i, held):
        at = pl.multiple_of((blocks - 1 - i) * 8, 8)
        a = dec_s[pl.ds(at, 8), :]
        g = sg_s[pl.ds(at, 8), :]
        b = a * g
        for s in (1, 2, 4):
            keep = row < 8 - s
            b = a * jnp.where(keep, pltpu.roll(b, 8 - s, 0), 0.0) + b
            a = a * jnp.where(keep, pltpu.roll(a, 8 - s, 0), 1.0)
        m = a * held + b
        lam_s[pl.ds(at, 8), :] = g + jnp.where(row == 7, held, pltpu.roll(m, 7, 0))
        return jnp.broadcast_to(m[0:1, :], (8, width))

    carry[...] = lax.fori_loop(0, blocks, step, carry[...], unroll=4)
    lam = lam_s[...]
    conv_gate = lam * gated
    dinp = lam * scale * conv
    dscale = lam * inp * conv
    dlog = jnp.where(reset, 0.0, (lam * prev - dscale * dec / scale) * dec)
    recur_grad = vec_ref[7:8, :] * dlog * rec * (1.0 - rec)
    input_grad = dinp * inp * (1.0 - inp)
    rlow = recur_grad.astype(BF)
    ilow = input_grad.astype(BF)
    low = conv.astype(BF)
    rwg_ref[...] += dot(low, rlow, 0, 0)
    iwg_ref[...] += dot(low, ilow, 0, 0)
    conv_grad = conv_gate + dot(rlow, rw_ref[...], 1, 1) + dot(ilow, iw_ref[...], 1, 1)
    lin = lin_ref[...].astype(F32)
    linear_grad = vec_ref[0:1, :] * conv_grad

    def add(at, value):
        sum_ref[at : at + 1, :] += jnp.sum(value, axis=0, keepdims=True)

    add(0, conv_grad * lin)
    for k in range(1, CONV):
        masked = conv_grad * meta_ref[:, k : k + 1]
        gbuf[k - 1, 0:rows, :] = masked
        moved = gbuf[k - 1, k : k + rows, :]
        gbuf[k - 1, rows : rows + 8, :] = masked[0:8, :]
        linear_grad = linear_grad + vec_ref[k : k + 1, :] * moved
        add(k, moved * lin)
    llow_ref[...] = (linear_grad * own).astype(BF)
    add(4, conv_grad)
    add(5, recur_grad)
    add(6, input_grad)
    add(7, vec_ref[9:10, :] * rec * dlog)


def forward_call(lin, gpre, meta, vecs, rw, iw):
    tokens, win = lin.shape
    bw = rw.shape[1]
    rows = min(CHUNK, tokens)
    grid = (win // bw, tokens // rows)
    tok = pl.BlockSpec((rows, bw), lambda h, j: (j, h))
    mspec = pl.BlockSpec((rows, meta.shape[1]), lambda h, j: (j, 0))
    vspec = pl.BlockSpec((vecs.shape[0], bw), lambda h, j: (0, h))
    wspec = pl.BlockSpec((bw, bw), lambda h, j: (h, 0))
    full = jax.ShapeDtypeStruct((tokens, win), F32)
    return pl.pallas_call(
        forward_kernel,
        grid=grid,
        in_specs=[tok, tok, mspec, vspec, wspec, wspec],
        out_specs=[tok] * 5,
        out_shape=[jax.ShapeDtypeStruct((tokens, win), BF), full, full, full, full],
        scratch_shapes=[
            pltpu.VMEM((rows + 8, bw), F32),
            pltpu.VMEM((rows, bw), F32),
            pltpu.VMEM((rows, bw), F32),
            pltpu.VMEM((rows, bw), F32),
            pltpu.VMEM((8, bw), F32),
        ],
        compiler_params=pltpu.CompilerParams(vmem_limit_bytes=40 << 20),
        cost_estimate=pl.CostEstimate(
            flops=tokens * win * (4 * bw + 100), bytes_accessed=tokens * win * 24, transcendentals=tokens * win * 6
        ),
        name="recur_forward",
    )(lin, gpre, meta, vecs, rw, iw)


def backward_call(mg, gpre, conv, rec, inp, prev, lin, meta, vecs, rw, iw):
    tokens, win = lin.shape
    bw = rw.shape[1]
    rows = min(CHUNK, tokens)
    steps = tokens // rows
    grid = (win // bw, steps)
    tok = pl.BlockSpec((rows, bw), lambda h, j: (steps - 1 - j, h))
    mspec = pl.BlockSpec((rows, meta.shape[1]), lambda h, j: (steps - 1 - j, 0))
    vspec = pl.BlockSpec((vecs.shape[0], bw), lambda h, j: (0, h))
    wspec = pl.BlockSpec((bw, bw), lambda h, j: (h, 0))
    sspec = pl.BlockSpec((8, bw), lambda h, j: (0, h))
    lows = jax.ShapeDtypeStruct((tokens, win), BF)
    wgrad = jax.ShapeDtypeStruct((win, bw), F32)
    return pl.pallas_call(
        backward_kernel,
        grid=grid,
        in_specs=[tok] * 7 + [mspec, vspec, wspec, wspec],
        out_specs=[tok, tok, wspec, wspec, sspec],
        out_shape=[lows, lows, wgrad, wgrad, jax.ShapeDtypeStruct((8, win), F32)],
        scratch_shapes=[
            pltpu.VMEM((rows, bw), F32),
            pltpu.VMEM((rows, bw), F32),
            pltpu.VMEM((rows, bw), F32),
            pltpu.VMEM((CONV - 1, rows + 8, bw), F32),
            pltpu.VMEM((8, bw), F32),
        ],
        compiler_params=pltpu.CompilerParams(vmem_limit_bytes=40 << 20),
        cost_estimate=pl.CostEstimate(
            flops=tokens * win * (8 * bw + 150), bytes_accessed=tokens * win * 30, transcendentals=tokens * win * 6
        ),
        name="recur_backward",
    )(mg, gpre, conv, rec, inp, prev, lin, meta, vecs, rw, iw)


def exchange(value, axes):
    return lax.all_to_all(value, axes, split_axis=0, concat_axis=0, tiled=True)


def in_order(flag, mine, other, axis):
    return jnp.where(
        flag == 0, jnp.concatenate([mine, other], axis=axis), jnp.concatenate([other, mine], axis=axis)
    )


def gather_rows(rows, axes):
    count = lax.axis_size(axes)
    mine = exchange(jnp.broadcast_to(rows[None], (count,) + rows.shape), axes)
    other = lax.ppermute(mine, "core", SWAP)
    both = in_order(lax.axis_index("core"), mine[:, None], other[:, None], 1)
    return both.reshape((-1,) + rows.shape[1:])


def scatter_sum(partial, axes, tok):
    core = lax.axis_index("core")
    blocks = partial.reshape((-1, 2, tok) + partial.shape[1:])
    mine = lax.dynamic_index_in_dim(blocks, core, 1, keepdims=False)
    away = lax.dynamic_index_in_dim(blocks, 1 - core, 1, keepdims=False)
    got = lax.ppermute(away, "core", SWAP)
    pair = (mine.astype(F32) + got.astype(F32)).astype(BF)
    return jnp.sum(exchange(pair, axes).astype(F32), axis=0)


def pad_last(value, width):
    extra = width - value.shape[-1]
    return value if extra == 0 else jnp.pad(value, [(0, 0)] * (value.ndim - 1) + [(0, extra)])


def per_device(
    inputs, segment_ids, first_gain, gelu_in_w, linear_in_w, conv_weight, conv_bias, recur_gate_w, recur_gate_b,
    input_gate_w, input_gate_b, decay_param, out_proj_w, second_gain, mlp_gate_w, mlp_up_w, mlp_down_w, out_grad,
):
    n_hi, n_lo, n_cx, n_core = (lax.axis_size(a) for a in EVERY)
    hi, lo, cx, core = (lax.axis_index(a) for a in EVERY)
    n_ctx = n_cx * n_core
    n_dp = n_hi * n_lo
    n_dev = n_dp * n_ctx
    ctx = cx * n_core + core
    tok, width = inputs.shape
    tokens = segment_ids.shape[1]
    chans = linear_in_w.shape[1]
    bw = recur_gate_w.shape[1]
    hidden_units = mlp_gate_w.shape[1]
    own_ch = chans // n_ctx
    starts = [own_ch * c // bw for c in range(n_ctx)]
    span = max((own_ch * (c + 1) - 1) // bw - starts[c] + 1 for c in range(n_ctx))
    starts = [min(s, HEADS - span) for s in starts]
    win = span * bw
    head0 = jnp.array(starts, jnp.int32)[ctx]
    ch0 = head0 * bw
    own_off = own_ch * ctx - ch0
    ff_own = hidden_units // (n_lo * n_ctx)
    ff_pad = -(-ff_own // 128) * 128

    piece = width // n_dev
    small = jnp.concatenate(
        [v[None] for v in (first_gain, second_gain)]
        + [conv_weight]
        + [v[None] for v in (conv_bias, recur_gate_b, input_gate_b, decay_param)],
        axis=0,
    )
    small_all = exchange(jnp.broadcast_to(small[None], (n_dev,) + small.shape), EVERY)
    small_all = small_all.transpose(1, 0, 2).reshape(small.shape[0], width).astype(F32)
    gain_first = small_all[0]
    gain_second = small_all[1]

    windows = [
        jnp.concatenate(
            [gelu_in_w[:, s * bw : s * bw + win], linear_in_w[:, s * bw : s * bw + win]], axis=1
        )
        for s in starts
    ]
    gl_part = exchange(jnp.stack(windows), CTX).reshape(-1, 2 * win)
    gl_w = lax.all_gather(gl_part, DP, axis=0, tiled=True)
    gates_all = lax.all_gather(jnp.concatenate([recur_gate_w, input_gate_w], axis=1), EVERY, axis=0, tiled=True)
    gates_win = lax.dynamic_slice_in_dim(gates_all, ch0, win)
    recur_w = gates_win[:, :bw]
    input_w = gates_win[:, bw:]
    proj_all = lax.all_gather(out_proj_w, EVERY, axis=0, tiled=True)
    proj_w = lax.dynamic_slice_in_dim(proj_all, ch0, win)

    r_first = lax.rsqrt(jnp.mean(inputs * inputs, axis=-1, keepdims=True) + 1e-06)
    normed = (inputs * r_first * gain_first).astype(BF)
    normed_all = gather_rows(normed, "cxy")

    down_grad = lax.all_gather(out_grad.astype(BF), CUBE, axis=0, tiled=True)

    def columns(weight):
        parts = weight.reshape(weight.shape[0], n_ctx, n_lo, ff_own).transpose(2, 1, 0, 3)
        return pad_last(parts.reshape(n_lo * n_ctx, weight.shape[0], ff_own), ff_pad)

    gu_send = jnp.concatenate([columns(mlp_gate_w), columns(mlp_up_w)], axis=2)
    gu_mine = exchange(gu_send, CUBE).reshape(-1, 2 * ff_pad)
    gu_other = lax.ppermute(gu_mine, "hi", SWAP)
    gu_w = in_order(hi, gu_mine, gu_other, 0)
    down_other = lax.ppermute(mlp_down_w, "hi", SWAP)
    n_cube = n_lo * n_ctx
    half = n_cube // 2
    to_a, to_b = [], []
    for q in range(n_cube):
        lower, upper = q // 2, q // 2 + half
        near, far = (lower, upper) if q % 2 == 0 else (upper, lower)
        place = lambda t: (t % n_lo) * n_ctx + t // n_lo
        to_a.append((q, place(near)))
        to_b.append((q, place(far)))
    odd = core
    same = hi == odd
    down_a = lax.ppermute(jnp.where(same, mlp_down_w, down_other), CUBE, to_a)
    down_b = lax.ppermute(jnp.where(same, down_other, mlp_down_w), CUBE, to_b)
    slot = ctx * n_lo + lo
    down_w = in_order((slot >= half).astype(jnp.int32), down_a, down_b, 0)
    down_w = jnp.pad(down_w, ((0, ff_pad - ff_own), (0, 0)))

    ids = segment_ids[0]
    metas = [jnp.concatenate([jnp.ones((1,), F32), (ids[1:] != ids[:-1]).astype(F32)])]
    for k in range(1, CONV):
        metas.append(jnp.concatenate([jnp.zeros((k,), F32), (ids[k:] == ids[:-k]).astype(F32)]))
    meta = jnp.stack(metas, axis=1)
    vec_win = lax.dynamic_slice_in_dim(small_all[2:], ch0, win, axis=1)
    decay_win = vec_win[7:8]
    place_in = jnp.arange(win) - own_off
    own_mask = ((place_in >= 0) & (place_in < own_ch)).astype(F32)[None]
    vecs = jnp.concatenate(
        [
            vec_win[:7],
            -8.0 * jax.nn.softplus(decay_win),
            own_mask,
            -8.0 * jax.nn.sigmoid(decay_win),
            jnp.zeros((6, win), F32),
        ],
        axis=0,
    )
    gelu_pre = dot(normed_all, gl_w[:, :win], 1, 0)
    linear_out = dot(normed_all, gl_w[:, win:], 1, 0).astype(BF)
    mixed, prev, conv_out, rec, inp = forward_call(linear_out, gelu_pre, meta, vecs, recur_w, input_w)
    proj_part = dot(mixed, proj_w, 1, 0).astype(BF)
    hidden = inputs + scatter_sum(proj_part, "cxy", tok)
    mixed_own = lax.dynamic_slice_in_dim(mixed, own_off, own_ch, axis=1)
    mixed_all = lax.all_gather(mixed_own, CTX, axis=0, tiled=False)

    r_second = lax.rsqrt(jnp.mean(hidden * hidden, axis=-1, keepdims=True) + 1e-06)
    second = (hidden * r_second * gain_second).astype(BF)
    second_all = gather_rows(second, ("lo", "cxy"))
    pre = dot(second_all, gu_w, 1, 0)
    gate_pre, up_pre = pre[:, :ff_pad], pre[:, ff_pad:]
    act_grad = dot(down_grad, down_w, 1, 1)
    gel, slope = gelu_parts(gate_pre)
    activation = (gel * up_pre).astype(BF)
    gu_low = jnp.concatenate([(act_grad * up_pre * slope).astype(BF), (act_grad * gel).astype(BF)], axis=1)
    second_part = dot(gu_low, gu_w, 1, 1).astype(BF)
    second_grad = scatter_sum(second_part, ("lo", "cxy"), tok)
    out_part = dot(activation, down_w, 1, 0).astype(BF)
    output = hidden + lax.psum_scatter(out_part, CUBE, scatter_dimension=0, tiled=True).astype(F32)

    grad_gu = dot(second_all, gu_low, 0, 0).astype(BF)
    grad_down = dot(activation, down_grad, 0, 0).astype(BF)

    def settle(partial, axis):
        size = partial.shape[axis] // n_hi
        mine = lax.dynamic_slice_in_dim(partial, hi * size, size, axis)
        away = lax.dynamic_slice_in_dim(partial, (1 - hi) * size, size, axis)
        both = (mine.astype(F32) + lax.ppermute(away, "hi", SWAP).astype(F32)).astype(BF)
        if n_lo == 1:
            return both, None
        size = size // n_lo
        mine = lax.dynamic_slice_in_dim(both, lo * size, size, axis)
        away = lax.dynamic_slice_in_dim(both, (1 - lo) * size, size, axis)
        return mine, lax.ppermute(away, "lo", SWAP)

    gu_a, gu_b = settle(grad_gu, 0)
    dn_a, dn_b = settle(grad_down, 1)
    grad_gate = in_order(lo, gu_a[:, :ff_own], gu_b[:, :ff_own], 1).astype(F32)
    grad_up = in_order(
        lo, gu_a[:, ff_pad : ff_pad + ff_own], gu_b[:, ff_pad : ff_pad + ff_own], 1
    ).astype(F32)
    grad_dn = in_order(lo, dn_a[:ff_own], dn_b[:ff_own], 0).astype(F32)

    hidden_part, grad_gain_two = rms_back(hidden, gain_second, second_grad)
    hidden_grad = out_grad + hidden_part
    branch = hidden_grad.astype(BF)
    branch_all = gather_rows(branch, "cxy")

    mixed_grad = dot(branch_all, proj_w, 1, 1)
    gelu_low, linear_low, recur_wg, input_wg, sums = backward_call(
        mixed_grad, gelu_pre, conv_out, rec, inp, prev, linear_out, meta, vecs, recur_w, input_w
    )
    branch_cols = lax.dynamic_slice_in_dim(branch_all, ctx * (width // n_ctx), width // n_ctx, axis=1)
    grad_proj = jnp.einsum("ctr,td->crd", mixed_all, branch_cols, preferred_element_type=F32)
    grad_proj = grad_proj.reshape(chans, width // n_ctx).astype(BF)
    grad_proj = lax.psum_scatter(grad_proj, DP, scatter_dimension=0, tiled=True).astype(F32)
    lows = jnp.concatenate([gelu_low, linear_low], axis=1)
    own_lows = jnp.concatenate(
        [
            lax.dynamic_slice_in_dim(gelu_low, own_off, own_ch, axis=1),
            lax.dynamic_slice_in_dim(linear_low, own_off, own_ch, axis=1),
        ],
        axis=1,
    )
    grad_gl = dot(normed_all, own_lows, 0, 0).astype(BF)
    grad_gl = lax.psum_scatter(grad_gl, DP, scatter_dimension=0, tiled=True).astype(F32)
    first_part = dot(lows, gl_w, 1, 1).astype(BF)
    first_grad = scatter_sum(first_part, "cxy", tok)
    input_part, grad_gain_one = rms_back(inputs, gain_first, first_grad)
    input_grad = hidden_grad + input_part

    packed = jnp.concatenate([recur_wg, input_wg, pad_last(sums.T, 128)], axis=1)
    packed = lax.dynamic_slice_in_dim(packed, own_off, own_ch, axis=0)
    packed = jnp.sum(exchange(packed.reshape(n_dp, own_ch // n_dp, packed.shape[1]), DP), axis=0)
    routes = [(d * n_ctx + c, c * n_dp + d) for d in range(n_dp) for c in range(n_ctx)]
    packed = lax.ppermute(packed, EVERY, routes)
    grad_recur_w = packed[:, :bw]
    grad_input_w = packed[:, bw : 2 * bw]
    rest = packed[:, 2 * bw : 2 * bw + 8].T
    gains = jnp.stack([grad_gain_one, grad_gain_two]).reshape(2, n_dev, piece).transpose(1, 0, 2)
    gains = jnp.sum(exchange(gains, EVERY), axis=0)

    return (
        output,
        input_grad,
        gains[0],
        grad_gl[:, :own_ch],
        grad_gl[:, own_ch:],
        rest[:CONV],
        rest[4],
        grad_recur_w,
        rest[5],
        grad_input_w,
        rest[6],
        rest[7],
        grad_proj,
        gains[1],
        grad_gate,
        grad_up,
        grad_dn,
    )


def solution(mesh):
    n_dp = mesh.shape["dp"]
    n_ctx = mesh.shape["context"]
    inner = Mesh(mesh.devices.reshape(2, n_dp // 2, n_ctx // 2, 2), EVERY)
    rows = P(EVERY, None)
    vec = P(EVERY)
    return jax.shard_map(
        per_device,
        mesh=inner,
        in_specs=(
            rows, P(DP, None), vec, rows, rows, P(None, EVERY), vec, rows, vec, rows, vec, vec, rows, vec,
            rows, rows, rows, rows,
        ),
        out_specs=(
            rows, rows, vec, P(DP, CTX), P(DP, CTX), P(None, EVERY), vec, rows, vec, rows, vec, vec,
            P(DP, CTX), vec, P(DP, CTX), P(DP, CTX), P(CTX, DP),
        ),
        check_vma=False,
    )
```

```python
import functools

import jax
import jax.numpy as jnp
from jax import lax
from jax.experimental import pallas as pl
from jax.experimental.pallas import tpu as pltpu
from jax.sharding import Mesh
from jax.sharding import PartitionSpec as P

HEADS = 10
CONV = 4
CHUNK = 256
BF = jnp.bfloat16
F32 = jnp.float32
DP = ("hi", "lo")
CTX = ("cxy", "core")
CUBE = ("lo", "cxy", "core")
EVERY = ("hi", "lo", "cxy", "core")
SWAP = [(0, 1), (1, 0)]


def dot(a, b, ca, cb):
    return lax.dot_general(a, b, (((ca,), (cb,)), ((), ())), preferred_element_type=F32)


def gelu_parts(x):
    c0 = 0.7978845608028654
    c1 = 0.044715
    x2 = x * x
    th = jnp.tanh(c0 * x * (1.0 + c1 * x2))
    half = 0.5 * (1.0 + th)
    slope = half + 0.5 * x * (1.0 - th * th) * c0 * (1.0 + 3.0 * c1 * x2)
    return x * half, slope


def minus_expm1(x):
    series = 1.0 + x * (1.0 / 8.0)
    for n in range(7, 1, -1):
        series = 1.0 + x * (1.0 / n) * series
    return jnp.where(x > -0.5, -x * series, 1.0 - jnp.exp(x))


def forward_kernel(
    lin_ref, gpre_ref, meta_ref, vec_ref, rw_ref, iw_ref,
    mixed_ref, prev_ref, conv_ref, rec_ref, inp_ref,
    xbuf, dec_s, drv_s, st_s, carry,
):
    rows = lin_ref.shape[0]
    first = pl.program_id(1) == 0

    @pl.when(first)
    def _():
        xbuf[0:8, :] = jnp.zeros((8, xbuf.shape[1]), F32)
        carry[...] = jnp.zeros_like(carry)

    x = lin_ref[...].astype(F32)
    xbuf[8 : 8 + rows, :] = x
    conv = vec_ref[4:5, :] + vec_ref[0:1, :] * x
    for k in range(1, CONV):
        conv = conv + vec_ref[k : k + 1, :] * (xbuf[8 - k : 8 - k + rows, :] * meta_ref[:, k : k + 1])
    xbuf[0:8, :] = x[rows - 8 : rows, :]
    low = conv.astype(BF)
    rec = jax.nn.sigmoid(jnp.dot(low, rw_ref[...], preferred_element_type=F32) + vec_ref[5:6, :])
    inp = jax.nn.sigmoid(jnp.dot(low, iw_ref[...], preferred_element_type=F32) + vec_ref[6:7, :])
    reset = meta_ref[:, 0:1] > 0.5
    log_decay = vec_ref[7:8, :] * rec
    scale = jnp.where(reset, 1.0, jnp.sqrt(minus_expm1(2.0 * log_decay)))
    dec_s[...] = jnp.where(reset, 0.0, jnp.exp(log_decay))
    drv_s[...] = scale * inp * conv
    conv_ref[...] = conv
    rec_ref[...] = rec
    inp_ref[...] = inp
    width = carry.shape[1]
    row = lax.broadcasted_iota(jnp.int32, (8, width), 0)

    def step(i, held):
        at = pl.multiple_of(i * 8, 8)
        a = dec_s[pl.ds(at, 8), :]
        b = drv_s[pl.ds(at, 8), :]
        for s in (1, 2, 4):
            keep = row >= s
            b = a * jnp.where(keep, pltpu.roll(b, s, 0), 0.0) + b
            a = a * jnp.where(keep, pltpu.roll(a, s, 0), 1.0)
        h = a * held + b
        st_s[pl.ds(at, 8), :] = h
        prev_ref[pl.ds(at, 8), :] = jnp.where(row == 0, held, pltpu.roll(h, 1, 0))
        return jnp.broadcast_to(h[7:8, :], (8, width))

    carry[...] = lax.fori_loop(0, rows // 8, step, carry[...], unroll=4)
    gel, _ = gelu_parts(gpre_ref[...])
    mixed_ref[...] = (gel * st_s[...] * vec_ref[8:9, :]).astype(BF)


def backward_kernel(
    mg_ref, gpre_ref, conv_ref, rec_ref, inp_ref, prev_ref, lin_ref, meta_ref, vec_ref, rw_ref, iw_ref,
    glow_ref, llow_ref, rwg_ref, iwg_ref, sum_ref,
    dec_s, sg_s, lam_s, gbuf, carry,
):
    rows = lin_ref.shape[0]
    first = pl.program_id(1) == 0

    @pl.when(first)
    def _():
        carry[...] = jnp.zeros_like(carry)
        for k in range(CONV - 1):
            gbuf[k, rows : rows + 8, :] = jnp.zeros((8, gbuf.shape[2]), F32)
        rwg_ref[...] = jnp.zeros_like(rwg_ref)
        iwg_ref[...] = jnp.zeros_like(iwg_ref)
        sum_ref[...] = jnp.zeros_like(sum_ref)

    mg = mg_ref[...]
    conv = conv_ref[...]
    rec = rec_ref[...]
    inp = inp_ref[...]
    prev = prev_ref[...]
    own = vec_ref[8:9, :]
    gel, slope = gelu_parts(gpre_ref[...])
    reset = meta_ref[:, 0:1] > 0.5
    log_decay = vec_ref[7:8, :] * rec
    scale = jnp.where(reset, 1.0, jnp.sqrt(minus_expm1(2.0 * log_decay)))
    dec = jnp.where(reset, 0.0, jnp.exp(log_decay))
    gated = scale * inp
    states = dec * prev + gated * conv
    glow_ref[...] = (mg * states * slope * own).astype(BF)
    dec_s[...] = dec
    sg_s[...] = mg * gel
    width = carry.shape[1]
    row = lax.broadcasted_iota(jnp.int32, (8, width), 0)
    blocks = rows // 8

    def step(i, held):
        at = pl.multiple_of((blocks - 1 - i) * 8, 8)
        a = dec_s[pl.ds(at, 8), :]
        g = sg_s[pl.ds(at, 8), :]
        b = a * g
        for s in (1, 2, 4):
            keep = row < 8 - s
            b = a * jnp.where(keep, pltpu.roll(b, 8 - s, 0), 0.0) + b
            a = a * jnp.where(keep, pltpu.roll(a, 8 - s, 0), 1.0)
        m = a * held + b
        lam_s[pl.ds(at, 8), :] = g + jnp.where(row == 7, held, pltpu.roll(m, 7, 0))
        return jnp.broadcast_to(m[0:1, :], (8, width))

    carry[...] = lax.fori_loop(0, blocks, step, carry[...], unroll=4)
    lam = lam_s[...]
    conv_gate = lam * gated
    dinp = lam * scale * conv
    dscale = lam * inp * conv
    dlog = jnp.where(reset, 0.0, (lam * prev - dscale * dec / scale) * dec)
    recur_grad = vec_ref[7:8, :] * dlog * rec * (1.0 - rec)
    input_grad = dinp * inp * (1.0 - inp)
    rlow = recur_grad.astype(BF)
    ilow = input_grad.astype(BF)
    low = conv.astype(BF)
    rwg_ref[...] += dot(low, rlow, 0, 0)
    iwg_ref[...] += dot(low, ilow, 0, 0)
    conv_grad = conv_gate + dot(rlow, rw_ref[...], 1, 1) + dot(ilow, iw_ref[...], 1, 1)
    lin = lin_ref[...].astype(F32)
    linear_grad = vec_ref[0:1, :] * conv_grad

    def add(at, value):
        sum_ref[at : at + 1, :] += jnp.sum(value, axis=0, keepdims=True)

    add(0, conv_grad * lin)
    for k in range(1, CONV):
        masked = conv_grad * meta_ref[:, k : k + 1]
        gbuf[k - 1, 0:rows, :] = masked
        moved = gbuf[k - 1, k : k + rows, :]
        gbuf[k - 1, rows : rows + 8, :] = masked[0:8, :]
        linear_grad = linear_grad + vec_ref[k : k + 1, :] * moved
        add(k, moved * lin)
    llow_ref[...] = (linear_grad * own).astype(BF)
    add(4, conv_grad)
    add(5, recur_grad)
    add(6, input_grad)
    add(7, vec_ref[9:10, :] * rec * dlog)


def forward_call(lin, gpre, meta, vecs, rw, iw):
    tokens, win = lin.shape
    bw = rw.shape[1]
    rows = min(CHUNK, tokens)
    grid = (win // bw, tokens // rows)
    tok = pl.BlockSpec((rows, bw), lambda h, j: (j, h))
    mspec = pl.BlockSpec((rows, meta.shape[1]), lambda h, j: (j, 0))
    vspec = pl.BlockSpec((vecs.shape[0], bw), lambda h, j: (0, h))
    wspec = pl.BlockSpec((bw, bw), lambda h, j: (h, 0))
    full = jax.ShapeDtypeStruct((tokens, win), F32)
    return pl.pallas_call(
        forward_kernel,
        grid=grid,
        in_specs=[tok, tok, mspec, vspec, wspec, wspec],
        out_specs=[tok] * 5,
        out_shape=[jax.ShapeDtypeStruct((tokens, win), BF), full, full, full, full],
        scratch_shapes=[
            pltpu.VMEM((rows + 8, bw), F32),
            pltpu.VMEM((rows, bw), F32),
            pltpu.VMEM((rows, bw), F32),
            pltpu.VMEM((rows, bw), F32),
            pltpu.VMEM((8, bw), F32),
        ],
        compiler_params=pltpu.CompilerParams(vmem_limit_bytes=40 << 20),
        cost_estimate=pl.CostEstimate(
            flops=tokens * win * (4 * bw + 100), bytes_accessed=tokens * win * 24, transcendentals=tokens * win * 6
        ),
        name="recur_forward",
    )(lin, gpre, meta, vecs, rw, iw)


def backward_call(mg, gpre, conv, rec, inp, prev, lin, meta, vecs, rw, iw):
    tokens, win = lin.shape
    bw = rw.shape[1]
    rows = min(CHUNK, tokens)
    steps = tokens // rows
    grid = (win // bw, steps)
    tok = pl.BlockSpec((rows, bw), lambda h, j: (steps - 1 - j, h))
    mspec = pl.BlockSpec((rows, meta.shape[1]), lambda h, j: (steps - 1 - j, 0))
    vspec = pl.BlockSpec((vecs.shape[0], bw), lambda h, j: (0, h))
    wspec = pl.BlockSpec((bw, bw), lambda h, j: (h, 0))
    sspec = pl.BlockSpec((8, bw), lambda h, j: (0, h))
    lows = jax.ShapeDtypeStruct((tokens, win), BF)
    wgrad = jax.ShapeDtypeStruct((win, bw), F32)
    return pl.pallas_call(
        backward_kernel,
        grid=grid,
        in_specs=[tok] * 7 + [mspec, vspec, wspec, wspec],
        out_specs=[tok, tok, wspec, wspec, sspec],
        out_shape=[lows, lows, wgrad, wgrad, jax.ShapeDtypeStruct((8, win), F32)],
        scratch_shapes=[
            pltpu.VMEM((rows, bw), F32),
            pltpu.VMEM((rows, bw), F32),
            pltpu.VMEM((rows, bw), F32),
            pltpu.VMEM((CONV - 1, rows + 8, bw), F32),
            pltpu.VMEM((8, bw), F32),
        ],
        compiler_params=pltpu.CompilerParams(vmem_limit_bytes=40 << 20),
        cost_estimate=pl.CostEstimate(
            flops=tokens * win * (8 * bw + 150), bytes_accessed=tokens * win * 30, transcendentals=tokens * win * 6
        ),
        name="recur_backward",
    )(mg, gpre, conv, rec, inp, prev, lin, meta, vecs, rw, iw)


def exchange(value, axes):
    return lax.all_to_all(value, axes, split_axis=0, concat_axis=0, tiled=True)


def in_order(flag, mine, other, axis):
    return jnp.where(
        flag == 0, jnp.concatenate([mine, other], axis=axis), jnp.concatenate([other, mine], axis=axis)
    )


def chain_sum(partial, count):
    here = lax.axis_index("hi") * (count // 2) + lax.axis_index("lo")
    size = partial.shape[0] // count
    block = lambda d: lax.dynamic_slice_in_dim(partial, jnp.clip(d, 0, count - 1) * size, size).astype(F32)
    total = block(here)
    for way in (1, -1):
        held = None
        for k in range(count - 1):
            value = block(here + way * (count - 1 - k))
            value = value if held is None else value + held
            pairs = [(z, z + 1) for z in range(k + 1)]
            if way < 0:
                pairs = [(count - 1 - a, count - 1 - b) for a, b in pairs]
            held = lax.ppermute(value.astype(BF), DP, pairs).astype(F32)
        total = total + held
    return total


def device(lo, cx, core):
    return {"lo": lo, "cxy": cx, "core": core}


class Group:
    def __init__(self, n_lo, n_cx, cube):
        self.n_cx = n_cx
        self.count = n_lo * n_cx if cube else n_cx
        self.cube = cube
        self.lo = lax.axis_index("lo")
        self.cx = lax.axis_index("cxy")
        self.core = lax.axis_index("core")
        self.place = self.lo * n_cx + self.cx if cube else self.cx

    def at(self, step):
        return lax.rem(self.place + step + self.count, self.count)

    def peer(self, step):
        spot = self.at(step)
        lo = spot // self.n_cx if self.cube else self.lo
        return device(lo, lax.rem(spot, self.n_cx), self.core)

    def sibling(self):
        return device(self.lo, self.cx, 1 - self.core)


def across():
    return {"hi": 1 - lax.axis_index("hi")}


def meet(group, both=False):
    barrier = pltpu.get_barrier_semaphore()
    if both:
        pl.semaphore_signal(barrier, inc=1, device_id=across(), device_id_type=pl.DeviceIdType.MESH)
    for step in range(1, group.count):
        pl.semaphore_signal(barrier, inc=1, device_id=group.peer(step), device_id_type=pl.DeviceIdType.MESH)
    pl.semaphore_signal(barrier, inc=1, device_id=group.sibling(), device_id_type=pl.DeviceIdType.MESH)
    pl.semaphore_wait(barrier, group.count + int(both))


def send(src, dst, out_sem, in_sem, target):
    return pltpu.make_async_remote_copy(
        src_ref=src, dst_ref=dst, send_sem=out_sem, recv_sem=in_sem,
        device_id=target, device_id_type=pl.DeviceIdType.MESH,
    )


def spread_begin(group, src, out, sems):
    keep, out_sems, in_sems, pass_sems, mate_sems = sems
    mine = out.at[group.place * 2 + group.core]
    local = pltpu.make_async_copy(src, mine, keep)
    local.start()
    direct = [send(src, mine, out_sems.at[s], in_sems.at[s], group.peer(s)) for s in range(1, group.count)]
    for copy in direct:
        copy.start()
    mate = send(src, mine, pass_sems.at[0], mate_sems.at[0], group.sibling())
    mate.start()
    return local, direct, mate


def spread_end(group, src, out, sems, begun):
    keep, out_sems, in_sems, pass_sems, mate_sems = sems
    slot = lambda place, core: out.at[place * 2 + core]
    local, direct, first = begun
    mate = [first]
    for s in range(1, group.count):
        came = slot(group.at(-s), group.core)
        send(came, came, out_sems.at[s], in_sems.at[s], group.peer(s)).wait_recv()
        mate.append(send(came, came, pass_sems.at[s], mate_sems.at[s], group.sibling()))
        mate[s].start()
    local.wait()
    for copy in direct:
        copy.wait_send()
    for s in range(group.count):
        mate[s].wait_send()
        there = slot(group.at(-s), 1 - group.core)
        send(there, there, pass_sems.at[s], mate_sems.at[s], group.sibling()).wait_recv()


def spread(group, src, out, sems):
    spread_end(group, src, out, sems, spread_begin(group, src, out, sems))


def spread_sems(count):
    return [pltpu.SemaphoreType.DMA(())] + [pltpu.SemaphoreType.DMA((count,)) for _ in range(4)]


def fold(group, part, mate_buf, far_buf, mine, stage, total, sems):
    load_sems, pass_sems, mate_sems, out_sems, in_sems, stage_sems = sems
    order = list(range(1, group.count)) + [0]
    rows = total.shape[0]
    mates, loads, fars = {}, {}, {}
    for s in order:
        spot = group.at(s)
        mates[s] = send(
            part.at[spot, 1 - group.core], mate_buf.at[spot], pass_sems.at[s], mate_sems.at[s], group.sibling()
        )
        mates[s].start()
        loads[s] = pltpu.make_async_copy(part.at[spot, group.core], mine.at[s], load_sems.at[s])
        loads[s].start()
    for turn, s in enumerate(order):
        mates[s].wait_recv()
        slot = turn % 2
        fetch = pltpu.make_async_copy(mate_buf.at[group.at(s)], stage.at[slot], stage_sems.at[slot])
        fetch.start()
        loads[s].wait()
        fetch.wait()

        def add(r, held):
            at = pl.ds(pl.multiple_of(r * 16, 16), 16)
            value = mine[s, at, :].astype(F32) + stage[slot, at, :].astype(F32)
            if s:
                mine[s, at, :] = value.astype(BF)
            else:
                total[at, :] = value
            return held

        lax.fori_loop(0, rows // 16, add, 0)
        if s:
            fars[s] = send(mine.at[s], far_buf.at[s - 1], out_sems.at[s], in_sems.at[s], group.peer(s))
            fars[s].start()
    for turn, s in enumerate(order[:-1]):
        fars[s].wait_recv()
        slot = turn % 2
        fetch = pltpu.make_async_copy(far_buf.at[s - 1], stage.at[slot], stage_sems.at[slot])
        fetch.start()
        fetch.wait()

        def take(r, held):
            at = pl.ds(pl.multiple_of(r * 16, 16), 16)
            total[at, :] += stage[slot, at, :].astype(F32)
            return held

        lax.fori_loop(0, rows // 16, take, 0)
    for s in order:
        mates[s].wait_send()
        if s:
            fars[s].wait_send()


def fold_scratch(count, tok, width):
    return [
        pltpu.VMEM((count, tok, width), BF),
        pltpu.VMEM((2, tok, width), BF),
        pltpu.VMEM((tok, width), F32),
    ] + [pltpu.SemaphoreType.DMA((count,)) for _ in range(5)] + [pltpu.SemaphoreType.DMA((2,))]


def each_rows(rows, body):
    def run(r, held):
        body(pl.ds(pl.multiple_of(r * 16, 16), 16))
        return held

    lax.fori_loop(0, rows // 16, run, 0)


def middle_forward(n_lo, n_cx, part, away, inputs, gain, hidden, second_all, got, mate_buf, far_buf,
                   mine, stage, total, f0, f1, f2, f3, f4, f5, second, k, s0, s1, s2, s3, h0, h1):
    cube = Group(n_lo, n_cx, True)
    plane = Group(n_lo, n_cx, False)
    meet(cube, True)
    half = send(away, got, h0, h1, across())
    half.start()
    fold(plane, part, mate_buf, far_buf, mine, stage, total, (f0, f1, f2, f3, f4, f5))

    def norm(at):
        h = inputs[at, :] + total[at, :]
        hidden[at, :] = h
        r = lax.rsqrt(jnp.mean(h * h, axis=-1, keepdims=True) + 1e-06)
        second[at, :] = (h * r * gain[...]).astype(BF)

    each_rows(total.shape[0], norm)
    spread(cube, second, second_all, (k, s0, s1, s2, s3))
    half.wait()


def norm_back(values, gain, grad, base, out, gain_grad, at):
    v = values[at, :]
    g = grad[at, :]
    r = lax.rsqrt(jnp.mean(v * v, axis=-1, keepdims=True) + 1e-06)
    q = g * gain[...]
    back = base[at, :] + r * q - r * r * r * v * jnp.mean(q * v, axis=-1, keepdims=True)
    out[at, :] = back
    term = g * v * r
    gain_grad[...] += term[0:8, :] + term[8:16, :]
    return back


def middle_backward(n_lo, n_cx, part, away_a, away_b, hidden, out_grad, gain, hidden_grad, gain_grad, branch_all,
                    got_a, got_b, mate_buf, far_buf,
                    mine, stage, total, f0, f1, f2, f3, f4, f5, branch, k, s0, s1, s2, s3, h0, h1, h2, h3):
    cube = Group(n_lo, n_cx, True)
    plane = Group(n_lo, n_cx, False)
    meet(cube, True)
    halves = [send(away_a, got_a, h0, h1, across()), send(away_b, got_b, h2, h3, across())]
    for half in halves:
        half.start()
    fold(cube, part, mate_buf, far_buf, mine, stage, total, (f0, f1, f2, f3, f4, f5))
    gain_grad[...] = jnp.zeros_like(gain_grad)

    def norm(at):
        branch[at, :] = norm_back(hidden, gain, total, out_grad, hidden_grad, gain_grad, at).astype(BF)

    each_rows(total.shape[0], norm)
    spread(plane, branch, branch_all, (k, s0, s1, s2, s3))
    for half in halves:
        half.wait()


def last_backward(n_lo, n_cx, part, inputs, hidden_grad, gain, input_grad, gain_grad, mate_buf, far_buf,
                  mine, stage, total, f0, f1, f2, f3, f4, f5):
    plane = Group(n_lo, n_cx, False)
    meet(plane)
    fold(plane, part, mate_buf, far_buf, mine, stage, total, (f0, f1, f2, f3, f4, f5))
    gain_grad[...] = jnp.zeros_like(gain_grad)

    def norm(at):
        norm_back(inputs, gain, total, hidden_grad, input_grad, gain_grad, at)

    each_rows(total.shape[0], norm)


def comm_call(kernel, name, number, raw, args, outs, scratch, micros):
    any_spec = pl.BlockSpec(memory_space=pl.ANY)
    vmem = pl.BlockSpec(memory_space=pltpu.VMEM)
    return pl.pallas_call(
        kernel,
        in_specs=[any_spec] * len(raw) + [vmem] * len(args),
        out_specs=[vmem if inside else any_spec for _, inside in outs],
        out_shape=[shape for shape, _ in outs],
        scratch_shapes=scratch,
        compiler_params=pltpu.CompilerParams(
            collective_id=number, has_side_effects=True, vmem_limit_bytes=48 << 20
        ),
        cost_estimate=pl.CostEstimate(flops=micros * 10**9, bytes_accessed=micros * 10**6, transcendentals=0),
        name=name,
    )(*raw, *args)


def middle_forward_call(n_lo, n_cx, part, away, inputs, gain):
    tok, width = inputs.shape
    near = n_cx
    far = n_lo * n_cx
    rows = jax.ShapeDtypeStruct((tok, width), F32)
    bf = lambda n: jax.ShapeDtypeStruct((n, tok, width), BF)
    hidden, second_all, got, _, _ = comm_call(
        functools.partial(middle_forward, n_lo, n_cx), "sum_norm_gather_forward", 1,
        (part.reshape(near, 2, tok, width), away), (inputs, gain),
        [(rows, True), (bf(far * 2), False), (jax.ShapeDtypeStruct(away.shape, BF), False), (bf(near), False),
         (bf(near - 1), False)],
        fold_scratch(near, tok, width) + [pltpu.VMEM((tok, width), BF)] + spread_sems(far)
        + [pltpu.SemaphoreType.DMA(()) for _ in range(2)], 120,
    )
    return hidden, second_all.reshape(-1, width), got


def middle_backward_call(n_lo, n_cx, part, away_a, away_b, hidden, out_grad, gain):
    tok, width = hidden.shape
    near = n_cx
    far = n_lo * n_cx
    rows = jax.ShapeDtypeStruct((tok, width), F32)
    bf = lambda n: jax.ShapeDtypeStruct((n, tok, width), BF)
    hidden_grad, gain_grad, branch_all, got_a, got_b, _, _ = comm_call(
        functools.partial(middle_backward, n_lo, n_cx), "sum_norm_gather_backward", 2,
        (part.reshape(far, 2, tok, width), away_a, away_b), (hidden, out_grad, gain),
        [(rows, True), (jax.ShapeDtypeStruct((8, width), F32), True), (bf(near * 2), False),
         (jax.ShapeDtypeStruct(away_a.shape, BF), False), (jax.ShapeDtypeStruct(away_b.shape, BF), False),
         (bf(far), False), (bf(far - 1), False)],
        fold_scratch(far, tok, width) + [pltpu.VMEM((tok, width), BF)] + spread_sems(near)
        + [pltpu.SemaphoreType.DMA(()) for _ in range(4)], 120,
    )
    return hidden_grad, gain_grad, branch_all.reshape(-1, width), got_a, got_b


def last_backward_call(n_lo, n_cx, part, inputs, hidden_grad, gain):
    tok, width = inputs.shape
    near = n_cx
    rows = jax.ShapeDtypeStruct((tok, width), F32)
    bf = lambda n: jax.ShapeDtypeStruct((n, tok, width), BF)
    input_grad, gain_grad, _, _ = comm_call(
        functools.partial(last_backward, n_lo, n_cx), "sum_norm_backward", 3,
        (part.reshape(near, 2, tok, width),), (inputs, hidden_grad, gain),
        [(rows, True), (jax.ShapeDtypeStruct((8, width), F32), True), (bf(near), False), (bf(near - 1), False)],
        fold_scratch(near, tok, width), 50,
    )
    return input_grad, gain_grad


class Line:
    def __init__(self, n_hi, n_lo):
        self.n_lo = n_lo
        self.count = n_hi * n_lo
        self.z = lax.axis_index("hi") * n_lo + lax.axis_index("lo")

    def device(self, z):
        return {"hi": z // self.n_lo, "lo": lax.rem(z, self.n_lo)}

    def run(self, buf, sems, k, action):
        out_sems, in_sems = sems
        last = self.count - 1
        z = self.z
        for side, way in ((0, 1), (1, -1)):
            if way == 1:
                sends = jnp.logical_and(z >= k, z < last)
                comes = z >= k + 1
            else:
                sends = jnp.logical_and(z <= last - k, z > 0)
                comes = z <= last - 1 - k
            at = side * last + k
            if action == "recv":
                @pl.when(comes)
                def _():
                    plane = buf.at[z - way * (k + 1)]
                    send(plane, plane, out_sems.at[at], in_sems.at[at], self.device(z - way)).wait_recv()
            else:
                @pl.when(sends)
                def _():
                    plane = buf.at[z - way * k]
                    copy = send(plane, plane, out_sems.at[at], in_sems.at[at], self.device(z + way))
                    if action == "start":
                        copy.start()
                    else:
                        copy.wait_send()


def window_head(c, own_ch, bw, span):
    head = own_ch * c // bw
    top = HEADS - span
    return head - head // (top + 1) * (head - top)


def window_shard(head, n_dev, n_ctx, span):
    return head * ((n_dev - n_ctx) // (HEADS - span))


def gather_start(sizes, gl_send, gu_send, pg, normed, down,
                 gl_out, gu_out, pg_z, pg_win, normed_all, down_other,
                 local_sems, gl_s, gl_r, gu_s, gu_r, win_s, win_r, zp_s, zp_r, zg_s, zg_r, dn_s, dn_r,
                 k0, k1, k2, k3, k4):
    n_hi, n_lo, n_cx, n_core, own_ch, bw, span = sizes
    n_ctx = n_cx * n_core
    n_cube = n_lo * n_ctx
    n_dev = n_hi * n_cube
    hi = lax.axis_index("hi")
    lo = lax.axis_index("lo")
    cx = lax.axis_index("cxy")
    core = lax.axis_index("core")
    ctx = cx * n_core + core
    spot = lo * n_ctx + ctx
    number = hi * n_cube + spot
    line = Line(n_hi, n_lo)
    z = line.z
    plane = Group(n_lo, n_cx, False)
    in_plane = lambda c: {"cxy": c // n_core, "core": lax.rem(c, n_core)}
    in_cube = lambda u: {"lo": u // n_ctx, **in_plane(lax.rem(u, n_ctx))}

    barrier = pltpu.get_barrier_semaphore()

    def greet(i, held):
        other = lax.rem(number + i, n_dev)
        pl.semaphore_signal(
            barrier, inc=1, device_id={"hi": other // n_cube, **in_cube(lax.rem(other, n_cube))},
            device_id_type=pl.DeviceIdType.MESH,
        )
        return held

    lax.fori_loop(1, n_dev, greet, 0)
    pl.semaphore_wait(barrier, n_dev - 1)

    locals_ = [
        pltpu.make_async_copy(pg, pg_z.at[z], local_sems.at[0]),
        pltpu.make_async_copy(gl_send.at[ctx], gl_out.at[z, ctx], local_sems.at[1]),
        pltpu.make_async_copy(gu_send.at[spot], gu_out.at[spot], local_sems.at[2]),
    ]
    for copy in locals_:
        copy.start()
    locals_[0].wait()
    pg_sems, gl_sems = (zp_s, zp_r), (zg_s, zg_r)
    steps = line.count - 1
    line.run(pg_z, pg_sems, 0, "start")
    gl_copies = []
    for s in range(1, n_ctx):
        to = lax.rem(ctx + s, n_ctx)
        gl_copies.append(send(gl_send.at[to], gl_out.at[z, ctx], gl_s.at[s], gl_r.at[s], in_plane(to)))
        gl_copies[-1].start()
    spread_sems_ = (k0, k1, k2, k3, k4)
    mates = spread_begin(plane, normed, normed_all, spread_sems_)
    locals_[1].wait()
    for s in range(1, n_ctx):
        came = gl_out.at[z, lax.rem(ctx - s + n_ctx, n_ctx)]
        send(came, came, gl_s.at[s], gl_r.at[s], in_plane(lax.rem(ctx + s, n_ctx))).wait_recv()
    line.run(gl_out, gl_sems, 0, "start")
    for k in range(1, steps):
        line.run(pg_z, pg_sems, k - 1, "recv")
        line.run(pg_z, pg_sems, k, "start")
    line.run(pg_z, pg_sems, steps - 1, "recv")

    def window(src, dst):
        first = window_shard(window_head(dst, own_ch, bw, span), n_dev, n_ctx, span)
        turn = lax.rem(src - first + n_dev, n_ctx)
        return (first + turn) // n_ctx, turn

    shard, turn = window(ctx, ctx)
    own_window = pltpu.make_async_copy(pg_z.at[shard], pg_win.at[turn], local_sems.at[3])
    own_window.start()
    win_copies = []
    for s in range(1, n_ctx):
        to = lax.rem(ctx + s, n_ctx)
        shard, turn = window(ctx, to)
        win_copies.append(send(pg_z.at[shard], pg_win.at[turn], win_s.at[s], win_r.at[s], in_plane(to)))
        win_copies[-1].start()
    gu_copies = []
    for s in range(1, n_cube):
        to = lax.rem(spot + s, n_cube)
        gu_copies.append(send(gu_send.at[to], gu_out.at[spot], gu_s.at[s], gu_r.at[s], in_cube(to)))
        gu_copies[-1].start()
    for k in range(1, steps):
        line.run(gl_out, gl_sems, k - 1, "recv")
        line.run(gl_out, gl_sems, k, "start")
    down_copy = send(down, down_other, dn_s, dn_r, {"hi": 1 - hi})
    down_copy.start()
    spread_end(plane, normed, normed_all, spread_sems_, mates)
    for s in range(1, n_ctx):
        _, turn = window(lax.rem(ctx - s + n_ctx, n_ctx), ctx)
        came = pg_win.at[turn]
        send(came, came, win_s.at[s], win_r.at[s], in_plane(lax.rem(ctx + s, n_ctx))).wait_recv()
    for s in range(1, n_cube):
        came = gu_out.at[lax.rem(spot - s + n_cube, n_cube)]
        send(came, came, gu_s.at[s], gu_r.at[s], in_cube(lax.rem(spot + s, n_cube))).wait_recv()
    line.run(gl_out, gl_sems, steps - 1, "recv")
    own_window.wait()
    locals_[2].wait()
    for copy in gl_copies + win_copies + gu_copies:
        copy.wait_send()
    for k in range(steps):
        line.run(pg_z, pg_sems, k, "sent")
        line.run(gl_out, gl_sems, k, "sent")
    down_copy.wait()


def gather_start_call(sizes, gl_send, gu_send, pg, normed, down):
    n_hi, n_lo, n_cx, n_core = sizes[:4]
    n_ctx = n_cx * n_core
    n_cube = n_lo * n_ctx
    n_dp = n_hi * n_lo
    sds = lambda *shape: jax.ShapeDtypeStruct(shape, BF)
    any_spec = pl.BlockSpec(memory_space=pl.ANY)
    dma = lambda *n: pltpu.SemaphoreType.DMA(n)
    outs = [
        sds(n_dp, n_ctx, *gl_send.shape[1:]), sds(*gu_send.shape), sds(n_dp, *pg.shape), sds(n_ctx, *pg.shape),
        sds(n_ctx, *normed.shape), sds(*down.shape),
    ]
    hops = 2 * (n_dp - 1)
    got = pl.pallas_call(
        functools.partial(gather_start, sizes),
        in_specs=[any_spec] * 5,
        out_specs=[any_spec] * 6,
        out_shape=outs,
        scratch_shapes=[
            dma(4), dma(n_ctx), dma(n_ctx), dma(n_cube), dma(n_cube), dma(n_ctx), dma(n_ctx),
            dma(hops), dma(hops), dma(hops), dma(hops), dma(), dma(),
        ] + spread_sems(n_cx),
        compiler_params=pltpu.CompilerParams(collective_id=4, has_side_effects=True),
        cost_estimate=pl.CostEstimate(flops=10**11, bytes_accessed=10**8, transcendentals=0),
        name="gather_start",
    )(gl_send, gu_send, pg, normed, down)
    gl_out, gu_out, _, pg_win, normed_all, down_other = got
    return gl_out, gu_out, pg_win, normed_all, down_other


def pad_last(value, width):
    extra = width - value.shape[-1]
    return value if extra == 0 else jnp.pad(value, [(0, 0)] * (value.ndim - 1) + [(0, extra)])


def per_device(
    inputs, segment_ids, first_gain, gelu_in_w, linear_in_w, conv_weight, conv_bias, recur_gate_w, recur_gate_b,
    input_gate_w, input_gate_b, decay_param, out_proj_w, second_gain, mlp_gate_w, mlp_up_w, mlp_down_w, out_grad,
):
    n_hi, n_lo, n_cx, n_core = (lax.axis_size(a) for a in EVERY)
    hi, lo, cx, core = (lax.axis_index(a) for a in EVERY)
    n_ctx = n_cx * n_core
    n_dp = n_hi * n_lo
    n_dev = n_dp * n_ctx
    ctx = cx * n_core + core
    tok, width = inputs.shape
    tokens = segment_ids.shape[1]
    chans = linear_in_w.shape[1]
    bw = recur_gate_w.shape[1]
    hidden_units = mlp_gate_w.shape[1]
    own_ch = chans // n_ctx
    span = max((own_ch * (c + 1) - 1) // bw - own_ch * c // bw + 1 for c in range(n_ctx))
    starts = [window_head(c, own_ch, bw, span) for c in range(n_ctx)]
    win = span * bw
    head0 = window_head(ctx, own_ch, bw, span)
    ch0 = head0 * bw
    own_off = own_ch * ctx - ch0
    ff_own = hidden_units // (n_lo * n_ctx)
    ff_pad = -(-ff_own // 128) * 128

    piece = width // n_dev
    small = jnp.concatenate(
        [v[None] for v in (first_gain, second_gain)]
        + [conv_weight]
        + [v[None] for v in (conv_bias, recur_gate_b, input_gate_b, decay_param)],
        axis=0,
    )
    small_all = exchange(jnp.broadcast_to(small[None], (n_dev,) + small.shape), EVERY)
    small_all = small_all.transpose(1, 0, 2).reshape(small.shape[0], width).astype(F32)
    gain_first = small_all[0]
    gain_second = small_all[1]

    windows = [
        jnp.concatenate(
            [gelu_in_w[:, s * bw : s * bw + win], linear_in_w[:, s * bw : s * bw + win]], axis=1
        )
        for s in starts
    ]
    pg = jnp.concatenate([out_proj_w, recur_gate_w, input_gate_w], axis=1)

    r_first = lax.rsqrt(jnp.mean(inputs * inputs, axis=-1, keepdims=True) + 1e-06)
    normed = (inputs * r_first * gain_first).astype(BF)

    def columns(weight):
        parts = weight.reshape(weight.shape[0], n_ctx, n_lo, ff_own).transpose(2, 1, 0, 3)
        return pad_last(parts.reshape(n_lo * n_ctx, weight.shape[0], ff_own), ff_pad)

    gu_send = jnp.concatenate([columns(mlp_gate_w), columns(mlp_up_w)], axis=2)
    sizes = (n_hi, n_lo, n_cx, n_core, own_ch, bw, span)
    gl_w, gu_mine, pg_win, normed_all, down_other = gather_start_call(
        sizes, jnp.stack(windows), gu_send, pg, normed, mlp_down_w
    )
    gl_w = gl_w.reshape(width, 2 * win)
    gu_mine = gu_mine.reshape(-1, 2 * ff_pad)
    normed_all = normed_all.reshape(tokens, width)
    pg_win = lax.dynamic_slice_in_dim(
        pg_win.reshape(-1, pg.shape[1]), ch0 - window_shard(head0, n_dev, n_ctx, span) * piece, win
    )
    proj_w = pg_win[:, :width]
    recur_w = pg_win[:, width : width + bw]
    input_w = pg_win[:, width + bw :]
    n_cube = n_lo * n_ctx
    half = n_cube // 2
    to_a, to_b = [], []
    for q in range(n_cube):
        lower, upper = q // 2, q // 2 + half
        near, far = (lower, upper) if q % 2 == 0 else (upper, lower)
        place = lambda t: (t % n_lo) * n_ctx + t // n_lo
        to_a.append((q, place(near)))
        to_b.append((q, place(far)))
    odd = core
    same = hi == odd
    down_a = lax.ppermute(jnp.where(same, mlp_down_w, down_other), CUBE, to_a)
    down_b = lax.ppermute(jnp.where(same, down_other, mlp_down_w), CUBE, to_b)
    slot = ctx * n_lo + lo
    down_w = in_order((slot >= half).astype(jnp.int32), down_a, down_b, 0)
    down_w = jnp.pad(down_w, ((0, ff_pad - ff_own), (0, 0)))

    ids = segment_ids[0]
    metas = [jnp.concatenate([jnp.ones((1,), F32), (ids[1:] != ids[:-1]).astype(F32)])]
    for k in range(1, CONV):
        metas.append(jnp.concatenate([jnp.zeros((k,), F32), (ids[k:] == ids[:-k]).astype(F32)]))
    meta = jnp.stack(metas, axis=1)
    vec_win = lax.dynamic_slice_in_dim(small_all[2:], ch0, win, axis=1)
    decay_win = vec_win[7:8]
    place_in = jnp.arange(win) - own_off
    own_mask = ((place_in >= 0) & (place_in < own_ch)).astype(F32)[None]
    vecs = jnp.concatenate(
        [
            vec_win[:7],
            -8.0 * jax.nn.softplus(decay_win),
            own_mask,
            -8.0 * jax.nn.sigmoid(decay_win),
            jnp.zeros((6, win), F32),
        ],
        axis=0,
    )
    gelu_pre = dot(normed_all, gl_w[:, :win], 1, 0)
    linear_out = dot(normed_all, gl_w[:, win:], 1, 0).astype(BF)
    mixed, prev, conv_out, rec, inp = forward_call(linear_out, gelu_pre, meta, vecs, recur_w, input_w)
    proj_part = dot(mixed, proj_w, 1, 0).astype(BF)
    out_grad_low = lax.optimization_barrier((out_grad.astype(BF), proj_w))[0]
    down_grad = lax.all_gather(out_grad_low, CUBE, axis=0, tiled=True)
    hidden, second_all, gu_other = middle_forward_call(n_lo, n_cx, proj_part, gu_mine, inputs, gain_second[None])
    gu_w = in_order(hi, gu_mine, gu_other, 0)

    pre = dot(second_all, gu_w, 1, 0)
    gate_pre, up_pre = pre[:, :ff_pad], pre[:, ff_pad:]
    act_grad = dot(down_grad, down_w, 1, 1)
    gel, slope = gelu_parts(gate_pre)
    activation = (gel * up_pre).astype(BF)
    gu_low = jnp.concatenate([(act_grad * up_pre * slope).astype(BF), (act_grad * gel).astype(BF)], axis=1)
    second_part = dot(gu_low, gu_w, 1, 1).astype(BF)
    grad_gu = dot(second_all, gu_low, 0, 0).astype(BF)
    grad_down = dot(activation, down_grad, 0, 0).astype(BF)

    def half_of(partial, which, axis, parts):
        size = partial.shape[axis] // parts
        return lax.dynamic_slice_in_dim(partial, which * size, size, axis)

    away_gu = half_of(grad_gu, 1 - hi, 0, n_hi)
    away_dn = half_of(grad_down, 1 - hi, 1, n_hi)
    early = away_gu.shape[0] // 2
    hidden_grad, gain_two_rows, branch_all, got_gu, got_dn = middle_backward_call(
        n_lo, n_cx, second_part, away_gu[:early], away_dn, hidden, out_grad, gain_second[None]
    )
    rest_gu = lax.ppermute(lax.optimization_barrier((away_gu[early:], gain_two_rows))[0], "hi", SWAP)

    def settle(partial, got, axis):
        both = (half_of(partial, hi, axis, n_hi).astype(F32) + got.astype(F32)).astype(BF)
        return half_of(both, lo, axis, n_lo), lax.ppermute(half_of(both, 1 - lo, axis, n_lo), "lo", SWAP)

    dn_a, dn_b = settle(grad_down, got_dn, 1)
    gu_a, gu_b = settle(grad_gu, jnp.concatenate([got_gu, rest_gu], axis=0), 0)
    grad_gate = in_order(lo, gu_a[:, :ff_own], gu_b[:, :ff_own], 1).astype(F32)
    grad_up = in_order(
        lo, gu_a[:, ff_pad : ff_pad + ff_own], gu_b[:, ff_pad : ff_pad + ff_own], 1
    ).astype(F32)
    grad_dn = in_order(lo, dn_a[:ff_own], dn_b[:ff_own], 0).astype(F32)

    out_part = dot(activation, lax.optimization_barrier((down_w, gain_two_rows))[0], 1, 0).astype(BF)
    output = hidden + lax.psum_scatter(out_part, CUBE, scatter_dimension=0, tiled=True).astype(F32)

    mixed_grad = dot(branch_all, proj_w, 1, 1)
    gelu_low, linear_low, recur_wg, input_wg, sums = backward_call(
        mixed_grad, gelu_pre, conv_out, rec, inp, prev, linear_out, meta, vecs, recur_w, input_w
    )
    own_mixed = lax.dynamic_slice_in_dim(mixed, own_off, own_ch, axis=1)
    grad_proj = dot(own_mixed, branch_all, 0, 0).astype(BF).reshape(own_ch, n_ctx, width // n_ctx)
    grad_proj = exchange(grad_proj.transpose(1, 0, 2), CTX).reshape(chans, width // n_ctx)
    grad_proj = chain_sum(grad_proj, n_dp).astype(F32)
    lows = jnp.concatenate([gelu_low, linear_low], axis=1)
    own_lows = jnp.concatenate(
        [
            lax.dynamic_slice_in_dim(gelu_low, own_off, own_ch, axis=1),
            lax.dynamic_slice_in_dim(linear_low, own_off, own_ch, axis=1),
        ],
        axis=1,
    )
    grad_gl = dot(normed_all, own_lows, 0, 0).astype(BF)
    grad_gl = chain_sum(grad_gl, n_dp).astype(F32)
    first_part = dot(lows, gl_w, 1, 1).astype(BF)
    input_grad, gain_one_rows = last_backward_call(n_lo, n_cx, first_part, inputs, hidden_grad, gain_first[None])

    packed = jnp.concatenate([recur_wg, input_wg, pad_last(sums.T, 128)], axis=1)
    packed = lax.dynamic_slice_in_dim(packed, own_off, own_ch, axis=0)
    packed = jnp.sum(exchange(packed.reshape(n_dp, own_ch // n_dp, packed.shape[1]), DP), axis=0)
    routes = [(d * n_ctx + c, c * n_dp + d) for d in range(n_dp) for c in range(n_ctx)]
    packed = lax.ppermute(packed, EVERY, routes)
    grad_recur_w = packed[:, :bw]
    grad_input_w = packed[:, bw : 2 * bw]
    rest = packed[:, 2 * bw : 2 * bw + 8].T
    gains = jnp.stack([jnp.sum(gain_one_rows, axis=0), jnp.sum(gain_two_rows, axis=0)]).reshape(2, n_dev, piece).transpose(1, 0, 2)
    gains = jnp.sum(exchange(gains, EVERY), axis=0)

    return (
        output,
        input_grad,
        gains[0],
        grad_gl[:, :own_ch],
        grad_gl[:, own_ch:],
        rest[:CONV],
        rest[4],
        grad_recur_w,
        rest[5],
        grad_input_w,
        rest[6],
        rest[7],
        grad_proj,
        gains[1],
        grad_gate,
        grad_up,
        grad_dn,
    )


def solution(mesh):
    n_dp = mesh.shape["dp"]
    n_ctx = mesh.shape["context"]
    inner = Mesh(mesh.devices.reshape(2, n_dp // 2, n_ctx // 2, 2), EVERY)
    rows = P(EVERY, None)
    vec = P(EVERY)
    return jax.shard_map(
        per_device,
        mesh=inner,
        in_specs=(
            rows, P(DP, None), vec, rows, rows, P(None, EVERY), vec, rows, vec, rows, vec, vec, rows, vec,
            rows, rows, rows, rows,
        ),
        out_specs=(
            rows, rows, vec, P(DP, CTX), P(DP, CTX), P(None, EVERY), vec, rows, vec, rows, vec, vec,
            P(DP, CTX), vec, P(DP, CTX), P(DP, CTX), P(CTX, DP),
        ),
        check_vma=False,
    )
```

```python
import functools

import jax
import jax.numpy as jnp
from jax import lax
from jax.experimental import pallas as pl
from jax.experimental.pallas import tpu as pltpu
from jax.sharding import Mesh
from jax.sharding import PartitionSpec as P

HEADS = 10
CONV = 4
CHUNK = 256
BF = jnp.bfloat16
F32 = jnp.float32
DP = ("hi", "lo")
CTX = ("cxy", "core")
CUBE = ("lo", "cxy", "core")
EVERY = ("hi", "lo", "cxy", "core")
SWAP = [(0, 1), (1, 0)]


def dot(a, b, ca, cb):
    return lax.dot_general(a, b, (((ca,), (cb,)), ((), ())), preferred_element_type=F32)


def gelu_parts(x):
    c0 = 0.7978845608028654
    c1 = 0.044715
    x2 = x * x
    th = jnp.tanh(c0 * x * (1.0 + c1 * x2))
    half = 0.5 * (1.0 + th)
    slope = half + 0.5 * x * (1.0 - th * th) * c0 * (1.0 + 3.0 * c1 * x2)
    return x * half, slope


def minus_expm1(x):
    series = 1.0 + x * (1.0 / 8.0)
    for n in range(7, 1, -1):
        series = 1.0 + x * (1.0 / n) * series
    return jnp.where(x > -0.5, -x * series, 1.0 - jnp.exp(x))


def forward_kernel(
    lin_ref, gpre_ref, meta_ref, vec_ref, rw_ref, iw_ref,
    mixed_ref, prev_ref, conv_ref, rec_ref, inp_ref,
    xbuf, dec_s, drv_s, st_s, carry,
):
    rows = lin_ref.shape[0]
    first = pl.program_id(1) == 0

    @pl.when(first)
    def _():
        xbuf[0:8, :] = jnp.zeros((8, xbuf.shape[1]), F32)
        carry[...] = jnp.zeros_like(carry)

    x = lin_ref[...].astype(F32)
    xbuf[8 : 8 + rows, :] = x
    conv = vec_ref[4:5, :] + vec_ref[0:1, :] * x
    for k in range(1, CONV):
        conv = conv + vec_ref[k : k + 1, :] * (xbuf[8 - k : 8 - k + rows, :] * meta_ref[:, k : k + 1])
    xbuf[0:8, :] = x[rows - 8 : rows, :]
    low = conv.astype(BF)
    rec = jax.nn.sigmoid(jnp.dot(low, rw_ref[...], preferred_element_type=F32) + vec_ref[5:6, :])
    inp = jax.nn.sigmoid(jnp.dot(low, iw_ref[...], preferred_element_type=F32) + vec_ref[6:7, :])
    reset = meta_ref[:, 0:1] > 0.5
    log_decay = vec_ref[7:8, :] * rec
    scale = jnp.where(reset, 1.0, jnp.sqrt(minus_expm1(2.0 * log_decay)))
    dec_s[...] = jnp.where(reset, 0.0, jnp.exp(log_decay))
    drv_s[...] = scale * inp * conv
    conv_ref[...] = conv
    rec_ref[...] = rec
    inp_ref[...] = inp
    width = carry.shape[1]
    row = lax.broadcasted_iota(jnp.int32, (8, width), 0)

    def step(i, held):
        at = pl.multiple_of(i * 8, 8)
        a = dec_s[pl.ds(at, 8), :]
        b = drv_s[pl.ds(at, 8), :]
        for s in (1, 2, 4):
            keep = row >= s
            b = a * jnp.where(keep, pltpu.roll(b, s, 0), 0.0) + b
            a = a * jnp.where(keep, pltpu.roll(a, s, 0), 1.0)
        h = a * held + b
        st_s[pl.ds(at, 8), :] = h
        prev_ref[pl.ds(at, 8), :] = jnp.where(row == 0, held, pltpu.roll(h, 1, 0))
        return jnp.broadcast_to(h[7:8, :], (8, width))

    carry[...] = lax.fori_loop(0, rows // 8, step, carry[...], unroll=4)
    gel, _ = gelu_parts(gpre_ref[...])
    mixed_ref[...] = (gel * st_s[...] * vec_ref[8:9, :]).astype(BF)


def backward_kernel(
    mg_ref, gpre_ref, conv_ref, rec_ref, inp_ref, prev_ref, lin_ref, meta_ref, vec_ref, rw_ref, iw_ref,
    glow_ref, llow_ref, rwg_ref, iwg_ref, sum_ref,
    dec_s, sg_s, lam_s, gbuf, carry,
):
    rows = lin_ref.shape[0]
    first = pl.program_id(1) == 0

    @pl.when(first)
    def _():
        carry[...] = jnp.zeros_like(carry)
        for k in range(CONV - 1):
            gbuf[k, rows : rows + 8, :] = jnp.zeros((8, gbuf.shape[2]), F32)
        rwg_ref[...] = jnp.zeros_like(rwg_ref)
        iwg_ref[...] = jnp.zeros_like(iwg_ref)
        sum_ref[...] = jnp.zeros_like(sum_ref)

    mg = mg_ref[...]
    conv = conv_ref[...]
    rec = rec_ref[...]
    inp = inp_ref[...]
    prev = prev_ref[...]
    own = vec_ref[8:9, :]
    gel, slope = gelu_parts(gpre_ref[...])
    reset = meta_ref[:, 0:1] > 0.5
    log_decay = vec_ref[7:8, :] * rec
    scale = jnp.where(reset, 1.0, jnp.sqrt(minus_expm1(2.0 * log_decay)))
    dec = jnp.where(reset, 0.0, jnp.exp(log_decay))
    gated = scale * inp
    states = dec * prev + gated * conv
    glow_ref[...] = (mg * states * slope * own).astype(BF)
    dec_s[...] = dec
    sg_s[...] = mg * gel
    width = carry.shape[1]
    row = lax.broadcasted_iota(jnp.int32, (8, width), 0)
    blocks = rows // 8

    def step(i, held):
        at = pl.multiple_of((blocks - 1 - i) * 8, 8)
        a = dec_s[pl.ds(at, 8), :]
        g = sg_s[pl.ds(at, 8), :]
        b = a * g
        for s in (1, 2, 4):
            keep = row < 8 - s
            b = a * jnp.where(keep, pltpu.roll(b, 8 - s, 0), 0.0) + b
            a = a * jnp.where(keep, pltpu.roll(a, 8 - s, 0), 1.0)
        m = a * held + b
        lam_s[pl.ds(at, 8), :] = g + jnp.where(row == 7, held, pltpu.roll(m, 7, 0))
        return jnp.broadcast_to(m[0:1, :], (8, width))

    carry[...] = lax.fori_loop(0, blocks, step, carry[...], unroll=4)
    lam = lam_s[...]
    conv_gate = lam * gated
    dinp = lam * scale * conv
    dscale = lam * inp * conv
    dlog = jnp.where(reset, 0.0, (lam * prev - dscale * dec / scale) * dec)
    recur_grad = vec_ref[7:8, :] * dlog * rec * (1.0 - rec)
    input_grad = dinp * inp * (1.0 - inp)
    rlow = recur_grad.astype(BF)
    ilow = input_grad.astype(BF)
    low = conv.astype(BF)
    rwg_ref[...] += dot(low, rlow, 0, 0)
    iwg_ref[...] += dot(low, ilow, 0, 0)
    conv_grad = conv_gate + dot(rlow, rw_ref[...], 1, 1) + dot(ilow, iw_ref[...], 1, 1)
    lin = lin_ref[...].astype(F32)
    linear_grad = vec_ref[0:1, :] * conv_grad

    def add(at, value):
        sum_ref[at : at + 1, :] += jnp.sum(value, axis=0, keepdims=True)

    add(0, conv_grad * lin)
    for k in range(1, CONV):
        masked = conv_grad * meta_ref[:, k : k + 1]
        gbuf[k - 1, 0:rows, :] = masked
        moved = gbuf[k - 1, k : k + rows, :]
        gbuf[k - 1, rows : rows + 8, :] = masked[0:8, :]
        linear_grad = linear_grad + vec_ref[k : k + 1, :] * moved
        add(k, moved * lin)
    llow_ref[...] = (linear_grad * own).astype(BF)
    add(4, conv_grad)
    add(5, recur_grad)
    add(6, input_grad)
    add(7, vec_ref[9:10, :] * rec * dlog)


def forward_call(lin, gpre, meta, vecs, rw, iw):
    tokens, win = lin.shape
    bw = rw.shape[1]
    rows = min(CHUNK, tokens)
    grid = (win // bw, tokens // rows)
    tok = pl.BlockSpec((rows, bw), lambda h, j: (j, h))
    mspec = pl.BlockSpec((rows, meta.shape[1]), lambda h, j: (j, 0))
    vspec = pl.BlockSpec((vecs.shape[0], bw), lambda h, j: (0, h))
    wspec = pl.BlockSpec((bw, bw), lambda h, j: (h, 0))
    full = jax.ShapeDtypeStruct((tokens, win), F32)
    return pl.pallas_call(
        forward_kernel,
        grid=grid,
        in_specs=[tok, tok, mspec, vspec, wspec, wspec],
        out_specs=[tok] * 5,
        out_shape=[jax.ShapeDtypeStruct((tokens, win), BF), full, full, full, full],
        scratch_shapes=[
            pltpu.VMEM((rows + 8, bw), F32),
            pltpu.VMEM((rows, bw), F32),
            pltpu.VMEM((rows, bw), F32),
            pltpu.VMEM((rows, bw), F32),
            pltpu.VMEM((8, bw), F32),
        ],
        compiler_params=pltpu.CompilerParams(vmem_limit_bytes=40 << 20),
        cost_estimate=pl.CostEstimate(
            flops=tokens * win * (4 * bw + 100), bytes_accessed=tokens * win * 24, transcendentals=tokens * win * 6
        ),
        name="recur_forward",
    )(lin, gpre, meta, vecs, rw, iw)


def backward_call(mg, gpre, conv, rec, inp, prev, lin, meta, vecs, rw, iw):
    tokens, win = lin.shape
    bw = rw.shape[1]
    rows = min(CHUNK, tokens)
    steps = tokens // rows
    grid = (win // bw, steps)
    tok = pl.BlockSpec((rows, bw), lambda h, j: (steps - 1 - j, h))
    mspec = pl.BlockSpec((rows, meta.shape[1]), lambda h, j: (steps - 1 - j, 0))
    vspec = pl.BlockSpec((vecs.shape[0], bw), lambda h, j: (0, h))
    wspec = pl.BlockSpec((bw, bw), lambda h, j: (h, 0))
    sspec = pl.BlockSpec((8, bw), lambda h, j: (0, h))
    lows = jax.ShapeDtypeStruct((tokens, win), BF)
    wgrad = jax.ShapeDtypeStruct((win, bw), F32)
    return pl.pallas_call(
        backward_kernel,
        grid=grid,
        in_specs=[tok] * 7 + [mspec, vspec, wspec, wspec],
        out_specs=[tok, tok, wspec, wspec, sspec],
        out_shape=[lows, lows, wgrad, wgrad, jax.ShapeDtypeStruct((8, win), F32)],
        scratch_shapes=[
            pltpu.VMEM((rows, bw), F32),
            pltpu.VMEM((rows, bw), F32),
            pltpu.VMEM((rows, bw), F32),
            pltpu.VMEM((CONV - 1, rows + 8, bw), F32),
            pltpu.VMEM((8, bw), F32),
        ],
        compiler_params=pltpu.CompilerParams(vmem_limit_bytes=40 << 20),
        cost_estimate=pl.CostEstimate(
            flops=tokens * win * (8 * bw + 150), bytes_accessed=tokens * win * 30, transcendentals=tokens * win * 6
        ),
        name="recur_backward",
    )(mg, gpre, conv, rec, inp, prev, lin, meta, vecs, rw, iw)


def exchange(value, axes):
    return lax.all_to_all(value, axes, split_axis=0, concat_axis=0, tiled=True)


def in_order(flag, mine, other, axis):
    return jnp.where(
        flag == 0, jnp.concatenate([mine, other], axis=axis), jnp.concatenate([other, mine], axis=axis)
    )


def send(src, dst, out_sem, in_sem, target):
    return pltpu.make_async_remote_copy(
        src_ref=src, dst_ref=dst, send_sem=out_sem, recv_sem=in_sem,
        device_id=target, device_id_type=pl.DeviceIdType.MESH,
    )


def across():
    return {"hi": 1 - lax.axis_index("hi")}


def sibling():
    return {"core": 1 - lax.axis_index("core")}


def meet(targets):
    barrier = pltpu.get_barrier_semaphore()
    for target in targets:
        pl.semaphore_signal(barrier, inc=1, device_id=target, device_id_type=pl.DeviceIdType.MESH)
    pl.semaphore_wait(barrier, len(targets))


def subsets(bits):
    out = [()]
    for b in bits:
        out += [m + (b,) for m in out]
    return out


def lane_slices(width, parts):
    tiles = width // 128
    cuts = [tiles * i // parts * 128 for i in range(parts + 1)]
    return [pl.ds(a, b - a) for a, b in zip(cuts[:-1], cuts[1:])]


class Group:
    def __init__(self, n_lo, n_cx, cube):
        self.n_cx = n_cx
        self.near = list(range(n_cx.bit_length() - 1))
        self.far = len(self.near)
        self.cube = cube and n_lo == 2
        self.bits = self.near + ([self.far] if self.cube else [])
        self.count = n_cx * (2 if self.cube else 1)
        self.lo = lax.axis_index("lo")
        self.cx = lax.axis_index("cxy")
        self.core = lax.axis_index("core")
        self.place = self.lo * n_cx + self.cx if self.cube else self.cx

    def delta(self, bit):
        stride = 1 << bit
        return stride * (1 - 2 * lax.rem(self.place // stride, 2))

    def at(self, mask):
        spot = self.place
        for bit in mask:
            spot = spot + self.delta(bit)
        return spot

    def partner(self, bit):
        if bit == self.far:
            return {"lo": 1 - self.lo}
        return {"cxy": self.cx + self.delta(bit)}

    def partners(self):
        return [self.partner(bit) for bit in self.bits]

    def orders(self):
        return [self.bits[i:] + self.bits[:i] for i in range(len(self.bits))]


class Spread:
    def __init__(self, group, src, out, sems):
        self.group, self.src, self.out = group, src, out
        self.keep, self.out_sems, self.in_sems, self.pass_sems, self.mate_sems = sems
        self.orders = group.orders()
        self.lanes = lane_slices(src.shape[-1], len(self.orders))
        self.moves = []
        index = 0
        for s in range(len(group.bits)):
            row = []
            for order, lanes in zip(self.orders, self.lanes):
                for mask in subsets(order[:s]):
                    row.append((index, lanes, mask, order[s]))
                    index += 1
            self.moves.append(row)

    @staticmethod
    def sems(group_bits, parts):
        moves = parts * ((1 << group_bits) - 1)
        return [
            pltpu.SemaphoreType.DMA(()), pltpu.SemaphoreType.DMA((moves,)), pltpu.SemaphoreType.DMA((moves,)),
            pltpu.SemaphoreType.DMA((moves + 1,)), pltpu.SemaphoreType.DMA((moves + 1,)),
        ]

    def block(self, mask, core):
        return self.group.at(mask) * 2 + core

    def copy(self, move):
        index, lanes, mask, bit = move
        dst = self.out.at[self.block(mask, self.group.core), :, lanes]
        src = dst if mask else self.src.at[:, lanes]
        return send(src, dst, self.out_sems.at[index], self.in_sems.at[index], self.group.partner(bit))

    def relay(self, move, core):
        index, lanes, mask, bit = move
        ref = self.out.at[self.block(mask + (bit,), core), :, lanes]
        return send(ref, ref, self.pass_sems.at[index + 1], self.mate_sems.at[index + 1], sibling())

    def own(self):
        mine = self.out.at[self.block((), self.group.core)]
        local = pltpu.make_async_copy(self.src, mine, self.keep)
        return local, send(self.src, mine, self.pass_sems.at[0], self.mate_sems.at[0], sibling())

    def begin(self):
        self.start(0)
        for copy in self.own():
            copy.start()

    def start(self, s):
        for move in self.moves[s]:
            self.copy(move).start()

    def finish(self, s):
        for move in self.moves[s]:
            index, lanes, mask, bit = move
            came = self.out.at[self.block(mask + (bit,), self.group.core), :, lanes]
            send(came, came, self.out_sems.at[index], self.in_sems.at[index], self.group.partner(bit)).wait_recv()

    def pass_on(self, s):
        for move in self.moves[s]:
            self.relay(move, self.group.core).start()

    def step(self, s):
        self.finish(s)
        if s + 1 < len(self.moves):
            self.start(s + 1)
        self.pass_on(s)

    def end(self):
        local, mate = self.own()
        local.wait()
        mate.wait_send()
        other = self.out.at[self.block((), 1 - self.group.core)]
        send(other, other, self.pass_sems.at[0], self.mate_sems.at[0], sibling()).wait_recv()
        for row in self.moves:
            for move in row:
                self.copy(move).wait_send()
                self.relay(move, self.group.core).wait_send()
                self.relay(move, 1 - self.group.core).wait_recv()


class Fold:
    def __init__(self, group, part, mate_buf, scratch):
        self.group, self.part, self.mate_buf = group, part, mate_buf
        (self.mine, self.far, self.stage, self.total,
         self.load_sems, self.pass_sems, self.mate_sems, self.out_sems, self.in_sems, self.stage_sems) = scratch
        self.orders = group.orders()
        self.lanes = lane_slices(part.shape[-1], len(self.orders))
        self.rows = self.total.shape[0]
        self.moves = []
        index = slot0 = 0
        levels = len(group.bits)
        for s in range(levels):
            row = []
            for order, lanes in zip(self.orders, self.lanes):
                for n, mask in enumerate(subsets(order[s + 1 :])):
                    row.append((index, lanes, mask, order[s], slot0 + n))
                    index += 1
            self.moves.append(row)
            slot0 += 1 << (levels - s - 1)
        masks = []
        for order in self.orders:
            masks += [m for m in subsets(group.bits) if order[0] in m and m not in masks]
        masks += [m for m in subsets(group.bits) if m and m not in masks] + [()]
        self.masks = masks

    @staticmethod
    def scratch(bits, parts, tok, width):
        count = 1 << bits
        moves = parts * (count - 1)
        dma = lambda n: pltpu.SemaphoreType.DMA((n,))
        return [
            pltpu.VMEM((count, tok, width), BF), pltpu.VMEM((count - 1, tok, width), BF),
            pltpu.VMEM((2, tok, width), BF), pltpu.VMEM((tok, width), F32),
            dma(count), dma(count), dma(count), dma(moves), dma(moves), dma(2),
        ]

    def mate(self, n):
        spot = self.group.at(self.masks[n])
        return send(
            self.part.at[spot, 1 - self.group.core], self.mate_buf.at[spot],
            self.pass_sems.at[n], self.mate_sems.at[n], sibling(),
        )

    def load(self, n):
        spot = self.group.at(self.masks[n])
        return pltpu.make_async_copy(self.part.at[spot, self.group.core], self.mine.at[spot], self.load_sems.at[n])

    def fetch(self, n):
        return pltpu.make_async_copy(
            self.mate_buf.at[self.group.at(self.masks[n])], self.stage.at[n % 2], self.stage_sems.at[n % 2]
        )

    def begin(self):
        for n in range(len(self.masks)):
            self.mate(n).start()
            self.load(n).start()

    def pairs(self):
        started = [False] * len(self.orders)
        count = len(self.masks)
        self.mate(0).wait_recv()
        self.fetch(0).start()
        for n, mask in enumerate(self.masks):
            if n + 1 < count:
                self.mate(n + 1).wait_recv()
                self.fetch(n + 1).start()
            self.load(n).wait()
            self.fetch(n).wait()
            spot = self.group.at(mask)

            def add(at, spot=spot, mask=mask, n=n):
                value = self.mine[spot, at, :].astype(F32) + self.stage[n % 2, at, :].astype(F32)
                if mask:
                    self.mine[spot, at, :] = value.astype(BF)
                else:
                    self.total[at, :] = value

            each_rows(self.rows, add)
            for j, order in enumerate(self.orders):
                need = [m for m in self.masks if order[0] in m]
                if not started[j] and all(m in self.masks[: n + 1] for m in need):
                    started[j] = True
                    self.start(0, j)

    def copy(self, move):
        index, lanes, mask, bit, slot = move
        return send(
            self.mine.at[self.group.at(mask + (bit,)), :, lanes], self.far.at[slot, :, lanes],
            self.out_sems.at[index], self.in_sems.at[index], self.group.partner(bit),
        )

    def start(self, s, part=None):
        per = len(self.moves[s]) // len(self.orders)
        for n, move in enumerate(self.moves[s]):
            if part is None or n // per == part:
                self.copy(move).start()

    def take(self, s):
        per = len(self.moves[s]) // len(self.orders)
        for n, move in enumerate(self.moves[s]):
            self.copy(move).wait_recv()
            index, lanes, mask, bit, slot = move
            spot = self.group.at(mask)

            def add(at):
                value = self.far[slot, at, lanes].astype(F32)
                if mask:
                    self.mine[spot, at, lanes] = (self.mine[spot, at, lanes].astype(F32) + value).astype(BF)
                else:
                    self.total[at, lanes] += value

            each_rows(self.rows, add)
            if (n + 1) % per == 0 and s + 1 < len(self.moves):
                self.start(s + 1, n // per)

    def end(self):
        for n in range(len(self.masks)):
            self.mate(n).wait_send()
        for row in self.moves:
            for move in row:
                self.copy(move).wait_send()


def each_rows(rows, body):
    def run(r, held):
        body(pl.ds(pl.multiple_of(r * 16, 16), 16))
        return held

    lax.fori_loop(0, rows // 16, run, 0)


N_FOLD = 10
N_SPREAD = 5


def middle_forward(n_lo, n_cx, part, inputs, gain, hidden, second_all, mate_buf, *scratch):
    fold_s, rest = scratch[:N_FOLD], scratch[N_FOLD:]
    spread_s, (second,) = rest[:N_SPREAD], rest[N_SPREAD:]
    cube = Group(n_lo, n_cx, True)
    plane = Group(n_lo, n_cx, False)
    meet(cube.partners() + [sibling()])
    fold = Fold(plane, part, mate_buf, fold_s)
    fold.begin()
    fold.pairs()
    for s in range(len(plane.bits)):
        fold.take(s)

    def norm(at):
        h = inputs[at, :] + fold.total[at, :]
        hidden[at, :] = h
        r = lax.rsqrt(jnp.mean(h * h, axis=-1, keepdims=True) + 1e-06)
        second[at, :] = (h * r * gain[...]).astype(BF)

    each_rows(fold.rows, norm)
    rows = Spread(cube, second, second_all, spread_s)
    rows.begin()
    for s in range(len(cube.bits)):
        rows.step(s)
    fold.end()
    rows.end()


def norm_back(values, gain, grad, base, out, gain_grad, at):
    v = values[at, :]
    g = grad[at, :]
    r = lax.rsqrt(jnp.mean(v * v, axis=-1, keepdims=True) + 1e-06)
    q = g * gain[...]
    back = base[at, :] + r * q - r * r * r * v * jnp.mean(q * v, axis=-1, keepdims=True)
    out[at, :] = back
    term = g * v * r
    gain_grad[...] += term[0:8, :] + term[8:16, :]
    return back


def middle_backward(n_lo, n_cx, part, hidden, out_grad, gain, hidden_grad, gain_grad, branch_all, mate_buf, *scratch):
    fold_s, rest = scratch[:N_FOLD], scratch[N_FOLD:]
    spread_s, (branch,) = rest[:N_SPREAD], rest[N_SPREAD:]
    cube = Group(n_lo, n_cx, True)
    plane = Group(n_lo, n_cx, False)
    meet(cube.partners() + [sibling()])
    fold = Fold(cube, part, mate_buf, fold_s)
    fold.begin()
    fold.pairs()
    for s in range(len(cube.bits)):
        fold.take(s)
    gain_grad[...] = jnp.zeros_like(gain_grad)

    def norm(at):
        branch[at, :] = norm_back(hidden, gain, fold.total, out_grad, hidden_grad, gain_grad, at).astype(BF)

    each_rows(fold.rows, norm)
    rows = Spread(plane, branch, branch_all, spread_s)
    rows.begin()
    for s in range(len(plane.bits)):
        rows.step(s)
    fold.end()
    rows.end()


class Chain:
    def __init__(self, z, count, part, blocks, came, sems, along):
        self.z, self.count, self.part, self.blocks, self.came, self.along = z, count, part, blocks, came, along
        self.load_sems, self.out_sems, self.in_sems = sems

    @staticmethod
    def scratch(count, rows, cols):
        hops = 2 * (count - 1)
        return [pltpu.VMEM((count, rows, cols), BF), pltpu.VMEM((hops, rows, cols), BF)] + dma_sems(count, hops, hops)

    def load(self, d):
        return pltpu.make_async_copy(self.part.at[d], self.blocks.at[d], self.load_sems.at[d])

    def begin(self):
        for d in range(self.count):
            self.load(d).start()

    def ready(self):
        for d in range(self.count):
            self.load(d).wait()

    def sides(self, k):
        last = self.count - 1
        z = self.z
        yield 0, 1, jnp.logical_and(z <= k, z < last), jnp.logical_and(z >= 1, z <= k + 1)
        yield 1, -1, jnp.logical_and(z >= last - k, z > 0), jnp.logical_and(z <= last - 1, z >= last - 1 - k)

    def copy(self, side, way, k):
        at = side * (self.count - 1) + k
        block = self.blocks.at[self.z + way * (self.count - 1 - k)]
        return send(block, self.came.at[at], self.out_sems.at[at], self.in_sems.at[at], self.along(self.z + way))

    def start(self, k):
        for side, way, sends, _ in self.sides(k):
            @pl.when(sends)
            def _():
                self.copy(side, way, k).start()

    def take(self, k, total):
        final = k == self.count - 2
        for side, way, _, comes in self.sides(k):
            at = side * (self.count - 1) + k

            @pl.when(comes)
            def _():
                land = self.came.at[at]
                send(land, land, self.out_sems.at[at], self.in_sems.at[at], self.along(self.z - way)).wait_recv()

                def add(rows):
                    value = self.came[at, rows, :].astype(F32)
                    if final:
                        total[rows, :] += value
                    else:
                        spot = self.z + way * (self.count - 2 - k)
                        self.blocks[spot, rows, :] = (self.blocks[spot, rows, :].astype(F32) + value).astype(BF)

                each_rows(total.shape[0], add)

    def own(self, total):
        def put(rows):
            total[rows, :] = self.blocks[self.z, rows, :].astype(F32)

        each_rows(total.shape[0], put)

    def end(self):
        for k in range(self.count - 1):
            for side, way, sends, _ in self.sides(k):
                @pl.when(sends)
                def _():
                    self.copy(side, way, k).wait_send()


N_CHAIN = 5


def last_backward(n_lo, n_cx, n_hi, with_out, part, sums, *refs):
    if with_out:
        out_part, inputs, hidden_grad, gain, hidden, input_grad, gain_grad, summed, mate_a, output, mate_b, *scratch = refs
    else:
        inputs, hidden_grad, gain, hidden, input_grad, gain_grad, summed, mate_a, *scratch = refs
    fold_a, rest = scratch[:N_FOLD], scratch[N_FOLD:]
    chain_s, fold_b = rest[:N_CHAIN], rest[N_CHAIN:]
    cube = Group(n_lo, n_cx, True)
    plane = Group(n_lo, n_cx, False)
    n_dp = n_hi * n_lo
    z = lax.axis_index("hi") * n_lo + lax.axis_index("lo")
    along = lambda d: {"hi": d // n_lo, "lo": lax.rem(d, n_lo)}
    meet([cube.partner(b) for b in cube.near] + [sibling()] + [along(lax.rem(z + i, n_dp)) for i in range(1, n_dp)])
    first = Fold(plane, part, mate_a, fold_a)
    chain = Chain(z, n_dp, sums, chain_s[0], chain_s[1], chain_s[2:], along)
    chain.begin()
    first.begin()
    if with_out:
        outs = Fold(cube, out_part, mate_b, fold_b)
        outs.begin()
    hops = n_dp - 1
    chain.ready()
    chain.start(0)
    chain.own(summed)
    first.pairs()
    if with_out:
        outs.pairs()
    first.take(0)
    for k in range(hops - 1):
        chain.take(k, summed)
        chain.start(k + 1)
        if with_out and k + 1 < len(cube.bits):
            outs.take(k)
        if k + 1 < len(plane.bits):
            first.take(k + 1)
    for s in range(hops, len(plane.bits)):
        first.take(s)
    gain_grad[...] = jnp.zeros_like(gain_grad)

    def norm(at):
        norm_back(inputs, gain, first.total, hidden_grad, input_grad, gain_grad, at)

    each_rows(first.rows, norm)
    if with_out:
        for s in range(min(hops - 1, len(cube.bits) - 1), len(cube.bits)):
            outs.take(s)

        def finish(at):
            output[at, :] = hidden[at, :] + outs.total[at, :]

        each_rows(outs.rows, finish)
    chain.take(hops - 1, summed)
    first.end()
    if with_out:
        outs.end()
    chain.end()


def comm_call(kernel, name, number, raw, args, outs, scratch, micros):
    any_spec = pl.BlockSpec(memory_space=pl.ANY)
    vmem = pl.BlockSpec(memory_space=pltpu.VMEM)
    return pl.pallas_call(
        kernel,
        in_specs=[any_spec] * len(raw) + [vmem] * len(args),
        out_specs=[vmem if inside else any_spec for _, inside in outs],
        out_shape=[shape for shape, _ in outs],
        scratch_shapes=scratch,
        compiler_params=pltpu.CompilerParams(
            collective_id=number, has_side_effects=True, vmem_limit_bytes=56 << 20
        ),
        cost_estimate=pl.CostEstimate(flops=micros * 10**9, bytes_accessed=micros * 10**6, transcendentals=0),
        name=name,
    )(*raw, *args)


def dma_sems(*counts):
    return [pltpu.SemaphoreType.DMA((n,) if n else ()) for n in counts]


def middle_forward_call(n_lo, n_cx, part, inputs, gain):
    tok, width = inputs.shape
    near = n_cx.bit_length() - 1
    far = near + n_lo - 1
    rows = jax.ShapeDtypeStruct((tok, width), F32)
    sds = lambda *shape: jax.ShapeDtypeStruct(shape, BF)
    hidden, second_all, _ = comm_call(
        functools.partial(middle_forward, n_lo, n_cx), "sum_norm_gather_forward", 1,
        (part.reshape(n_cx, 2, tok, width),), (inputs, gain),
        [(rows, True), (sds(n_lo * n_cx * 2, tok, width), False), (sds(n_cx, tok, width), False)],
        Fold.scratch(near, near, tok, width) + Spread.sems(far, far) + [pltpu.VMEM((tok, width), BF)], 1,
    )
    return hidden, second_all.reshape(-1, width)


def middle_backward_call(n_lo, n_cx, part, hidden, out_grad, gain):
    tok, width = hidden.shape
    near = n_cx.bit_length() - 1
    far = near + n_lo - 1
    rows = jax.ShapeDtypeStruct((tok, width), F32)
    sds = lambda *shape: jax.ShapeDtypeStruct(shape, BF)
    hidden_grad, gain_grad, branch_all, _ = comm_call(
        functools.partial(middle_backward, n_lo, n_cx), "sum_norm_gather_backward", 2,
        (part.reshape(n_lo * n_cx, 2, tok, width),), (hidden, out_grad, gain),
        [(rows, True), (jax.ShapeDtypeStruct((8, width), F32), True), (sds(n_cx * 2, tok, width), False),
         (sds(n_lo * n_cx, tok, width), False)],
        Fold.scratch(far, far, tok, width) + Spread.sems(near, near) + [pltpu.VMEM((tok, width), BF)], 100,
    )
    return hidden_grad, gain_grad, branch_all.reshape(-1, width)


def last_backward_call(n_hi, n_lo, n_cx, part, out_part, sums, inputs, hidden_grad, gain, hidden):
    tok, width = inputs.shape
    near = n_cx.bit_length() - 1
    far = near + n_lo - 1
    n_dp = n_hi * n_lo
    with_out = n_lo * n_cx <= 8
    rows = jax.ShapeDtypeStruct((tok, width), F32)
    sds = lambda *shape: jax.ShapeDtypeStruct(shape, BF)
    sums = sums.reshape(n_dp, -1, sums.shape[1])
    raw = (part.reshape(n_cx, 2, tok, width), sums)
    outs = [(rows, True), (jax.ShapeDtypeStruct((8, width), F32), True),
            (jax.ShapeDtypeStruct(sums.shape[1:], F32), True), (sds(n_cx, tok, width), False)]
    scratch = Fold.scratch(near, near, tok, width) + Chain.scratch(*sums.shape)
    if with_out:
        raw += (out_part.reshape(n_lo * n_cx, 2, tok, width),)
        outs += [(rows, True), (sds(n_lo * n_cx, tok, width), False)]
        scratch += Fold.scratch(far, far, tok, width)
    got = comm_call(
        functools.partial(last_backward, n_lo, n_cx, n_hi, with_out), "sum_norm_backward", 3,
        raw, (inputs, hidden_grad, gain, hidden), outs, scratch, 1,
    )
    input_grad, gain_grad, summed = got[:3]
    if with_out:
        output = got[4]
    else:
        output = hidden + lax.psum_scatter(out_part, CUBE, scatter_dimension=0, tiled=True).astype(F32)
    return input_grad, gain_grad, output, summed


class Line:
    def __init__(self, n_hi, n_lo):
        self.n_lo = n_lo
        self.count = n_hi * n_lo
        self.z = lax.axis_index("hi") * n_lo + lax.axis_index("lo")

    def device(self, z):
        return {"hi": z // self.n_lo, "lo": lax.rem(z, self.n_lo)}

    def run(self, part, sems, k, action):
        out_sems, in_sems, pass_sems, mate_sems = sems
        last = self.count - 1
        z = self.z
        for side, way in ((0, 1), (1, -1)):
            if way == 1:
                sends = jnp.logical_and(z >= k, z < last)
                comes = z >= k + 1
            else:
                sends = jnp.logical_and(z <= last - k, z > 0)
                comes = z <= last - 1 - k
            at = side * last + k
            if action in ("recv", "mate_recv"):
                @pl.when(comes)
                def _():
                    if action == "recv":
                        plane = part(z - way * (k + 1), False)
                        send(plane, plane, out_sems.at[at], in_sems.at[at], self.device(z - way)).wait_recv()
                        if pass_sems is not None:
                            send(plane, plane, pass_sems.at[at], mate_sems.at[at], sibling()).start()
                    else:
                        plane = part(z - way * (k + 1), False)
                        send(plane, plane, pass_sems.at[at], mate_sems.at[at], sibling()).wait_send()
                        plane = part(z - way * (k + 1), True)
                        send(plane, plane, pass_sems.at[at], mate_sems.at[at], sibling()).wait_recv()
            else:
                @pl.when(sends)
                def _():
                    plane = part(z - way * k, False)
                    copy = send(plane, plane, out_sems.at[at], in_sems.at[at], self.device(z + way))
                    if action == "start":
                        copy.start()
                    else:
                        copy.wait_send()


def clamp_head(head, top):
    return head - head // (top + 1) * (head - top)


def window_head(c, own_ch, bw, span):
    return clamp_head(own_ch * c // bw, HEADS - span)


def chip_head(chip, own_ch, bw, span):
    return clamp_head(window_head(2 * chip, own_ch, bw, span), HEADS - span - 1)


def window_shard(head, n_dev, n_ctx, span):
    return head * ((n_dev - n_ctx) // (HEADS - span))


def gather_start(sizes, gelu_w, lin_w, proj, rgate, igate, normed, down, gate_w, up_w,
                 gl_out, gu_out, pg_z, pg_win, normed_all, down_other,
                 gu_send, own_pg, own_gl, own_rest, gl_s, gl_r, mate_s, mate_r, gu_s, gu_r, win_s, win_r,
                 zp_s, zp_r, zg_s, zg_r, zm_s, zm_r, dn_s, dn_r, *spread_s):
    n_hi, n_lo, n_cx, n_core, own_ch, bw, span = sizes
    n_ctx = n_cx * n_core
    n_cube = n_lo * n_ctx
    n_dev = n_hi * n_cube
    hi = lax.axis_index("hi")
    lo = lax.axis_index("lo")
    cx = lax.axis_index("cxy")
    core = lax.axis_index("core")
    ctx = cx * n_core + core
    spot = lo * n_ctx + ctx
    number = hi * n_cube + spot
    line = Line(n_hi, n_lo)
    z = line.z
    wide = (span + 1) * bw
    width = proj.shape[1]
    in_plane = lambda c: {"cxy": c // n_core, "core": lax.rem(c, n_core)}
    in_cube = lambda u: {"lo": u // n_ctx, **in_plane(lax.rem(u, n_ctx))}

    barrier = pltpu.get_barrier_semaphore()

    def greet(i, held):
        other = lax.rem(number + i, n_dev)
        pl.semaphore_signal(
            barrier, inc=1, device_id={"hi": other // n_cube, **in_cube(lax.rem(other, n_cube))},
            device_id_type=pl.DeviceIdType.MESH,
        )
        return held

    lax.fori_loop(1, n_dev, greet, 0)
    pl.semaphore_wait(barrier, n_dev - 1)

    pg_parts = [(proj, 0, width), (rgate, width, bw), (igate, width + bw, bw)]
    pg_own = [
        pltpu.make_async_copy(ref, pg_z.at[z, :, pl.ds(a, n)], own_pg.at[i]) for i, (ref, a, n) in enumerate(pg_parts)
    ]
    for copy in pg_own:
        copy.start()

    def columns(ref, chip):
        at = pl.multiple_of(chip_head(chip, own_ch, bw, span) * bw, bw)
        return ref.at[:, pl.ds(at, wide)]

    mine = lambda i: gl_out.at[z, cx, core, :, pl.ds(i * wide, wide)]
    gl_own = [pltpu.make_async_copy(columns(ref, cx), mine(i), own_gl.at[i]) for i, ref in enumerate((gelu_w, lin_w))]
    gl_copies = []
    for s in range(1, n_cx):
        to = lax.rem(cx + s, n_cx)
        for i, ref in enumerate((gelu_w, lin_w)):
            gl_copies.append(
                send(columns(ref, to), mine(i), gl_s.at[2 * s + i], gl_r.at[2 * s + i], {"cxy": to})
            )
            gl_copies[-1].start()
    for copy in gl_own:
        copy.start()
    pg_part = lambda plane, other: pg_z.at[plane]
    gl_part = lambda plane, other: gl_out.at[plane, :, 1 - core if other else core]
    pg_sems, gl_sems = (zp_s, zp_r, None, None), (zg_s, zg_r, zm_s, zm_r)
    steps = line.count - 1
    for copy in pg_own:
        copy.wait()
    line.run(pg_part, pg_sems, 0, "start")
    rows = Spread(Group(n_lo, n_cx, False), normed, normed_all, spread_s)
    rows.begin()
    for copy in gl_own:
        copy.wait()
    for s in range(1, n_cx):
        for i in range(2):
            came = gl_out.at[z, lax.rem(cx - s + n_cx, n_cx), core, :, pl.ds(i * wide, wide)]
            send(came, came, gl_s.at[2 * s + i], gl_r.at[2 * s + i], {"cxy": lax.rem(cx + s, n_cx)}).wait_recv()
    line.run(gl_part, gl_sems, 0, "start")
    own_plane = gl_part(z, False)
    own_mate = send(own_plane, own_plane, mate_s, mate_r, sibling())
    own_mate.start()

    ff_own = gate_w.shape[1] // n_cube
    ff_pad = gu_send.shape[2] // 2
    shard_rows = gate_w.shape[0]
    for u in range(n_cube):
        first = (u % n_ctx) * (n_lo * ff_own) + (u // n_ctx) * ff_own
        for i, ref in enumerate((gate_w, up_w)):
            gu_send[u, :, i * ff_pad : i * ff_pad + ff_own] = ref[:, first : first + ff_own]
            if ff_pad > ff_own:
                gu_send[u, :, i * ff_pad + ff_own : (i + 1) * ff_pad] = jnp.zeros((shard_rows, ff_pad - ff_own), BF)

    for k in range(1, steps):
        line.run(pg_part, pg_sems, k - 1, "recv")
        line.run(pg_part, pg_sems, k, "start")
    for s in range(len(rows.moves)):
        rows.step(s)
    line.run(pg_part, pg_sems, steps - 1, "recv")

    def window(src, dst):
        first = window_shard(window_head(dst, own_ch, bw, span), n_dev, n_ctx, span)
        turn = lax.rem(src - first + n_dev, n_ctx)
        return (first + turn) // n_ctx, turn

    shard, turn = window(ctx, ctx)
    own_window = pltpu.make_async_copy(pg_z.at[shard], pg_win.at[turn], own_rest.at[0])
    own_window.start()
    win_copies = []
    for s in range(1, n_ctx):
        to = lax.rem(ctx + s, n_ctx)
        shard, turn = window(ctx, to)
        win_copies.append(send(pg_z.at[shard], pg_win.at[turn], win_s.at[s], win_r.at[s], in_plane(to)))
        win_copies[-1].start()
    line.run(gl_part, gl_sems, 0, "recv")
    if steps > 1:
        line.run(gl_part, gl_sems, 1, "start")
    own_gu = pltpu.make_async_copy(gu_send.at[spot], gu_out.at[spot], own_rest.at[1])
    own_gu.start()
    gu_copies = []
    for s in range(1, n_cube):
        to = lax.rem(spot + s, n_cube)
        gu_copies.append(send(gu_send.at[to], gu_out.at[spot], gu_s.at[s], gu_r.at[s], in_cube(to)))
        gu_copies[-1].start()
    down_copy = send(down, down_other, dn_s, dn_r, across())
    for k in range(2, steps):
        line.run(gl_part, gl_sems, k - 1, "recv")
        line.run(gl_part, gl_sems, k, "start")
    down_copy.start()
    line.run(gl_part, gl_sems, steps - 1, "recv")
    rows.end()
    for s in range(1, n_ctx):
        _, turn = window(lax.rem(ctx - s + n_ctx, n_ctx), ctx)
        came = pg_win.at[turn]
        send(came, came, win_s.at[s], win_r.at[s], in_plane(lax.rem(ctx + s, n_ctx))).wait_recv()
    for s in range(1, n_cube):
        came = gu_out.at[lax.rem(spot - s + n_cube, n_cube)]
        send(came, came, gu_s.at[s], gu_r.at[s], in_cube(lax.rem(spot + s, n_cube))).wait_recv()
    own_window.wait()
    own_gu.wait()
    for copy in gl_copies + win_copies + gu_copies:
        copy.wait_send()
    own_mate.wait_send()
    other_plane = gl_part(z, True)
    send(other_plane, other_plane, mate_s, mate_r, sibling()).wait_recv()
    for k in range(steps):
        line.run(pg_part, pg_sems, k, "sent")
        line.run(gl_part, gl_sems, k, "sent")
        line.run(gl_part, gl_sems, k, "mate_recv")
    down_copy.wait()


def gather_start_call(sizes, gelu_w, lin_w, proj, rgate, igate, normed, down, gate_w, up_w, ff_pad):
    n_hi, n_lo, n_cx, n_core, own_ch, bw, span = sizes
    n_ctx = n_cx * n_core
    n_cube = n_lo * n_ctx
    n_dp = n_hi * n_lo
    shard, width = proj.shape
    near = n_cx.bit_length() - 1
    wide = (span + 1) * bw
    sds = lambda *shape: jax.ShapeDtypeStruct(shape, BF)
    any_spec = pl.BlockSpec(memory_space=pl.ANY)
    vmem = pl.BlockSpec(memory_space=pltpu.VMEM)
    pg_width = width + 2 * bw
    hops = 2 * (n_dp - 1)
    gl_out, gu_out, _, pg_win, normed_all, down_other = pl.pallas_call(
        functools.partial(gather_start, sizes),
        in_specs=[any_spec] * 7 + [vmem] * 2,
        out_specs=[any_spec] * 6,
        out_shape=[
            sds(n_dp, n_cx, n_core, shard, 2 * wide), sds(n_cube, shard, 2 * ff_pad), sds(n_dp, shard, pg_width),
            sds(n_ctx, shard, pg_width), sds(n_ctx, *normed.shape), sds(*down.shape),
        ],
        scratch_shapes=[pltpu.VMEM((n_cube, shard, 2 * ff_pad), BF)]
        + dma_sems(3, 2, 2, 2 * n_cx, 2 * n_cx, 0, 0, n_cube, n_cube, n_ctx, n_ctx, hops, hops, hops, hops, hops, hops, 0, 0)
        + Spread.sems(near, near),
        compiler_params=pltpu.CompilerParams(collective_id=4, has_side_effects=True, vmem_limit_bytes=40 << 20),
        cost_estimate=pl.CostEstimate(flops=10**11, bytes_accessed=10**8, transcendentals=0),
        name="gather_start",
    )(gelu_w, lin_w, proj, rgate, igate, normed, down, gate_w, up_w)
    return gl_out.reshape(width, 2 * wide), gu_out.reshape(-1, 2 * ff_pad), pg_win.reshape(-1, pg_width), normed_all.reshape(-1, width), down_other


def swap_first(value):
    return lax.ppermute(value, DP, [(0, 1), (3, 2)]), lax.ppermute(value, DP, [(1, 2), (2, 1)])


def swap_second(to_inner, crossed):
    return lax.ppermute(to_inner, DP, [(1, 2), (2, 1)]), lax.ppermute(crossed, DP, [(1, 0), (2, 3)])


def pad_last(value, width):
    extra = width - value.shape[-1]
    return value if extra == 0 else jnp.pad(value, [(0, 0)] * (value.ndim - 1) + [(0, extra)])


def per_device(
    inputs, segment_ids, first_gain, gelu_in_w, linear_in_w, conv_weight, conv_bias, recur_gate_w, recur_gate_b,
    input_gate_w, input_gate_b, decay_param, out_proj_w, second_gain, mlp_gate_w, mlp_up_w, mlp_down_w, out_grad,
):
    n_hi, n_lo, n_cx, n_core = (lax.axis_size(a) for a in EVERY)
    hi, lo, cx, core = (lax.axis_index(a) for a in EVERY)
    n_ctx = n_cx * n_core
    n_dp = n_hi * n_lo
    n_dev = n_dp * n_ctx
    ctx = cx * n_core + core
    tok, width = inputs.shape
    tokens = segment_ids.shape[1]
    chans = linear_in_w.shape[1]
    bw = recur_gate_w.shape[1]
    hidden_units = mlp_gate_w.shape[1]
    own_ch = chans // n_ctx
    span = max((own_ch * (c + 1) - 1) // bw - own_ch * c // bw + 1 for c in range(n_ctx))
    win = span * bw
    head0 = window_head(ctx, own_ch, bw, span)
    ch0 = head0 * bw
    own_off = own_ch * ctx - ch0
    ff_own = hidden_units // (n_lo * n_ctx)
    ff_pad = -(-ff_own // 128) * 128

    piece = width // n_dev
    small = jnp.concatenate(
        [v[None] for v in (first_gain, second_gain)]
        + [conv_weight]
        + [v[None] for v in (conv_bias, recur_gate_b, input_gate_b, decay_param)],
        axis=0,
    )
    small_all = exchange(jnp.broadcast_to(small[None], (n_dev,) + small.shape), EVERY)
    small_all = small_all.transpose(1, 0, 2).reshape(small.shape[0], width).astype(F32)
    gain_first = small_all[0]
    gain_second = small_all[1]

    r_first = lax.rsqrt(jnp.mean(inputs * inputs, axis=-1, keepdims=True) + 1e-06)
    normed = (inputs * r_first * gain_first).astype(BF)

    sizes = (n_hi, n_lo, n_cx, n_core, own_ch, bw, span)
    gl_w, gu_mine, pg_win, normed_all, down_other = gather_start_call(
        sizes, gelu_in_w, linear_in_w, out_proj_w, recur_gate_w, input_gate_w, normed, mlp_down_w,
        mlp_gate_w, mlp_up_w, ff_pad,
    )
    wide = win + bw
    chip_off = (head0 - chip_head(cx, own_ch, bw, span)) * bw
    gelu_w = lax.dynamic_slice_in_dim(gl_w[:, :wide], chip_off, win, axis=1)
    lin_w = lax.dynamic_slice_in_dim(gl_w[:, wide:], chip_off, win, axis=1)
    pg_win = lax.dynamic_slice_in_dim(pg_win, ch0 - window_shard(head0, n_dev, n_ctx, span) * piece, win)
    proj_w = pg_win[:, :width]
    recur_w = pg_win[:, width : width + bw]
    input_w = pg_win[:, width + bw :]

    gu_other = lax.ppermute(gu_mine, "hi", SWAP)
    n_cube = n_lo * n_ctx
    half = n_cube // 2
    to_a, to_b = [], []
    place = lambda t: (t % n_lo) * n_ctx + t // n_lo
    for q in range(n_cube):
        lower, upper = q // 2, q // 2 + half
        near, far = (lower, upper) if q % 2 == 0 else (upper, lower)
        to_a.append((q, place(near)))
        to_b.append((q, place(far)))
    same = hi == core
    down_a = lax.ppermute(jnp.where(same, mlp_down_w, down_other), CUBE, to_a)
    down_b = lax.ppermute(jnp.where(same, down_other, mlp_down_w), CUBE, to_b)
    slot = ctx * n_lo + lo
    down_w = in_order((slot >= half).astype(jnp.int32), down_a, down_b, 0)
    down_w = jnp.pad(down_w, ((0, ff_pad - ff_own), (0, 0)))
    cot = lax.optimization_barrier((out_grad.astype(BF), down_other))[0]
    down_grad = lax.all_gather(cot, CUBE, axis=0, tiled=True)

    ids = segment_ids[0]
    metas = [jnp.concatenate([jnp.ones((1,), F32), (ids[1:] != ids[:-1]).astype(F32)])]
    for k in range(1, CONV):
        metas.append(jnp.concatenate([jnp.zeros((k,), F32), (ids[k:] == ids[:-k]).astype(F32)]))
    meta = jnp.stack(metas, axis=1)
    vec_win = lax.dynamic_slice_in_dim(small_all[2:], ch0, win, axis=1)
    decay_win = vec_win[7:8]
    place_in = jnp.arange(win) - own_off
    own_mask = ((place_in >= 0) & (place_in < own_ch)).astype(F32)[None]
    vecs = jnp.concatenate(
        [
            vec_win[:7],
            -8.0 * jax.nn.softplus(decay_win),
            own_mask,
            -8.0 * jax.nn.sigmoid(decay_win),
            jnp.zeros((6, win), F32),
        ],
        axis=0,
    )
    gelu_pre = dot(normed_all, gelu_w, 1, 0)
    linear_out = dot(normed_all, lin_w, 1, 0).astype(BF)
    mixed, prev, conv_out, rec, inp = forward_call(linear_out, gelu_pre, meta, vecs, recur_w, input_w)
    proj_part = dot(mixed, proj_w, 1, 0).astype(BF)
    hidden, second_all = middle_forward_call(n_lo, n_cx, proj_part, inputs, gain_second[None])
    gu_w = in_order(hi, gu_mine, gu_other, 0)

    pre = dot(second_all, gu_w, 1, 0)
    gate_pre, up_pre = pre[:, :ff_pad], pre[:, ff_pad:]
    act_grad = dot(down_grad, down_w, 1, 1)
    gel, slope = gelu_parts(gate_pre)
    activation = (gel * up_pre).astype(BF)
    gu_low = jnp.concatenate([(act_grad * up_pre * slope).astype(BF), (act_grad * gel).astype(BF)], axis=1)
    second_part = dot(gu_low, gu_w, 1, 1).astype(BF)
    grad_gu = dot(second_all, gu_low, 0, 0).astype(BF)
    grad_down = dot(activation, down_grad, 0, 0).astype(BF)

    def half_of(partial, which, axis, parts):
        size = partial.shape[axis] // parts
        return lax.dynamic_slice_in_dim(partial, which * size, size, axis)

    gu_stage = swap_first(half_of(grad_gu, 1 - hi, 0, n_hi))
    dn_stage = swap_first(half_of(grad_down, 1 - hi, 1, n_hi))
    hidden_grad, gain_two_rows, branch_all = middle_backward_call(
        n_lo, n_cx, second_part, hidden, out_grad, gain_second[None]
    )

    branch_all, *stages = lax.optimization_barrier((branch_all,) + gu_stage + dn_stage)
    dn_stage = swap_second(*stages[2:])
    gu_stage = swap_second(*stages[:2])
    inner = hi != lo

    def settle(partial, got, axis):
        both = (half_of(partial, hi, axis, n_hi).astype(F32) + got.astype(F32)).astype(BF)
        return half_of(both, lo, axis, n_lo), lax.ppermute(half_of(both, 1 - lo, axis, n_lo), "lo", SWAP)

    out_part = dot(activation, lax.optimization_barrier((down_w, gain_two_rows))[0], 1, 0).astype(BF)

    own_mixed = lax.dynamic_slice_in_dim(mixed, own_off, own_ch, axis=1)
    grad_proj = dot(own_mixed, branch_all, 0, 0).astype(BF).reshape(own_ch, n_ctx, width // n_ctx)
    grad_proj = exchange(grad_proj.transpose(1, 0, 2), CTX).reshape(chans, width // n_ctx)
    mixed_grad = dot(branch_all, proj_w, 1, 1)
    gelu_low, linear_low, recur_wg, input_wg, sums = backward_call(
        mixed_grad, gelu_pre, conv_out, rec, inp, prev, linear_out, meta, vecs, recur_w, input_w
    )
    gelu_low, linear_low, *dn_stage = lax.optimization_barrier((gelu_low, linear_low) + dn_stage)
    got_dn = jnp.where(inner, *dn_stage)
    got_gu = jnp.where(inner, *gu_stage)
    own_lows = jnp.concatenate(
        [
            lax.dynamic_slice_in_dim(gelu_low, own_off, own_ch, axis=1),
            lax.dynamic_slice_in_dim(linear_low, own_off, own_ch, axis=1),
        ],
        axis=1,
    )
    grad_gl = dot(normed_all, own_lows, 0, 0).astype(BF)
    first_part = (dot(gelu_low, gelu_w, 1, 1) + dot(linear_low, lin_w, 1, 1)).astype(BF)
    grad_three = jnp.concatenate([grad_gl, grad_proj], axis=1)
    dn_a, dn_b = settle(grad_down, got_dn, 1)
    gu_a, gu_b = settle(grad_gu, got_gu, 0)
    first_part, dn_a, gu_a = lax.optimization_barrier((first_part, dn_a, gu_a))
    input_grad, gain_one_rows, output, grad_three = last_backward_call(
        n_hi, n_lo, n_cx, first_part, out_part, grad_three, inputs, hidden_grad, gain_first[None], hidden
    )
    grad_gl = grad_three[:, : 2 * own_ch]
    grad_proj = grad_three[:, 2 * own_ch :]
    grad_gate = in_order(lo, gu_a[:, :ff_own], gu_b[:, :ff_own], 1).astype(F32)
    grad_up = in_order(
        lo, gu_a[:, ff_pad : ff_pad + ff_own], gu_b[:, ff_pad : ff_pad + ff_own], 1
    ).astype(F32)
    grad_dn = in_order(lo, dn_a[:ff_own], dn_b[:ff_own], 0).astype(F32)

    packed = jnp.concatenate([recur_wg, input_wg, pad_last(sums.T, 128)], axis=1)
    packed = lax.dynamic_slice_in_dim(packed, own_off, own_ch, axis=0)
    packed = jnp.sum(exchange(packed.reshape(n_dp, own_ch // n_dp, packed.shape[1]), DP), axis=0)
    routes = [(d * n_ctx + c, c * n_dp + d) for d in range(n_dp) for c in range(n_ctx)]
    packed = lax.ppermute(packed, EVERY, routes)
    grad_recur_w = packed[:, :bw]
    grad_input_w = packed[:, bw : 2 * bw]
    rest = packed[:, 2 * bw : 2 * bw + 8].T
    gains = jnp.stack([jnp.sum(gain_one_rows, axis=0), jnp.sum(gain_two_rows, axis=0)]).reshape(2, n_dev, piece).transpose(1, 0, 2)
    gains = jnp.sum(exchange(gains, EVERY), axis=0)

    return (
        output,
        input_grad,
        gains[0],
        grad_gl[:, :own_ch],
        grad_gl[:, own_ch:],
        rest[:CONV],
        rest[4],
        grad_recur_w,
        rest[5],
        grad_input_w,
        rest[6],
        rest[7],
        grad_proj,
        gains[1],
        grad_gate,
        grad_up,
        grad_dn,
    )


def solution(mesh):
    n_dp = mesh.shape["dp"]
    n_ctx = mesh.shape["context"]
    inner = Mesh(mesh.devices.reshape(2, n_dp // 2, n_ctx // 2, 2), EVERY)
    rows = P(EVERY, None)
    vec = P(EVERY)
    return jax.shard_map(
        per_device,
        mesh=inner,
        in_specs=(
            rows, P(DP, None), vec, rows, rows, P(None, EVERY), vec, rows, vec, rows, vec, vec, rows, vec,
            rows, rows, rows, rows,
        ),
        out_specs=(
            rows, rows, vec, P(DP, CTX), P(DP, CTX), P(None, EVERY), vec, rows, vec, rows, vec, vec,
            P(DP, CTX), vec, P(DP, CTX), P(DP, CTX), P(CTX, DP),
        ),
        check_vma=False,
    )
```

```python
import functools

import jax
import jax.numpy as jnp
from jax import lax
from jax.experimental import pallas as pl
from jax.experimental.pallas import tpu as pltpu
from jax.sharding import Mesh
from jax.sharding import PartitionSpec as P

HEADS = 10
CONV = 4
CHUNK = 256
BF = jnp.bfloat16
F32 = jnp.float32
DP = ("hi", "lo")
CTX = ("cxy", "core")
CUBE = ("lo", "cxy", "core")
EVERY = ("hi", "lo", "cxy", "core")
SWAP = [(0, 1), (1, 0)]


def dot(a, b, ca, cb):
    return lax.dot_general(a, b, (((ca,), (cb,)), ((), ())), preferred_element_type=F32)


def gelu_parts(x):
    c0 = 0.7978845608028654
    c1 = 0.044715
    x2 = x * x
    th = jnp.tanh(c0 * x * (1.0 + c1 * x2))
    half = 0.5 * (1.0 + th)
    slope = half + 0.5 * x * (1.0 - th * th) * c0 * (1.0 + 3.0 * c1 * x2)
    return x * half, slope


def minus_expm1(x):
    series = 1.0 + x * (1.0 / 8.0)
    for n in range(7, 1, -1):
        series = 1.0 + x * (1.0 / n) * series
    return jnp.where(x > -0.5, -x * series, 1.0 - jnp.exp(x))


def forward_kernel(
    lin_ref, gpre_ref, meta_ref, vec_ref, rw_ref, iw_ref,
    mixed_ref, prev_ref, conv_ref, rec_ref, inp_ref,
    xbuf, dec_s, drv_s, st_s, carry,
):
    rows = lin_ref.shape[0]
    first = pl.program_id(1) == 0

    @pl.when(first)
    def _():
        xbuf[0:8, :] = jnp.zeros((8, xbuf.shape[1]), F32)
        carry[...] = jnp.zeros_like(carry)

    x = lin_ref[...].astype(F32)
    xbuf[8 : 8 + rows, :] = x
    conv = vec_ref[4:5, :] + vec_ref[0:1, :] * x
    for k in range(1, CONV):
        conv = conv + vec_ref[k : k + 1, :] * (xbuf[8 - k : 8 - k + rows, :] * meta_ref[:, k : k + 1])
    xbuf[0:8, :] = x[rows - 8 : rows, :]
    low = conv.astype(BF)
    rec = jax.nn.sigmoid(jnp.dot(low, rw_ref[...], preferred_element_type=F32) + vec_ref[5:6, :])
    inp = jax.nn.sigmoid(jnp.dot(low, iw_ref[...], preferred_element_type=F32) + vec_ref[6:7, :])
    reset = meta_ref[:, 0:1] > 0.5
    log_decay = vec_ref[7:8, :] * rec
    scale = jnp.where(reset, 1.0, jnp.sqrt(minus_expm1(2.0 * log_decay)))
    dec_s[...] = jnp.where(reset, 0.0, jnp.exp(log_decay))
    drv_s[...] = scale * inp * conv
    conv_ref[...] = conv
    rec_ref[...] = rec
    inp_ref[...] = inp
    width = carry.shape[1]
    row = lax.broadcasted_iota(jnp.int32, (8, width), 0)

    def step(i, held):
        at = pl.multiple_of(i * 8, 8)
        a = dec_s[pl.ds(at, 8), :]
        b = drv_s[pl.ds(at, 8), :]
        for s in (1, 2, 4):
            keep = row >= s
            b = a * jnp.where(keep, pltpu.roll(b, s, 0), 0.0) + b
            a = a * jnp.where(keep, pltpu.roll(a, s, 0), 1.0)
        h = a * held + b
        st_s[pl.ds(at, 8), :] = h
        prev_ref[pl.ds(at, 8), :] = jnp.where(row == 0, held, pltpu.roll(h, 1, 0))
        return jnp.broadcast_to(h[7:8, :], (8, width))

    carry[...] = lax.fori_loop(0, rows // 8, step, carry[...], unroll=4)
    gel, _ = gelu_parts(gpre_ref[...])
    mixed_ref[...] = (gel * st_s[...] * vec_ref[8:9, :]).astype(BF)


def backward_kernel(
    mg_ref, gpre_ref, conv_ref, rec_ref, inp_ref, prev_ref, lin_ref, meta_ref, vec_ref, rw_ref, iw_ref,
    glow_ref, llow_ref, rwg_ref, iwg_ref, sum_ref,
    dec_s, sg_s, lam_s, gbuf, carry,
):
    rows = lin_ref.shape[0]
    first = pl.program_id(1) == 0

    @pl.when(first)
    def _():
        carry[...] = jnp.zeros_like(carry)
        for k in range(CONV - 1):
            gbuf[k, rows : rows + 8, :] = jnp.zeros((8, gbuf.shape[2]), F32)
        rwg_ref[...] = jnp.zeros_like(rwg_ref)
        iwg_ref[...] = jnp.zeros_like(iwg_ref)
        sum_ref[...] = jnp.zeros_like(sum_ref)

    mg = mg_ref[...]
    conv = conv_ref[...]
    rec = rec_ref[...]
    inp = inp_ref[...]
    prev = prev_ref[...]
    own = vec_ref[8:9, :]
    gel, slope = gelu_parts(gpre_ref[...])
    reset = meta_ref[:, 0:1] > 0.5
    log_decay = vec_ref[7:8, :] * rec
    scale = jnp.where(reset, 1.0, jnp.sqrt(minus_expm1(2.0 * log_decay)))
    dec = jnp.where(reset, 0.0, jnp.exp(log_decay))
    gated = scale * inp
    states = dec * prev + gated * conv
    glow_ref[...] = (mg * states * slope * own).astype(BF)
    dec_s[...] = dec
    sg_s[...] = mg * gel
    width = carry.shape[1]
    row = lax.broadcasted_iota(jnp.int32, (8, width), 0)
    blocks = rows // 8

    def step(i, held):
        at = pl.multiple_of((blocks - 1 - i) * 8, 8)
        a = dec_s[pl.ds(at, 8), :]
        g = sg_s[pl.ds(at, 8), :]
        b = a * g
        for s in (1, 2, 4):
            keep = row < 8 - s
            b = a * jnp.where(keep, pltpu.roll(b, 8 - s, 0), 0.0) + b
            a = a * jnp.where(keep, pltpu.roll(a, 8 - s, 0), 1.0)
        m = a * held + b
        lam_s[pl.ds(at, 8), :] = g + jnp.where(row == 7, held, pltpu.roll(m, 7, 0))
        return jnp.broadcast_to(m[0:1, :], (8, width))

    carry[...] = lax.fori_loop(0, blocks, step, carry[...], unroll=4)
    lam = lam_s[...]
    conv_gate = lam * gated
    dinp = lam * scale * conv
    dscale = lam * inp * conv
    dlog = jnp.where(reset, 0.0, (lam * prev - dscale * dec / scale) * dec)
    recur_grad = vec_ref[7:8, :] * dlog * rec * (1.0 - rec)
    input_grad = dinp * inp * (1.0 - inp)
    rlow = recur_grad.astype(BF)
    ilow = input_grad.astype(BF)
    low = conv.astype(BF)
    rwg_ref[...] += dot(low, rlow, 0, 0)
    iwg_ref[...] += dot(low, ilow, 0, 0)
    conv_grad = conv_gate + dot(rlow, rw_ref[...], 1, 1) + dot(ilow, iw_ref[...], 1, 1)
    lin = lin_ref[...].astype(F32)
    linear_grad = vec_ref[0:1, :] * conv_grad

    def add(at, value):
        sum_ref[at : at + 1, :] += jnp.sum(value, axis=0, keepdims=True)

    add(0, conv_grad * lin)
    for k in range(1, CONV):
        masked = conv_grad * meta_ref[:, k : k + 1]
        gbuf[k - 1, 0:rows, :] = masked
        moved = gbuf[k - 1, k : k + rows, :]
        gbuf[k - 1, rows : rows + 8, :] = masked[0:8, :]
        linear_grad = linear_grad + vec_ref[k : k + 1, :] * moved
        add(k, moved * lin)
    llow_ref[...] = (linear_grad * own).astype(BF)
    add(4, conv_grad)
    add(5, recur_grad)
    add(6, input_grad)
    add(7, vec_ref[9:10, :] * rec * dlog)


def forward_call(lin, gpre, meta, vecs, rw, iw):
    tokens, win = lin.shape
    bw = rw.shape[1]
    rows = min(CHUNK, tokens)
    grid = (win // bw, tokens // rows)
    tok = pl.BlockSpec((rows, bw), lambda h, j: (j, h))
    mspec = pl.BlockSpec((rows, meta.shape[1]), lambda h, j: (j, 0))
    vspec = pl.BlockSpec((vecs.shape[0], bw), lambda h, j: (0, h))
    wspec = pl.BlockSpec((bw, bw), lambda h, j: (h, 0))
    full = jax.ShapeDtypeStruct((tokens, win), F32)
    return pl.pallas_call(
        forward_kernel,
        grid=grid,
        in_specs=[tok, tok, mspec, vspec, wspec, wspec],
        out_specs=[tok] * 5,
        out_shape=[jax.ShapeDtypeStruct((tokens, win), BF), full, full, full, full],
        scratch_shapes=[
            pltpu.VMEM((rows + 8, bw), F32),
            pltpu.VMEM((rows, bw), F32),
            pltpu.VMEM((rows, bw), F32),
            pltpu.VMEM((rows, bw), F32),
            pltpu.VMEM((8, bw), F32),
        ],
        compiler_params=pltpu.CompilerParams(vmem_limit_bytes=40 << 20),
        cost_estimate=pl.CostEstimate(
            flops=tokens * win * (4 * bw + 100), bytes_accessed=tokens * win * 24, transcendentals=tokens * win * 6
        ),
        name="recur_forward",
    )(lin, gpre, meta, vecs, rw, iw)


def backward_call(mg, gpre, conv, rec, inp, prev, lin, meta, vecs, rw, iw):
    tokens, win = lin.shape
    bw = rw.shape[1]
    rows = min(CHUNK, tokens)
    steps = tokens // rows
    grid = (win // bw, steps)
    tok = pl.BlockSpec((rows, bw), lambda h, j: (steps - 1 - j, h))
    mspec = pl.BlockSpec((rows, meta.shape[1]), lambda h, j: (steps - 1 - j, 0))
    vspec = pl.BlockSpec((vecs.shape[0], bw), lambda h, j: (0, h))
    wspec = pl.BlockSpec((bw, bw), lambda h, j: (h, 0))
    sspec = pl.BlockSpec((8, bw), lambda h, j: (0, h))
    lows = jax.ShapeDtypeStruct((tokens, win), BF)
    wgrad = jax.ShapeDtypeStruct((win, bw), F32)
    return pl.pallas_call(
        backward_kernel,
        grid=grid,
        in_specs=[tok] * 7 + [mspec, vspec, wspec, wspec],
        out_specs=[tok, tok, wspec, wspec, sspec],
        out_shape=[lows, lows, wgrad, wgrad, jax.ShapeDtypeStruct((8, win), F32)],
        scratch_shapes=[
            pltpu.VMEM((rows, bw), F32),
            pltpu.VMEM((rows, bw), F32),
            pltpu.VMEM((rows, bw), F32),
            pltpu.VMEM((CONV - 1, rows + 8, bw), F32),
            pltpu.VMEM((8, bw), F32),
        ],
        compiler_params=pltpu.CompilerParams(vmem_limit_bytes=40 << 20),
        cost_estimate=pl.CostEstimate(
            flops=tokens * win, bytes_accessed=tokens * win, transcendentals=0
        ),
        name="recur_backward",
    )(mg, gpre, conv, rec, inp, prev, lin, meta, vecs, rw, iw)


def exchange(value, axes):
    return lax.all_to_all(value, axes, split_axis=0, concat_axis=0, tiled=True)


def in_order(flag, mine, other, axis):
    return jnp.where(
        flag == 0, jnp.concatenate([mine, other], axis=axis), jnp.concatenate([other, mine], axis=axis)
    )


def send(src, dst, out_sem, in_sem, target):
    return pltpu.make_async_remote_copy(
        src_ref=src, dst_ref=dst, send_sem=out_sem, recv_sem=in_sem,
        device_id=target, device_id_type=pl.DeviceIdType.MESH,
    )


def across():
    return {"hi": 1 - lax.axis_index("hi")}


def sibling():
    return {"core": 1 - lax.axis_index("core")}


def meet(targets):
    barrier = pltpu.get_barrier_semaphore()
    for target in targets:
        pl.semaphore_signal(barrier, inc=1, device_id=target, device_id_type=pl.DeviceIdType.MESH)
    pl.semaphore_wait(barrier, len(targets))


def subsets(bits):
    out = [()]
    for b in bits:
        out += [m + (b,) for m in out]
    return out


def lane_slices(width, parts):
    tiles = width // 128
    cuts = [tiles * i // parts * 128 for i in range(parts + 1)]
    return [pl.ds(a, b - a) for a, b in zip(cuts[:-1], cuts[1:])]


class Group:
    def __init__(self, n_lo, n_cx, cube):
        self.n_cx = n_cx
        self.near = list(range(n_cx.bit_length() - 1))
        self.far = len(self.near)
        self.cube = cube and n_lo == 2
        self.bits = self.near + ([self.far] if self.cube else [])
        self.count = n_cx * (2 if self.cube else 1)
        self.lo = lax.axis_index("lo")
        self.cx = lax.axis_index("cxy")
        self.core = lax.axis_index("core")
        self.place = self.lo * n_cx + self.cx if self.cube else self.cx

    def delta(self, bit):
        stride = 1 << bit
        return stride * (1 - 2 * lax.rem(self.place // stride, 2))

    def at(self, mask):
        spot = self.place
        for bit in mask:
            spot = spot + self.delta(bit)
        return spot

    def partner(self, bit):
        if bit == self.far:
            return {"lo": 1 - self.lo}
        return {"cxy": self.cx + self.delta(bit)}

    def partners(self):
        return [self.partner(bit) for bit in self.bits]

    def orders(self, light):
        if light is None or not self.cube:
            return [self.bits[i:] + self.bits[:i] for i in range(len(self.bits))]
        near = [self.near[i:] + self.near[:i] for i in range(len(self.near))]
        return [[self.far] + o if light == "first" else o + [self.far] for o in near]


class Spread:
    def __init__(self, group, src, out, sems, light=None):
        self.group, self.src, self.out = group, src, out
        self.keep, self.out_sems, self.in_sems, self.pass_sems, self.mate_sems = sems
        self.orders = group.orders(light)
        self.lanes = lane_slices(src.shape[-1], len(self.orders))
        self.moves = []
        index = 0
        for s in range(len(group.bits)):
            row = []
            for order, lanes in zip(self.orders, self.lanes):
                for mask in subsets(order[:s]):
                    row.append((index, lanes, mask, order[s]))
                    index += 1
            self.moves.append(row)

    @staticmethod
    def sems(group_bits, parts):
        moves = parts * ((1 << group_bits) - 1)
        return [
            pltpu.SemaphoreType.DMA(()), pltpu.SemaphoreType.DMA((moves,)), pltpu.SemaphoreType.DMA((moves,)),
            pltpu.SemaphoreType.DMA((moves + 1,)), pltpu.SemaphoreType.DMA((moves + 1,)),
        ]

    def block(self, mask, core):
        return self.group.at(mask) * 2 + core

    def copy(self, move):
        index, lanes, mask, bit = move
        dst = self.out.at[self.block(mask, self.group.core), :, lanes]
        src = dst if mask else self.src.at[:, lanes]
        return send(src, dst, self.out_sems.at[index], self.in_sems.at[index], self.group.partner(bit))

    def relay(self, move, core):
        index, lanes, mask, bit = move
        ref = self.out.at[self.block(mask + (bit,), core), :, lanes]
        return send(ref, ref, self.pass_sems.at[index + 1], self.mate_sems.at[index + 1], sibling())

    def own(self):
        mine = self.out.at[self.block((), self.group.core)]
        local = pltpu.make_async_copy(self.src, mine, self.keep)
        return local, send(self.src, mine, self.pass_sems.at[0], self.mate_sems.at[0], sibling())

    def begin(self):
        self.start(0)
        for copy in self.own():
            copy.start()

    def start(self, s):
        for move in self.moves[s]:
            self.copy(move).start()

    def finish(self, s):
        for move in self.moves[s]:
            index, lanes, mask, bit = move
            came = self.out.at[self.block(mask + (bit,), self.group.core), :, lanes]
            send(came, came, self.out_sems.at[index], self.in_sems.at[index], self.group.partner(bit)).wait_recv()

    def pass_on(self, s):
        for move in self.moves[s]:
            self.relay(move, self.group.core).start()

    def step(self, s):
        self.finish(s)
        if s + 1 < len(self.moves):
            self.start(s + 1)
        self.pass_on(s)

    def end(self):
        local, mate = self.own()
        local.wait()
        mate.wait_send()
        other = self.out.at[self.block((), 1 - self.group.core)]
        send(other, other, self.pass_sems.at[0], self.mate_sems.at[0], sibling()).wait_recv()
        for row in self.moves:
            for move in row:
                self.copy(move).wait_send()
                self.relay(move, self.group.core).wait_send()
                self.relay(move, 1 - self.group.core).wait_recv()


class Fold:
    def __init__(self, group, part, mate_buf, scratch, light=None):
        self.group, self.part, self.mate_buf = group, part, mate_buf
        (self.mine, self.far, self.stage, self.total,
         self.load_sems, self.pass_sems, self.mate_sems, self.out_sems, self.in_sems, self.stage_sems) = scratch
        self.orders = group.orders(light)
        self.lanes = lane_slices(part.shape[-1], len(self.orders))
        self.rows = self.total.shape[0]
        self.moves = []
        index = slot0 = 0
        levels = len(group.bits)
        for s in range(levels):
            row = []
            for order, lanes in zip(self.orders, self.lanes):
                for n, mask in enumerate(subsets(order[s + 1 :])):
                    row.append((index, lanes, mask, order[s], slot0 + n))
                    index += 1
            self.moves.append(row)
            slot0 += 1 << (levels - s - 1)
        masks = []
        for order in self.orders:
            masks += [m for m in subsets(group.bits) if order[0] in m and m not in masks]
        masks += [m for m in subsets(group.bits) if m and m not in masks] + [()]
        self.masks = masks

    @staticmethod
    def scratch(bits, parts, tok, width):
        count = 1 << bits
        moves = parts * (count - 1)
        dma = lambda n: pltpu.SemaphoreType.DMA((n,))
        return [
            pltpu.VMEM((count, tok, width), BF), pltpu.VMEM((count - 1, tok, width), BF),
            pltpu.VMEM((2, tok, width), BF), pltpu.VMEM((tok, width), F32),
            dma(count), dma(count), dma(count), dma(moves), dma(moves), dma(2),
        ]

    def mate(self, n):
        spot = self.group.at(self.masks[n])
        return send(
            self.part.at[spot, 1 - self.group.core], self.mate_buf.at[spot],
            self.pass_sems.at[n], self.mate_sems.at[n], sibling(),
        )

    def load(self, n):
        spot = self.group.at(self.masks[n])
        return pltpu.make_async_copy(self.part.at[spot, self.group.core], self.mine.at[spot], self.load_sems.at[n])

    def fetch(self, n):
        return pltpu.make_async_copy(
            self.mate_buf.at[self.group.at(self.masks[n])], self.stage.at[n % 2], self.stage_sems.at[n % 2]
        )

    def begin(self):
        for n in range(len(self.masks)):
            self.mate(n).start()
            self.load(n).start()

    def pairs(self):
        started = [False] * len(self.orders)
        count = len(self.masks)
        self.mate(0).wait_recv()
        self.fetch(0).start()
        for n, mask in enumerate(self.masks):
            if n + 1 < count:
                self.mate(n + 1).wait_recv()
                self.fetch(n + 1).start()
            self.load(n).wait()
            self.fetch(n).wait()
            spot = self.group.at(mask)

            def add(at, spot=spot, mask=mask, n=n):
                value = self.mine[spot, at, :].astype(F32) + self.stage[n % 2, at, :].astype(F32)
                if mask:
                    self.mine[spot, at, :] = value.astype(BF)
                else:
                    self.total[at, :] = value

            each_rows(self.rows, add)
            for j, order in enumerate(self.orders):
                need = [m for m in self.masks if order[0] in m]
                if not started[j] and all(m in self.masks[: n + 1] for m in need):
                    started[j] = True
                    self.start(0, j)

    def copy(self, move):
        index, lanes, mask, bit, slot = move
        return send(
            self.mine.at[self.group.at(mask + (bit,)), :, lanes], self.far.at[slot, :, lanes],
            self.out_sems.at[index], self.in_sems.at[index], self.group.partner(bit),
        )

    def start(self, s, part=None):
        per = len(self.moves[s]) // len(self.orders)
        for n, move in enumerate(self.moves[s]):
            if part is None or n // per == part:
                self.copy(move).start()

    def take(self, s):
        per = len(self.moves[s]) // len(self.orders)
        for n, move in enumerate(self.moves[s]):
            self.copy(move).wait_recv()
            index, lanes, mask, bit, slot = move
            spot = self.group.at(mask)

            def add(at):
                value = self.far[slot, at, lanes].astype(F32)
                if mask:
                    self.mine[spot, at, lanes] = (self.mine[spot, at, lanes].astype(F32) + value).astype(BF)
                else:
                    self.total[at, lanes] += value

            each_rows(self.rows, add)
            if (n + 1) % per == 0 and s + 1 < len(self.moves):
                self.start(s + 1, n // per)

    def end(self):
        for n in range(len(self.masks)):
            self.mate(n).wait_send()
        for row in self.moves:
            for move in row:
                self.copy(move).wait_send()


def each_rows(rows, body):
    def run(r, held):
        body(pl.ds(pl.multiple_of(r * 16, 16), 16))
        return held

    lax.fori_loop(0, rows // 16, run, 0)


N_FOLD = 10
N_SPREAD = 5


def middle_forward(n_lo, n_cx, part, inputs, gain, hidden, second_all, mate_buf, *scratch):
    fold_s, rest = scratch[:N_FOLD], scratch[N_FOLD:]
    spread_s, (second,) = rest[:N_SPREAD], rest[N_SPREAD:]
    cube = Group(n_lo, n_cx, True)
    plane = Group(n_lo, n_cx, False)
    meet(cube.partners() + [sibling()])
    fold = Fold(plane, part, mate_buf, fold_s)
    fold.begin()
    fold.pairs()
    for s in range(len(plane.bits)):
        fold.take(s)

    def norm(at):
        h = inputs[at, :] + fold.total[at, :]
        hidden[at, :] = h
        r = lax.rsqrt(jnp.mean(h * h, axis=-1, keepdims=True) + 1e-06)
        second[at, :] = (h * r * gain[...]).astype(BF)

    each_rows(fold.rows, norm)
    rows = Spread(cube, second, second_all, spread_s)
    rows.begin()
    for s in range(len(cube.bits)):
        rows.step(s)
    fold.end()
    rows.end()


def norm_back(values, gain, grad, base, out, gain_grad, at):
    v = values[at, :]
    g = grad[at, :]
    r = lax.rsqrt(jnp.mean(v * v, axis=-1, keepdims=True) + 1e-06)
    q = g * gain[...]
    back = base[at, :] + r * q - r * r * r * v * jnp.mean(q * v, axis=-1, keepdims=True)
    out[at, :] = back
    term = g * v * r
    gain_grad[...] += term[0:8, :] + term[8:16, :]
    return back


def middle_backward(n_lo, n_cx, part, hidden, out_grad, gain, hidden_grad, gain_grad, branch_all, mate_buf, *scratch):
    fold_s, rest = scratch[:N_FOLD], scratch[N_FOLD:]
    spread_s, (branch,) = rest[:N_SPREAD], rest[N_SPREAD:]
    cube = Group(n_lo, n_cx, True)
    plane = Group(n_lo, n_cx, False)
    meet(cube.partners() + [sibling()])
    fold = Fold(cube, part, mate_buf, fold_s)
    fold.begin()
    fold.pairs()
    for s in range(len(cube.bits)):
        fold.take(s)
    gain_grad[...] = jnp.zeros_like(gain_grad)

    def norm(at):
        branch[at, :] = norm_back(hidden, gain, fold.total, out_grad, hidden_grad, gain_grad, at).astype(BF)

    each_rows(fold.rows, norm)
    rows = Spread(plane, branch, branch_all, spread_s)
    rows.begin()
    for s in range(len(plane.bits)):
        rows.step(s)
    fold.end()
    rows.end()


class Chain:
    def __init__(self, z, count, part, blocks, came, sems, along):
        self.z, self.count, self.part, self.blocks, self.came, self.along = z, count, part, blocks, came, along
        self.load_sems, self.out_sems, self.in_sems = sems

    @staticmethod
    def scratch(parts, count, rows, cols):
        hops = 2 * (count - 1)
        return [pltpu.VMEM((count, rows, cols), BF), pltpu.VMEM((hops, rows, cols), BF)] + dma_sems(
            parts * count, hops, hops
        )

    def loads(self, d):
        first = 0
        for i, part in enumerate(self.part):
            cols = part.shape[2]
            dst = self.blocks.at[d, :, pl.ds(first, cols)] if len(self.part) > 1 else self.blocks.at[d]
            yield pltpu.make_async_copy(part.at[d], dst, self.load_sems.at[len(self.part) * d + i])
            first += cols

    def begin(self):
        for d in range(self.count):
            for copy in self.loads(d):
                copy.start()

    def ready(self):
        for d in range(self.count):
            for copy in self.loads(d):
                copy.wait()

    def sides(self, k):
        last = self.count - 1
        z = self.z
        yield 0, 1, jnp.logical_and(z <= k, z < last), jnp.logical_and(z >= 1, z <= k + 1)
        yield 1, -1, jnp.logical_and(z >= last - k, z > 0), jnp.logical_and(z <= last - 1, z >= last - 1 - k)

    def copy(self, side, way, k):
        at = side * (self.count - 1) + k
        block = self.blocks.at[self.z + way * (self.count - 1 - k)]
        return send(block, self.came.at[at], self.out_sems.at[at], self.in_sems.at[at], self.along(self.z + way))

    def start(self, k):
        for side, way, sends, _ in self.sides(k):
            @pl.when(sends)
            def _():
                self.copy(side, way, k).start()

    def take(self, k, total):
        final = k == self.count - 2
        for side, way, _, comes in self.sides(k):
            at = side * (self.count - 1) + k

            @pl.when(comes)
            def _():
                land = self.came.at[at]
                send(land, land, self.out_sems.at[at], self.in_sems.at[at], self.along(self.z - way)).wait_recv()

                def add(rows):
                    value = self.came[at, rows, :].astype(F32)
                    if final:
                        total[rows, :] += value
                    else:
                        spot = self.z + way * (self.count - 2 - k)
                        self.blocks[spot, rows, :] = (self.blocks[spot, rows, :].astype(F32) + value).astype(BF)

                each_rows(total.shape[0], add)

    def own(self, total):
        def put(rows):
            total[rows, :] = self.blocks[self.z, rows, :].astype(F32)

        each_rows(total.shape[0], put)

    def end(self):
        for k in range(self.count - 1):
            for side, way, sends, _ in self.sides(k):
                @pl.when(sends)
                def _():
                    self.copy(side, way, k).wait_send()


N_CHAIN = 5


def everywhere(n_hi, n_lo, n_cx):
    n_ctx = 2 * n_cx
    n_cube = n_lo * n_ctx
    number = (lax.axis_index("hi") * n_lo + lax.axis_index("lo")) * n_ctx + lax.axis_index("cxy") * 2
    number = number + lax.axis_index("core")

    def device(i):
        return {
            "hi": i // n_cube, "lo": lax.rem(i, n_cube) // n_ctx, "cxy": lax.rem(i, n_ctx) // 2, "core": lax.rem(i, 2),
        }

    return number, device, n_hi * n_cube


def meet_all(number, device, n_dev):
    barrier = pltpu.get_barrier_semaphore()

    def greet(i, held):
        other = device(lax.rem(number + i, n_dev))
        pl.semaphore_signal(barrier, inc=1, device_id=other, device_id_type=pl.DeviceIdType.MESH)
        return held

    lax.fori_loop(1, n_dev, greet, 0)
    pl.semaphore_wait(barrier, n_dev - 1)


def ff_block(u, n_lo, n_cx):
    lo, ctx = u // (2 * n_cx), u % (2 * n_cx)
    return (ctx % 2) * (n_lo * n_cx) + lo * n_cx + ctx // 2


class Exchange:
    def __init__(self, number, device, n_dev, src, came, sems, split):
        self.number, self.device, self.n_dev, self.split = number, device, n_dev, split
        self.src, self.came, (self.out_sems, self.in_sems) = src, came, sems

    def copy(self, i):
        to = lax.rem(self.number + i, self.n_dev)
        src = self.src.at[to] if self.split else self.src
        return send(src, self.came.at[self.number], self.out_sems.at[i], self.in_sems.at[i], self.device(to))

    def start(self):
        def run(i, held):
            self.copy(i).start()
            return held

        lax.fori_loop(1, self.n_dev, run, 0)

    def recv(self):
        def run(i, held):
            source = lax.rem(self.number - i + self.n_dev, self.n_dev)
            land = self.came.at[source]
            send(land, land, self.out_sems.at[i], self.in_sems.at[i], self.device(source)).wait_recv()
            return held

        lax.fori_loop(1, self.n_dev, run, 0)

    def end(self):
        def run(i, held):
            self.copy(i).wait_send()
            return held

        lax.fori_loop(1, self.n_dev, run, 0)


N_CHAIN = 5


def last_backward(n_lo, n_cx, n_hi, with_out, n_sums, part, *refs):
    sums, packed, refs = refs[:n_sums], refs[n_sums], refs[n_sums + 1 :]
    if with_out:
        (out_part, inputs, hidden_grad, gain, hidden, input_grad, gain_rows, packed_sum, summed, mate_a, output, mate_b,
         *scratch) = refs
    else:
        inputs, hidden_grad, gain, hidden, input_grad, gain_rows, packed_sum, summed, mate_a, *scratch = refs
    fold_a, rest = scratch[:N_FOLD], scratch[N_FOLD:]
    chain_s, rest = rest[:N_CHAIN], rest[N_CHAIN:]
    (pack_came, p_own, p_out, p_in), fold_b = rest[:4], rest[4:]
    cube = Group(n_lo, n_cx, True)
    plane = Group(n_lo, n_cx, False)
    n_dp = n_hi * n_lo
    z = lax.axis_index("hi") * n_lo + lax.axis_index("lo")
    along = lambda d: {"hi": d // n_lo, "lo": lax.rem(d, n_lo)}
    meet([cube.partner(b) for b in cube.near] + [sibling()] + [along(lax.rem(z + i, n_dp)) for i in range(1, n_dp)])
    first = Fold(plane, part, mate_a, fold_a)
    chain = Chain(z, n_dp, sums, chain_s[0], chain_s[1], chain_s[2:], along)
    chain.begin()
    first.begin()
    if with_out:
        outs = Fold(cube, out_part, mate_b, fold_b, "last")
        outs.begin()
    others = [lax.rem(z + i, n_dp) for i in range(1, n_dp)]
    pushes = [
        send(packed.at[d], pack_came.at[i + 1], p_out.at[i], p_in.at[i], along(d)) for i, d in enumerate(others)
    ]
    own_pack = pltpu.make_async_copy(packed.at[z], pack_came.at[0], p_own)
    own_pack.start()
    for push in pushes:
        push.start()
    hops = n_dp - 1
    chain.ready()
    chain.start(0)
    chain.own(summed)
    first.pairs()
    if with_out:
        outs.pairs()
    first.take(0)
    for k in range(hops - 1):
        chain.take(k, summed)
        chain.start(k + 1)
        if k + 1 < len(plane.bits):
            first.take(k + 1)
        if with_out and k + 1 < len(cube.bits):
            outs.take(k)
    for s in range(hops, len(plane.bits)):
        first.take(s)
    gain_rows[...] = jnp.zeros_like(gain_rows)

    def norm(at):
        norm_back(inputs, gain, first.total, hidden_grad, input_grad, gain_rows, at)

    each_rows(first.rows, norm)
    if with_out:
        for s in range(min(hops - 1, len(cube.bits) - 1), len(cube.bits)):
            outs.take(s)

        def finish(at):
            output[at, :] = hidden[at, :] + outs.total[at, :]

        each_rows(outs.rows, finish)
    own_pack.wait()
    value = pack_came[0]
    for i, push in enumerate(pushes):
        push.wait_recv()
        value = value + pack_came[i + 1]
    packed_sum[...] = value
    chain.take(hops - 1, summed)
    for push in pushes:
        push.wait_send()
    first.end()
    if with_out:
        outs.end()
    chain.end()


def comm_call(kernel, name, number, raw, args, outs, scratch, micros):
    any_spec = pl.BlockSpec(memory_space=pl.ANY)
    vmem = pl.BlockSpec(memory_space=pltpu.VMEM)
    return pl.pallas_call(
        kernel,
        in_specs=[any_spec] * len(raw) + [vmem] * len(args),
        out_specs=[vmem if inside else any_spec for _, inside in outs],
        out_shape=[shape for shape, _ in outs],
        scratch_shapes=scratch,
        compiler_params=pltpu.CompilerParams(
            collective_id=number, has_side_effects=True, vmem_limit_bytes=56 << 20
        ),
        cost_estimate=pl.CostEstimate(flops=micros * 10**9, bytes_accessed=micros * 10**6, transcendentals=0),
        name=name,
    )(*raw, *args)


def dma_sems(*counts):
    return [pltpu.SemaphoreType.DMA((n,) if n else ()) for n in counts]


def middle_forward_call(n_lo, n_cx, part, inputs, gain):
    tok, width = inputs.shape
    near = n_cx.bit_length() - 1
    far = near + n_lo - 1
    rows = jax.ShapeDtypeStruct((tok, width), F32)
    sds = lambda *shape: jax.ShapeDtypeStruct(shape, BF)
    hidden, second_all, _ = comm_call(
        functools.partial(middle_forward, n_lo, n_cx), "sum_norm_gather_forward", 1,
        (part.reshape(n_cx, 2, tok, width),), (inputs, gain),
        [(rows, True), (sds(n_lo * n_cx * 2, tok, width), False), (sds(n_cx, tok, width), False)],
        Fold.scratch(near, near, tok, width) + Spread.sems(far, far) + [pltpu.VMEM((tok, width), BF)], 1,
    )
    return hidden, second_all.reshape(-1, width)


def middle_backward_call(n_lo, n_cx, part, hidden, out_grad, gain):
    tok, width = hidden.shape
    near = n_cx.bit_length() - 1
    far = near + n_lo - 1
    rows = jax.ShapeDtypeStruct((tok, width), F32)
    sds = lambda *shape: jax.ShapeDtypeStruct(shape, BF)
    hidden_grad, gain_grad, branch_all, _ = comm_call(
        functools.partial(middle_backward, n_lo, n_cx), "sum_norm_gather_backward", 2,
        (part.reshape(n_lo * n_cx, 2, tok, width),), (hidden, out_grad, gain),
        [(rows, True), (jax.ShapeDtypeStruct((8, width), F32), True), (sds(n_cx * 2, tok, width), False),
         (sds(n_lo * n_cx, tok, width), False)],
        Fold.scratch(far, far, tok, width) + Spread.sems(near, near) + [pltpu.VMEM((tok, width), BF)], 100,
    )
    return hidden_grad, gain_grad, branch_all.reshape(-1, width)


def last_backward_call(n_hi, n_lo, n_cx, part, out_part, sums, packed, inputs, hidden_grad, gain, hidden):
    tok, width = inputs.shape
    near = n_cx.bit_length() - 1
    far = near + n_lo - 1
    n_dp = n_hi * n_lo
    with_out = n_lo * n_cx <= 8
    rows = jax.ShapeDtypeStruct((tok, width), F32)
    sds = lambda *shape: jax.ShapeDtypeStruct(shape, BF)
    full = lambda *shape: jax.ShapeDtypeStruct(shape, F32)
    if any(p.shape[1] % 128 for p in sums):
        sums = [jnp.concatenate(sums, axis=1)]
    sums = [p.reshape(n_dp, -1, p.shape[1]) for p in sums]
    summed_shape = (*sums[0].shape[1:2], sum(p.shape[2] for p in sums))
    packed = packed.reshape(n_dp, -1, packed.shape[1])
    raw = (part.reshape(n_cx, 2, tok, width), *sums, packed)
    outs = [(rows, True), (full(8, width), True), (full(*packed.shape[1:]), True), (full(*summed_shape), True),
            (sds(n_cx, tok, width), False)]
    scratch = Fold.scratch(near, near, tok, width) + Chain.scratch(len(sums), n_dp, *summed_shape)
    scratch += [pltpu.VMEM(packed.shape, F32)] + dma_sems(0, n_dp - 1, n_dp - 1)
    if with_out:
        raw += (out_part.reshape(n_lo * n_cx, 2, tok, width),)
        outs += [(rows, True), (sds(n_lo * n_cx, tok, width), False)]
        scratch += Fold.scratch(far, near, tok, width)
    got = comm_call(
        functools.partial(last_backward, n_lo, n_cx, n_hi, with_out, len(sums)), "sum_norm_backward", 3,
        raw, (inputs, hidden_grad, gain, hidden), outs, scratch, 1,
    )
    input_grad, gain_rows, packed_sum, summed = got[:4]
    if with_out:
        output = got[5]
    else:
        output = hidden + lax.psum_scatter(out_part, CUBE, scatter_dimension=0, tiled=True).astype(F32)
    return input_grad, gain_rows, packed_sum, output, summed


class Line:
    def __init__(self, n_hi, n_lo):
        self.n_lo = n_lo
        self.count = n_hi * n_lo
        self.z = lax.axis_index("hi") * n_lo + lax.axis_index("lo")

    def device(self, z):
        return {"hi": z // self.n_lo, "lo": lax.rem(z, self.n_lo)}

    def run(self, part, sems, k, action):
        out_sems, in_sems, pass_sems, mate_sems = sems
        last = self.count - 1
        z = self.z
        for side, way in ((0, 1), (1, -1)):
            if way == 1:
                sends = jnp.logical_and(z >= k, z < last)
                comes = z >= k + 1
            else:
                sends = jnp.logical_and(z <= last - k, z > 0)
                comes = z <= last - 1 - k
            at = side * last + k
            if action in ("recv", "mate_recv"):
                @pl.when(comes)
                def _():
                    if action == "recv":
                        plane = part(z - way * (k + 1), False)
                        send(plane, plane, out_sems.at[at], in_sems.at[at], self.device(z - way)).wait_recv()
                        if pass_sems is not None:
                            send(plane, plane, pass_sems.at[at], mate_sems.at[at], sibling()).start()
                    else:
                        plane = part(z - way * (k + 1), False)
                        send(plane, plane, pass_sems.at[at], mate_sems.at[at], sibling()).wait_send()
                        plane = part(z - way * (k + 1), True)
                        send(plane, plane, pass_sems.at[at], mate_sems.at[at], sibling()).wait_recv()
            else:
                @pl.when(sends)
                def _():
                    plane = part(z - way * k, False)
                    copy = send(plane, plane, out_sems.at[at], in_sems.at[at], self.device(z + way))
                    if action == "start":
                        copy.start()
                    else:
                        copy.wait_send()


def clamp_head(head, top):
    return head - head // (top + 1) * (head - top)


def window_head(c, own_ch, bw, span):
    return clamp_head(own_ch * c // bw, HEADS - span)


def chip_head(chip, own_ch, bw, span):
    return clamp_head(window_head(2 * chip, own_ch, bw, span), HEADS - span - 1)


def window_shard(head, n_dev, n_ctx, span):
    return head * ((n_dev - n_ctx) // (HEADS - span))


def gather_start(sizes, gelu_w, lin_w, proj, rgate, igate, small, down, gate_w, up_w, inputs,
                 gl_out, gu_out, pg_z, pg_win, normed_all, down_other, small_all,
                 gu_send, own_pg, own_gl, own_rest, gl_s, gl_r, mate_s, mate_r, gu_s, gu_r, win_s, win_r,
                 zp_s, zp_r, zg_s, zg_r, zm_s, zm_r, dn_s, dn_r,
                 normed, small_came, sm_own, sm_s, sm_r, *spread_s):
    n_hi, n_lo, n_cx, n_core, own_ch, bw, span = sizes
    n_ctx = n_cx * n_core
    n_cube = n_lo * n_ctx
    n_dev = n_hi * n_cube
    hi = lax.axis_index("hi")
    lo = lax.axis_index("lo")
    cx = lax.axis_index("cxy")
    core = lax.axis_index("core")
    ctx = cx * n_core + core
    spot = lo * n_ctx + ctx
    number = hi * n_cube + spot
    line = Line(n_hi, n_lo)
    z = line.z
    wide = (span + 1) * bw
    width = proj.shape[1]
    in_plane = lambda c: {"cxy": c // n_core, "core": lax.rem(c, n_core)}
    in_cube = lambda u: {"lo": u // n_ctx, **in_plane(lax.rem(u, n_ctx))}

    _, device, _ = everywhere(n_hi, n_lo, n_cx)
    meet_all(number, device, n_dev)
    vectors = Exchange(number, device, n_dev, small, small_came, (sm_s, sm_r), False)
    vectors.start()
    own_small = pltpu.make_async_copy(small, small_came.at[number], sm_own)
    own_small.start()

    pg_parts = [(proj, 0, width), (rgate, width, bw), (igate, width + bw, bw)]
    pg_own = [
        pltpu.make_async_copy(ref, pg_z.at[z, :, pl.ds(a, n)], own_pg.at[i]) for i, (ref, a, n) in enumerate(pg_parts)
    ]
    for copy in pg_own:
        copy.start()

    def columns(ref, chip):
        at = pl.multiple_of(chip_head(chip, own_ch, bw, span) * bw, bw)
        return ref.at[:, pl.ds(at, wide)]

    mine = lambda i: gl_out.at[z, cx, core, :, pl.ds(i * wide, wide)]
    gl_own = [pltpu.make_async_copy(columns(ref, cx), mine(i), own_gl.at[i]) for i, ref in enumerate((gelu_w, lin_w))]
    gl_copies = []
    for s in range(1, n_cx):
        to = lax.rem(cx + s, n_cx)
        for i, ref in enumerate((gelu_w, lin_w)):
            gl_copies.append(
                send(columns(ref, to), mine(i), gl_s.at[2 * s + i], gl_r.at[2 * s + i], {"cxy": to})
            )
            gl_copies[-1].start()
    for copy in gl_own:
        copy.start()
    pg_part = lambda plane, other: pg_z.at[plane]
    gl_part = lambda plane, other: gl_out.at[plane, :, 1 - core if other else core]
    pg_sems, gl_sems = (zp_s, zp_r, None, None), (zg_s, zg_r, zm_s, zm_r)
    steps = line.count - 1
    for copy in pg_own:
        copy.wait()
    line.run(pg_part, pg_sems, 0, "start")
    own_small.wait()
    vectors.recv()
    piece = width // n_dev
    for d in range(n_dev):
        small_all[:, d * piece : (d + 1) * piece] = small_came[d, :, 0:piece]
    gain = small_all[0:1, :].astype(F32)

    def norm(at):
        x = inputs[at, :]
        r = lax.rsqrt(jnp.mean(x * x, axis=-1, keepdims=True) + 1e-06)
        normed[at, :] = (x * r * gain).astype(BF)

    each_rows(normed.shape[0], norm)
    rows = Spread(Group(n_lo, n_cx, False), normed, normed_all, spread_s)
    rows.begin()
    for copy in gl_own:
        copy.wait()
    for s in range(1, n_cx):
        for i in range(2):
            came = gl_out.at[z, lax.rem(cx - s + n_cx, n_cx), core, :, pl.ds(i * wide, wide)]
            send(came, came, gl_s.at[2 * s + i], gl_r.at[2 * s + i], {"cxy": lax.rem(cx + s, n_cx)}).wait_recv()
    line.run(gl_part, gl_sems, 0, "start")
    own_plane = gl_part(z, False)
    own_mate = send(own_plane, own_plane, mate_s, mate_r, sibling())
    own_mate.start()

    ff_own = gate_w.shape[1] // n_cube
    ff_pad = gu_send.shape[2] // 2
    shard_rows = gate_w.shape[0]
    for u in range(n_cube):
        first = ff_block(u, n_lo, n_cx) * ff_own
        for i, ref in enumerate((gate_w, up_w)):
            gu_send[u, :, i * ff_pad : i * ff_pad + ff_own] = ref[:, first : first + ff_own]
            if ff_pad > ff_own:
                gu_send[u, :, i * ff_pad + ff_own : (i + 1) * ff_pad] = jnp.zeros((shard_rows, ff_pad - ff_own), BF)

    for k in range(1, steps):
        line.run(pg_part, pg_sems, k - 1, "recv")
        line.run(pg_part, pg_sems, k, "start")
    for s in range(len(rows.moves)):
        rows.step(s)
    line.run(pg_part, pg_sems, steps - 1, "recv")

    def window(src, dst):
        first = window_shard(window_head(dst, own_ch, bw, span), n_dev, n_ctx, span)
        turn = lax.rem(src - first + n_dev, n_ctx)
        return (first + turn) // n_ctx, turn

    shard, turn = window(ctx, ctx)
    own_window = pltpu.make_async_copy(pg_z.at[shard], pg_win.at[turn], own_rest.at[0])
    own_window.start()
    win_copies = []
    for s in range(1, n_ctx):
        to = lax.rem(ctx + s, n_ctx)
        shard, turn = window(ctx, to)
        win_copies.append(send(pg_z.at[shard], pg_win.at[turn], win_s.at[s], win_r.at[s], in_plane(to)))
        win_copies[-1].start()
    line.run(gl_part, gl_sems, 0, "recv")
    if steps > 1:
        line.run(gl_part, gl_sems, 1, "start")
    own_gu = pltpu.make_async_copy(gu_send.at[spot], gu_out.at[spot], own_rest.at[1])
    own_gu.start()
    gu_copies = []
    for s in range(1, n_cube):
        to = lax.rem(spot + s, n_cube)
        gu_copies.append(send(gu_send.at[to], gu_out.at[spot], gu_s.at[s], gu_r.at[s], in_cube(to)))
        gu_copies[-1].start()
    down_copy = send(down, down_other, dn_s, dn_r, across())
    for k in range(2, steps):
        line.run(gl_part, gl_sems, k - 1, "recv")
        line.run(gl_part, gl_sems, k, "start")
    down_copy.start()
    line.run(gl_part, gl_sems, steps - 1, "recv")
    rows.end()
    for s in range(1, n_ctx):
        _, turn = window(lax.rem(ctx - s + n_ctx, n_ctx), ctx)
        came = pg_win.at[turn]
        send(came, came, win_s.at[s], win_r.at[s], in_plane(lax.rem(ctx + s, n_ctx))).wait_recv()
    for s in range(1, n_cube):
        came = gu_out.at[lax.rem(spot - s + n_cube, n_cube)]
        send(came, came, gu_s.at[s], gu_r.at[s], in_cube(lax.rem(spot + s, n_cube))).wait_recv()
    own_window.wait()
    own_gu.wait()
    for copy in gl_copies + win_copies + gu_copies:
        copy.wait_send()
    own_mate.wait_send()
    other_plane = gl_part(z, True)
    send(other_plane, other_plane, mate_s, mate_r, sibling()).wait_recv()
    for k in range(steps):
        line.run(pg_part, pg_sems, k, "sent")
        line.run(gl_part, gl_sems, k, "sent")
        line.run(gl_part, gl_sems, k, "mate_recv")
    down_copy.wait()
    vectors.end()


def gather_start_call(sizes, gelu_w, lin_w, proj, rgate, igate, small, down, gate_w, up_w, inputs, ff_pad):
    n_hi, n_lo, n_cx, n_core, own_ch, bw, span = sizes
    n_ctx = n_cx * n_core
    n_cube = n_lo * n_ctx
    n_dp = n_hi * n_lo
    shard, width = proj.shape
    near = n_cx.bit_length() - 1
    wide = (span + 1) * bw
    sds = lambda *shape: jax.ShapeDtypeStruct(shape, BF)
    any_spec = pl.BlockSpec(memory_space=pl.ANY)
    vmem = pl.BlockSpec(memory_space=pltpu.VMEM)
    pg_width = width + 2 * bw
    hops = 2 * (n_dp - 1)
    gl_out, gu_out, _, pg_win, normed_all, down_other, small_all = pl.pallas_call(
        functools.partial(gather_start, sizes),
        in_specs=[any_spec] * 7 + [vmem] * 3,
        out_specs=[any_spec] * 6 + [vmem],
        out_shape=[
            sds(n_dp, n_cx, n_core, shard, 2 * wide), sds(n_cube, shard, 2 * ff_pad), sds(n_dp, shard, pg_width),
            sds(n_ctx, shard, pg_width), sds(n_ctx, *inputs.shape), sds(*down.shape),
            sds(small.shape[0], width),
        ],
        scratch_shapes=[pltpu.VMEM((n_cube, shard, 2 * ff_pad), BF)]
        + dma_sems(3, 2, 2, 2 * n_cx, 2 * n_cx, 0, 0, n_cube, n_cube, n_ctx, n_ctx, hops, hops, hops, hops, hops, hops, 0, 0)
        + [pltpu.VMEM(inputs.shape, BF), pltpu.VMEM((n_dp * n_ctx, *small.shape), BF)]
        + dma_sems(0, n_dp * n_ctx, n_dp * n_ctx) + Spread.sems(near, near),
        compiler_params=pltpu.CompilerParams(collective_id=4, has_side_effects=True, vmem_limit_bytes=40 << 20),
        cost_estimate=pl.CostEstimate(flops=10**11, bytes_accessed=10**8, transcendentals=0),
        name="gather_start",
    )(gelu_w, lin_w, proj, rgate, igate, small, down, gate_w, up_w, inputs)
    return gl_out.reshape(width, 2 * wide), gu_out.reshape(-1, 2 * ff_pad), pg_win.reshape(-1, pg_width), normed_all.reshape(-1, width), down_other, small_all


def swap_first(value):
    return lax.ppermute(value, DP, [(0, 1), (3, 2)]), lax.ppermute(value, DP, [(1, 2), (2, 1)])


def swap_second(to_inner, crossed):
    return lax.ppermute(to_inner, DP, [(1, 2), (2, 1)]), lax.ppermute(crossed, DP, [(1, 0), (2, 3)])


def pad_last(value, width):
    extra = width - value.shape[-1]
    return value if extra == 0 else jnp.pad(value, [(0, 0)] * (value.ndim - 1) + [(0, extra)])


def per_device(
    inputs, segment_ids, first_gain, gelu_in_w, linear_in_w, conv_weight, conv_bias, recur_gate_w, recur_gate_b,
    input_gate_w, input_gate_b, decay_param, out_proj_w, second_gain, mlp_gate_w, mlp_up_w, mlp_down_w, out_grad,
):
    n_hi, n_lo, n_cx, n_core = (lax.axis_size(a) for a in EVERY)
    hi, lo, cx, core = (lax.axis_index(a) for a in EVERY)
    n_ctx = n_cx * n_core
    n_dp = n_hi * n_lo
    n_dev = n_dp * n_ctx
    ctx = cx * n_core + core
    tok, width = inputs.shape
    tokens = segment_ids.shape[1]
    chans = linear_in_w.shape[1]
    bw = recur_gate_w.shape[1]
    hidden_units = mlp_gate_w.shape[1]
    own_ch = chans // n_ctx
    span = max((own_ch * (c + 1) - 1) // bw - own_ch * c // bw + 1 for c in range(n_ctx))
    win = span * bw
    head0 = window_head(ctx, own_ch, bw, span)
    ch0 = head0 * bw
    own_off = own_ch * ctx - ch0
    ff_own = hidden_units // (n_lo * n_ctx)
    ff_pad = -(-ff_own // 128) * 128

    piece = width // n_dev
    small = jnp.concatenate(
        [v[None] for v in (first_gain, second_gain)]
        + [conv_weight]
        + [v[None] for v in (conv_bias, recur_gate_b, input_gate_b, decay_param)],
        axis=0,
    )
    small = jnp.pad(small, ((0, 16 - small.shape[0]), (0, 128 - piece)))

    sizes = (n_hi, n_lo, n_cx, n_core, own_ch, bw, span)
    gl_w, gu_mine, pg_win, normed_all, down_other, small_all = gather_start_call(
        sizes, gelu_in_w, linear_in_w, out_proj_w, recur_gate_w, input_gate_w, small, mlp_down_w,
        mlp_gate_w, mlp_up_w, inputs, ff_pad,
    )
    small_all = small_all.astype(F32)
    gain_first = small_all[0]
    gain_second = small_all[1]
    wide = win + bw
    chip_off = (head0 - chip_head(cx, own_ch, bw, span)) * bw
    gelu_w = lax.dynamic_slice_in_dim(gl_w[:, :wide], chip_off, win, axis=1)
    lin_w = lax.dynamic_slice_in_dim(gl_w[:, wide:], chip_off, win, axis=1)
    pg_win = lax.dynamic_slice_in_dim(pg_win, ch0 - window_shard(head0, n_dev, n_ctx, span) * piece, win)
    proj_w = pg_win[:, :width]
    recur_w = pg_win[:, width : width + bw]
    input_w = pg_win[:, width + bw :]

    gu_other = lax.ppermute(gu_mine, "hi", SWAP)
    n_cube = n_lo * n_ctx
    keeps = hi == core
    down_keep = jnp.where(keeps, mlp_down_w, down_other)
    down_came = lax.ppermute(jnp.where(keeps, down_other, mlp_down_w), "core", SWAP)
    down_w = in_order(core, down_keep, down_came, 0)
    down_w = jnp.pad(down_w, ((0, ff_pad - ff_own), (0, 0)))
    cot = lax.optimization_barrier((out_grad.astype(BF), down_other))[0]
    down_grad = lax.all_gather(cot, CUBE, axis=0, tiled=True)

    ids = segment_ids[0]
    metas = [jnp.concatenate([jnp.ones((1,), F32), (ids[1:] != ids[:-1]).astype(F32)])]
    for k in range(1, CONV):
        metas.append(jnp.concatenate([jnp.zeros((k,), F32), (ids[k:] == ids[:-k]).astype(F32)]))
    meta = jnp.stack(metas, axis=1)
    vec_win = lax.dynamic_slice_in_dim(small_all[2:10], ch0, win, axis=1)
    decay_win = vec_win[7:8]
    place_in = jnp.arange(win) - own_off
    own_mask = ((place_in >= 0) & (place_in < own_ch)).astype(F32)[None]
    vecs = jnp.concatenate(
        [
            vec_win[:7],
            -8.0 * jax.nn.softplus(decay_win),
            own_mask,
            -8.0 * jax.nn.sigmoid(decay_win),
            jnp.zeros((6, win), F32),
        ],
        axis=0,
    )
    gelu_pre = dot(normed_all, gelu_w, 1, 0)
    linear_out = dot(normed_all, lin_w, 1, 0).astype(BF)
    mixed, prev, conv_out, rec, inp = forward_call(linear_out, gelu_pre, meta, vecs, recur_w, input_w)
    proj_part = dot(mixed, proj_w, 1, 0).astype(BF)
    hidden, second_all = middle_forward_call(n_lo, n_cx, proj_part, inputs, gain_second[None])
    gu_w = in_order(hi, gu_mine, gu_other, 0)

    pre = dot(second_all, gu_w, 1, 0)
    gate_pre, up_pre = pre[:, :ff_pad], pre[:, ff_pad:]
    act_grad = dot(down_grad, down_w, 1, 1)
    gel, slope = gelu_parts(gate_pre)
    activation = (gel * up_pre).astype(BF)
    gu_low = jnp.concatenate([(act_grad * up_pre * slope).astype(BF), (act_grad * gel).astype(BF)], axis=1)
    second_part = dot(gu_low, gu_w, 1, 1).astype(BF)

    def half_of(partial, which, axis, parts):
        size = partial.shape[axis] // parts
        return lax.dynamic_slice_in_dim(partial, which * size, size, axis)

    gu_stage = swap_first(dot(half_of(second_all, 1 - hi, 1, n_hi), gu_low, 0, 0).astype(BF))
    dn_stage = swap_first(dot(activation, half_of(down_grad, 1 - hi, 1, n_hi), 0, 0).astype(BF))
    hidden_grad, gain_two_rows, branch_all = middle_backward_call(
        n_lo, n_cx, second_part, hidden, out_grad, gain_second[None]
    )

    branch_all, *stages = lax.optimization_barrier((branch_all,) + gu_stage + dn_stage)
    dn_stage = swap_second(*stages[2:])
    gu_stage = swap_second(*stages[:2])
    inner = hi != lo

    late_second, late_cot = lax.optimization_barrier((second_all, down_grad, branch_all))[:2]
    own_gu = dot(half_of(late_second, hi, 1, n_hi), gu_low, 0, 0).astype(BF)
    own_dn = dot(activation, half_of(late_cot, hi, 1, n_hi), 0, 0).astype(BF)

    turns = [
        [
            (u, ((u % n_ctx // 2 + s) % 2) * n_ctx + ff_block(u, n_lo, n_cx) // 2)
            for u in range(n_cube)
        ]
        for s in range(2)
    ]

    def settle(partial, got, axis):
        both = (partial.astype(F32) + got.astype(F32)).astype(BF)
        odd = lax.rem(cx, 2)
        return tuple(lax.ppermute(half_of(both, lax.rem(odd + s, 2), axis, n_lo), CUBE, turns[s]) for s in range(2))

    out_part = dot(activation, lax.optimization_barrier((down_w, gain_two_rows))[0], 1, 0).astype(BF)

    own_mixed = lax.dynamic_slice_in_dim(mixed, own_off, own_ch, axis=1)
    grad_proj = dot(own_mixed, branch_all, 0, 0).astype(BF).reshape(own_ch, n_ctx, width // n_ctx)
    grad_proj = grad_proj.transpose(1, 0, 2)
    mixed_grad = dot(branch_all, proj_w, 1, 1)
    mixed_grad, own_gu, own_dn, out_part, grad_proj = lax.optimization_barrier(
        (mixed_grad, own_gu, own_dn, out_part, grad_proj)
    )
    grad_proj = exchange(grad_proj, CTX).reshape(chans, width // n_ctx)
    gelu_low, linear_low, recur_wg, input_wg, sums = backward_call(
        mixed_grad, gelu_pre, conv_out, rec, inp, prev, linear_out, meta, vecs, recur_w, input_w
    )
    gelu_low, linear_low, *stages = lax.optimization_barrier((gelu_low, linear_low, *dn_stage, *gu_stage))
    got_dn = jnp.where(inner, *stages[:2])
    got_gu = jnp.where(inner, *stages[2:])
    own_lows = jnp.concatenate(
        [
            lax.dynamic_slice_in_dim(gelu_low, own_off, own_ch, axis=1),
            lax.dynamic_slice_in_dim(linear_low, own_off, own_ch, axis=1),
        ],
        axis=1,
    )
    grad_gl = dot(normed_all, own_lows, 0, 0).astype(BF)
    first_part = dot(
        jnp.concatenate([gelu_low, linear_low], axis=1), jnp.concatenate([gelu_w, lin_w], axis=1), 1, 1
    ).astype(BF)
    dn_a, dn_b = settle(own_dn, got_dn, 1)
    gu_a, gu_b = settle(own_gu, got_gu, 0)
    first_part, dn_a, dn_b = lax.optimization_barrier((first_part, dn_a, dn_b))
    packed = jnp.concatenate([recur_wg, input_wg, pad_last(sums.T, 128)], axis=1)
    packed = lax.dynamic_slice_in_dim(packed, own_off, own_ch, axis=0)
    input_grad, gain_one_rows, packed, output, grad_three = last_backward_call(
        n_hi, n_lo, n_cx, first_part, out_part, (grad_gl, grad_proj), packed, inputs, hidden_grad, gain_first[None], hidden
    )
    routes = [(d * n_ctx + c, c * n_dp + d) for d in range(n_dp) for c in range(n_ctx)]
    packed = lax.ppermute(packed, EVERY, routes)
    grad_gl = grad_three[:, : 2 * own_ch]
    grad_proj = grad_three[:, 2 * own_ch :]
    grad_gate = in_order(lo, gu_a[:, :ff_own], gu_b[:, :ff_own], 1).astype(F32)
    grad_up = in_order(
        lo, gu_a[:, ff_pad : ff_pad + ff_own], gu_b[:, ff_pad : ff_pad + ff_own], 1
    ).astype(F32)
    grad_dn = in_order(lo, dn_a[:ff_own], dn_b[:ff_own], 0).astype(F32)

    grad_recur_w = packed[:, :bw]
    grad_input_w = packed[:, bw : 2 * bw]
    rest = packed[:, 2 * bw : 2 * bw + 8].T
    gains = jnp.stack([jnp.sum(gain_one_rows, axis=0), jnp.sum(gain_two_rows, axis=0)])
    gains = jnp.sum(exchange(gains.reshape(2, n_dev, piece).transpose(1, 0, 2), EVERY), axis=0)

    return (
        output,
        input_grad,
        gains[0],
        grad_gl[:, :own_ch],
        grad_gl[:, own_ch:],
        rest[:CONV],
        rest[4],
        grad_recur_w,
        rest[5],
        grad_input_w,
        rest[6],
        rest[7],
        grad_proj,
        gains[1],
        grad_gate,
        grad_up,
        grad_dn,
    )


def solution(mesh):
    n_dp = mesh.shape["dp"]
    n_ctx = mesh.shape["context"]
    inner = Mesh(mesh.devices.reshape(2, n_dp // 2, n_ctx // 2, 2), EVERY)
    rows = P(EVERY, None)
    vec = P(EVERY)
    return jax.shard_map(
        per_device,
        mesh=inner,
        in_specs=(
            rows, P(DP, None), vec, rows, rows, P(None, EVERY), vec, rows, vec, rows, vec, vec, rows, vec,
            rows, rows, rows, rows,
        ),
        out_specs=(
            rows, rows, vec, P(DP, CTX), P(DP, CTX), P(None, EVERY), vec, rows, vec, rows, vec, vec,
            P(DP, CTX), vec, P(DP, CTX), P(DP, CTX), P(CTX, DP),
        ),
        check_vma=False,
    )
```

```python
import functools

import jax
import jax.numpy as jnp
from jax import lax
from jax.experimental import pallas as pl
from jax.experimental.pallas import tpu as pltpu
from jax.sharding import Mesh
from jax.sharding import PartitionSpec as P

HEADS = 10
CONV = 4
CHUNK = 256
BF = jnp.bfloat16
F32 = jnp.float32
DP = ("hi", "lo")
CTX = ("cxy", "core")
CUBE = ("lo", "cxy", "core")
EVERY = ("hi", "lo", "cxy", "core")
SWAP = [(0, 1), (1, 0)]


def dot(a, b, ca, cb):
    return lax.dot_general(a, b, (((ca,), (cb,)), ((), ())), preferred_element_type=F32)


def gelu_parts(x):
    c0 = 0.7978845608028654
    c1 = 0.044715
    x2 = x * x
    th = jnp.tanh(c0 * x * (1.0 + c1 * x2))
    half = 0.5 * (1.0 + th)
    slope = half + 0.5 * x * (1.0 - th * th) * c0 * (1.0 + 3.0 * c1 * x2)
    return x * half, slope


def minus_expm1(x):
    series = 1.0 + x * (1.0 / 8.0)
    for n in range(7, 1, -1):
        series = 1.0 + x * (1.0 / n) * series
    return jnp.where(x > -0.5, -x * series, 1.0 - jnp.exp(x))


def forward_kernel(
    lin_ref, gpre_ref, meta_ref, vec_ref, rw_ref, iw_ref,
    mixed_ref, prev_ref, conv_ref, rec_ref, inp_ref,
    xbuf, dec_s, drv_s, st_s, carry,
):
    rows = lin_ref.shape[0]
    first = pl.program_id(1) == 0

    @pl.when(first)
    def _():
        xbuf[0:8, :] = jnp.zeros((8, xbuf.shape[1]), F32)
        carry[...] = jnp.zeros_like(carry)

    x = lin_ref[...].astype(F32)
    xbuf[8 : 8 + rows, :] = x
    conv = vec_ref[4:5, :] + vec_ref[0:1, :] * x
    for k in range(1, CONV):
        conv = conv + vec_ref[k : k + 1, :] * (xbuf[8 - k : 8 - k + rows, :] * meta_ref[:, k : k + 1])
    xbuf[0:8, :] = x[rows - 8 : rows, :]
    low = conv.astype(BF)
    rec = jax.nn.sigmoid(jnp.dot(low, rw_ref[...], preferred_element_type=F32) + vec_ref[5:6, :])
    inp = jax.nn.sigmoid(jnp.dot(low, iw_ref[...], preferred_element_type=F32) + vec_ref[6:7, :])
    reset = meta_ref[:, 0:1] > 0.5
    log_decay = vec_ref[7:8, :] * rec
    scale = jnp.where(reset, 1.0, jnp.sqrt(minus_expm1(2.0 * log_decay)))
    dec_s[...] = jnp.where(reset, 0.0, jnp.exp(log_decay))
    drv_s[...] = scale * inp * conv
    conv_ref[...] = conv
    rec_ref[...] = rec
    inp_ref[...] = inp
    width = carry.shape[1]
    row = lax.broadcasted_iota(jnp.int32, (8, width), 0)

    def step(i, held):
        at = pl.multiple_of(i * 8, 8)
        a = dec_s[pl.ds(at, 8), :]
        b = drv_s[pl.ds(at, 8), :]
        for s in (1, 2, 4):
            keep = row >= s
            b = a * jnp.where(keep, pltpu.roll(b, s, 0), 0.0) + b
            a = a * jnp.where(keep, pltpu.roll(a, s, 0), 1.0)
        h = a * held + b
        st_s[pl.ds(at, 8), :] = h
        prev_ref[pl.ds(at, 8), :] = jnp.where(row == 0, held, pltpu.roll(h, 1, 0))
        return jnp.broadcast_to(h[7:8, :], (8, width))

    carry[...] = lax.fori_loop(0, rows // 8, step, carry[...], unroll=4)
    gel, _ = gelu_parts(gpre_ref[...])
    mixed_ref[...] = (gel * st_s[...] * vec_ref[8:9, :]).astype(BF)


def backward_kernel(
    mg_ref, gpre_ref, conv_ref, rec_ref, inp_ref, prev_ref, lin_ref, meta_ref, vec_ref, rw_ref, iw_ref,
    glow_ref, llow_ref, rwg_ref, iwg_ref, sum_ref,
    dec_s, sg_s, lam_s, gbuf, carry,
):
    rows = lin_ref.shape[0]
    first = pl.program_id(1) == 0

    @pl.when(first)
    def _():
        carry[...] = jnp.zeros_like(carry)
        for k in range(CONV - 1):
            gbuf[k, rows : rows + 8, :] = jnp.zeros((8, gbuf.shape[2]), F32)
        rwg_ref[...] = jnp.zeros_like(rwg_ref)
        iwg_ref[...] = jnp.zeros_like(iwg_ref)
        sum_ref[...] = jnp.zeros_like(sum_ref)

    mg = mg_ref[...]
    conv = conv_ref[...]
    rec = rec_ref[...]
    inp = inp_ref[...]
    prev = prev_ref[...]
    own = vec_ref[8:9, :]
    gel, slope = gelu_parts(gpre_ref[...])
    reset = meta_ref[:, 0:1] > 0.5
    log_decay = vec_ref[7:8, :] * rec
    scale = jnp.where(reset, 1.0, jnp.sqrt(minus_expm1(2.0 * log_decay)))
    dec = jnp.where(reset, 0.0, jnp.exp(log_decay))
    gated = scale * inp
    states = dec * prev + gated * conv
    glow_ref[...] = (mg * states * slope * own).astype(BF)
    dec_s[...] = dec
    sg_s[...] = mg * gel
    width = carry.shape[1]
    row = lax.broadcasted_iota(jnp.int32, (8, width), 0)
    blocks = rows // 8

    def step(i, held):
        at = pl.multiple_of((blocks - 1 - i) * 8, 8)
        a = dec_s[pl.ds(at, 8), :]
        g = sg_s[pl.ds(at, 8), :]
        b = a * g
        for s in (1, 2, 4):
            keep = row < 8 - s
            b = a * jnp.where(keep, pltpu.roll(b, 8 - s, 0), 0.0) + b
            a = a * jnp.where(keep, pltpu.roll(a, 8 - s, 0), 1.0)
        m = a * held + b
        lam_s[pl.ds(at, 8), :] = g + jnp.where(row == 7, held, pltpu.roll(m, 7, 0))
        return jnp.broadcast_to(m[0:1, :], (8, width))

    carry[...] = lax.fori_loop(0, blocks, step, carry[...], unroll=4)
    lam = lam_s[...]
    conv_gate = lam * gated
    dinp = lam * scale * conv
    dscale = lam * inp * conv
    dlog = jnp.where(reset, 0.0, (lam * prev - dscale * dec / scale) * dec)
    recur_grad = vec_ref[7:8, :] * dlog * rec * (1.0 - rec)
    input_grad = dinp * inp * (1.0 - inp)
    rlow = recur_grad.astype(BF)
    ilow = input_grad.astype(BF)
    low = conv.astype(BF)
    rwg_ref[...] += dot(low, rlow, 0, 0)
    iwg_ref[...] += dot(low, ilow, 0, 0)
    conv_grad = conv_gate + dot(rlow, rw_ref[...], 1, 1) + dot(ilow, iw_ref[...], 1, 1)
    lin = lin_ref[...].astype(F32)
    linear_grad = vec_ref[0:1, :] * conv_grad

    def add(at, value):
        sum_ref[at : at + 1, :] += jnp.sum(value, axis=0, keepdims=True)

    add(0, conv_grad * lin)
    for k in range(1, CONV):
        masked = conv_grad * meta_ref[:, k : k + 1]
        gbuf[k - 1, 0:rows, :] = masked
        moved = gbuf[k - 1, k : k + rows, :]
        gbuf[k - 1, rows : rows + 8, :] = masked[0:8, :]
        linear_grad = linear_grad + vec_ref[k : k + 1, :] * moved
        add(k, moved * lin)
    llow_ref[...] = (linear_grad * own).astype(BF)
    add(4, conv_grad)
    add(5, recur_grad)
    add(6, input_grad)
    add(7, vec_ref[9:10, :] * rec * dlog)


def forward_call(lin, gpre, meta, vecs, rw, iw):
    tokens, win = lin.shape
    bw = rw.shape[1]
    rows = min(CHUNK, tokens)
    grid = (win // bw, tokens // rows)
    tok = pl.BlockSpec((rows, bw), lambda h, j: (j, h))
    mspec = pl.BlockSpec((rows, meta.shape[1]), lambda h, j: (j, 0))
    vspec = pl.BlockSpec((vecs.shape[0], bw), lambda h, j: (0, h))
    wspec = pl.BlockSpec((bw, bw), lambda h, j: (h, 0))
    full = jax.ShapeDtypeStruct((tokens, win), F32)
    return pl.pallas_call(
        forward_kernel,
        grid=grid,
        in_specs=[tok, tok, mspec, vspec, wspec, wspec],
        out_specs=[tok] * 5,
        out_shape=[jax.ShapeDtypeStruct((tokens, win), BF), full, full, full, full],
        scratch_shapes=[
            pltpu.VMEM((rows + 8, bw), F32),
            pltpu.VMEM((rows, bw), F32),
            pltpu.VMEM((rows, bw), F32),
            pltpu.VMEM((rows, bw), F32),
            pltpu.VMEM((8, bw), F32),
        ],
        compiler_params=pltpu.CompilerParams(vmem_limit_bytes=40 << 20),
        cost_estimate=pl.CostEstimate(
            flops=tokens * win * (4 * bw + 100), bytes_accessed=tokens * win * 24, transcendentals=tokens * win * 6
        ),
        name="recur_forward",
    )(lin, gpre, meta, vecs, rw, iw)


def backward_call(mg, gpre, conv, rec, inp, prev, lin, meta, vecs, rw, iw):
    tokens, win = lin.shape
    bw = rw.shape[1]
    rows = min(CHUNK, tokens)
    steps = tokens // rows
    grid = (win // bw, steps)
    tok = pl.BlockSpec((rows, bw), lambda h, j: (steps - 1 - j, h))
    mspec = pl.BlockSpec((rows, meta.shape[1]), lambda h, j: (steps - 1 - j, 0))
    vspec = pl.BlockSpec((vecs.shape[0], bw), lambda h, j: (0, h))
    wspec = pl.BlockSpec((bw, bw), lambda h, j: (h, 0))
    sspec = pl.BlockSpec((8, bw), lambda h, j: (0, h))
    lows = jax.ShapeDtypeStruct((tokens, win), BF)
    wgrad = jax.ShapeDtypeStruct((win, bw), F32)
    return pl.pallas_call(
        backward_kernel,
        grid=grid,
        in_specs=[tok] * 7 + [mspec, vspec, wspec, wspec],
        out_specs=[tok, tok, wspec, wspec, sspec],
        out_shape=[lows, lows, wgrad, wgrad, jax.ShapeDtypeStruct((8, win), F32)],
        scratch_shapes=[
            pltpu.VMEM((rows, bw), F32),
            pltpu.VMEM((rows, bw), F32),
            pltpu.VMEM((rows, bw), F32),
            pltpu.VMEM((CONV - 1, rows + 8, bw), F32),
            pltpu.VMEM((8, bw), F32),
        ],
        compiler_params=pltpu.CompilerParams(vmem_limit_bytes=40 << 20),
        cost_estimate=pl.CostEstimate(
            flops=tokens * win, bytes_accessed=tokens * win, transcendentals=0
        ),
        name="recur_backward",
    )(mg, gpre, conv, rec, inp, prev, lin, meta, vecs, rw, iw)


def exchange(value, axes):
    return lax.all_to_all(value, axes, split_axis=0, concat_axis=0, tiled=True)


def in_order(flag, mine, other, axis):
    return jnp.where(
        flag == 0, jnp.concatenate([mine, other], axis=axis), jnp.concatenate([other, mine], axis=axis)
    )


def send(src, dst, out_sem, in_sem, target):
    return pltpu.make_async_remote_copy(
        src_ref=src, dst_ref=dst, send_sem=out_sem, recv_sem=in_sem,
        device_id=target, device_id_type=pl.DeviceIdType.MESH,
    )


def across():
    return {"hi": 1 - lax.axis_index("hi")}


def sibling():
    return {"core": 1 - lax.axis_index("core")}


def meet(targets):
    barrier = pltpu.get_barrier_semaphore()
    for target in targets:
        pl.semaphore_signal(barrier, inc=1, device_id=target, device_id_type=pl.DeviceIdType.MESH)
    pl.semaphore_wait(barrier, len(targets))


def subsets(bits):
    out = [()]
    for b in bits:
        out += [m + (b,) for m in out]
    return out


def lane_slices(width, parts):
    tiles = width // 128
    cuts = [tiles * i // parts * 128 for i in range(parts + 1)]
    return [pl.ds(a, b - a) for a, b in zip(cuts[:-1], cuts[1:])]


class Group:
    def __init__(self, n_lo, n_cx, cube):
        self.n_cx = n_cx
        self.near = list(range(n_cx.bit_length() - 1))
        self.far = len(self.near)
        self.cube = cube and n_lo == 2
        self.bits = self.near + ([self.far] if self.cube else [])
        self.count = n_cx * (2 if self.cube else 1)
        self.lo = lax.axis_index("lo")
        self.cx = lax.axis_index("cxy")
        self.core = lax.axis_index("core")
        self.place = self.lo * n_cx + self.cx if self.cube else self.cx

    def delta(self, bit):
        stride = 1 << bit
        return stride * (1 - 2 * lax.rem(self.place // stride, 2))

    def at(self, mask):
        spot = self.place
        for bit in mask:
            spot = spot + self.delta(bit)
        return spot

    def partner(self, bit):
        if bit == self.far:
            return {"lo": 1 - self.lo}
        return {"cxy": self.cx + self.delta(bit)}

    def partners(self):
        return [self.partner(bit) for bit in self.bits]

    def orders(self, light):
        if light is None or not self.cube:
            return [self.bits[i:] + self.bits[:i] for i in range(len(self.bits))]
        near = [self.near[i:] + self.near[:i] for i in range(len(self.near))]
        return [[self.far] + o if light == "first" else o + [self.far] for o in near]


class Spread:
    def __init__(self, group, src, out, sems, light=None):
        self.group, self.src, self.out = group, src, out
        self.keep, self.out_sems, self.in_sems, self.pass_sems, self.mate_sems = sems
        self.orders = group.orders(light)
        self.lanes = lane_slices(src.shape[-1], len(self.orders))
        self.moves = []
        index = 0
        for s in range(len(group.bits)):
            row = []
            for order, lanes in zip(self.orders, self.lanes):
                for mask in subsets(order[:s]):
                    row.append((index, lanes, mask, order[s]))
                    index += 1
            self.moves.append(row)

    @staticmethod
    def sems(group_bits, parts):
        moves = parts * ((1 << group_bits) - 1)
        return [
            pltpu.SemaphoreType.DMA(()), pltpu.SemaphoreType.DMA((moves,)), pltpu.SemaphoreType.DMA((moves,)),
            pltpu.SemaphoreType.DMA((moves + 1,)), pltpu.SemaphoreType.DMA((moves + 1,)),
        ]

    def block(self, mask, core):
        return self.group.at(mask) * 2 + core

    def copy(self, move):
        index, lanes, mask, bit = move
        dst = self.out.at[self.block(mask, self.group.core), :, lanes]
        src = dst if mask else self.src.at[:, lanes]
        return send(src, dst, self.out_sems.at[index], self.in_sems.at[index], self.group.partner(bit))

    def relay(self, move, core):
        index, lanes, mask, bit = move
        ref = self.out.at[self.block(mask + (bit,), core), :, lanes]
        return send(ref, ref, self.pass_sems.at[index + 1], self.mate_sems.at[index + 1], sibling())

    def own(self):
        mine = self.out.at[self.block((), self.group.core)]
        local = pltpu.make_async_copy(self.src, mine, self.keep)
        return local, send(self.src, mine, self.pass_sems.at[0], self.mate_sems.at[0], sibling())

    def begin(self):
        self.start(0)
        for copy in self.own():
            copy.start()

    def start(self, s):
        for move in self.moves[s]:
            self.copy(move).start()

    def finish(self, s):
        for move in self.moves[s]:
            index, lanes, mask, bit = move
            came = self.out.at[self.block(mask + (bit,), self.group.core), :, lanes]
            send(came, came, self.out_sems.at[index], self.in_sems.at[index], self.group.partner(bit)).wait_recv()

    def pass_on(self, s):
        for move in self.moves[s]:
            self.relay(move, self.group.core).start()

    def step(self, s):
        self.finish(s)
        if s + 1 < len(self.moves):
            self.start(s + 1)
        self.pass_on(s)

    def end(self):
        local, mate = self.own()
        local.wait()
        mate.wait_send()
        other = self.out.at[self.block((), 1 - self.group.core)]
        send(other, other, self.pass_sems.at[0], self.mate_sems.at[0], sibling()).wait_recv()
        for row in self.moves:
            for move in row:
                self.copy(move).wait_send()
                self.relay(move, self.group.core).wait_send()
                self.relay(move, 1 - self.group.core).wait_recv()


class Fold:
    def __init__(self, group, part, mate_buf, scratch, light=None):
        self.group, self.part, self.mate_buf = group, part, mate_buf
        (self.mine, self.far, self.stage, self.total,
         self.load_sems, self.pass_sems, self.mate_sems, self.out_sems, self.in_sems, self.stage_sems) = scratch
        self.orders = group.orders(light)
        self.lanes = lane_slices(part.shape[-1], len(self.orders))
        self.rows = self.total.shape[0]
        self.moves = []
        index = slot0 = 0
        levels = len(group.bits)
        for s in range(levels):
            row = []
            for order, lanes in zip(self.orders, self.lanes):
                for n, mask in enumerate(subsets(order[s + 1 :])):
                    row.append((index, lanes, mask, order[s], slot0 + n))
                    index += 1
            self.moves.append(row)
            slot0 += 1 << (levels - s - 1)
        masks = []
        for order in self.orders:
            masks += [m for m in subsets(group.bits) if order[0] in m and m not in masks]
        masks += [m for m in subsets(group.bits) if m and m not in masks] + [()]
        self.masks = masks

    @staticmethod
    def scratch(bits, parts, tok, width):
        count = 1 << bits
        moves = parts * (count - 1)
        dma = lambda n: pltpu.SemaphoreType.DMA((n,))
        return [
            pltpu.VMEM((count, tok, width), BF), pltpu.VMEM((count - 1, tok, width), BF),
            pltpu.VMEM((2, tok, width), BF), pltpu.VMEM((tok, width), F32),
            dma(count), dma(count), dma(count), dma(moves), dma(moves), dma(2),
        ]

    def mate(self, n):
        spot = self.group.at(self.masks[n])
        return send(
            self.part.at[spot, 1 - self.group.core], self.mate_buf.at[spot],
            self.pass_sems.at[n], self.mate_sems.at[n], sibling(),
        )

    def load(self, n):
        spot = self.group.at(self.masks[n])
        return pltpu.make_async_copy(self.part.at[spot, self.group.core], self.mine.at[spot], self.load_sems.at[n])

    def fetch(self, n):
        return pltpu.make_async_copy(
            self.mate_buf.at[self.group.at(self.masks[n])], self.stage.at[n % 2], self.stage_sems.at[n % 2]
        )

    def begin(self):
        for n in range(len(self.masks)):
            self.mate(n).start()
            self.load(n).start()

    def pairs(self):
        started = [False] * len(self.orders)
        count = len(self.masks)
        self.mate(0).wait_recv()
        self.fetch(0).start()
        for n, mask in enumerate(self.masks):
            if n + 1 < count:
                self.mate(n + 1).wait_recv()
                self.fetch(n + 1).start()
            self.load(n).wait()
            self.fetch(n).wait()
            spot = self.group.at(mask)

            def add(at, spot=spot, mask=mask, n=n):
                value = self.mine[spot, at, :].astype(F32) + self.stage[n % 2, at, :].astype(F32)
                if mask:
                    self.mine[spot, at, :] = value.astype(BF)
                else:
                    self.total[at, :] = value

            each_rows(self.rows, add)
            for j, order in enumerate(self.orders):
                need = [m for m in self.masks if order[0] in m]
                if not started[j] and all(m in self.masks[: n + 1] for m in need):
                    started[j] = True
                    self.start(0, j)

    def copy(self, move):
        index, lanes, mask, bit, slot = move
        return send(
            self.mine.at[self.group.at(mask + (bit,)), :, lanes], self.far.at[slot, :, lanes],
            self.out_sems.at[index], self.in_sems.at[index], self.group.partner(bit),
        )

    def start(self, s, part=None):
        per = len(self.moves[s]) // len(self.orders)
        for n, move in enumerate(self.moves[s]):
            if part is None or n // per == part:
                self.copy(move).start()

    def take(self, s):
        per = len(self.moves[s]) // len(self.orders)
        for n, move in enumerate(self.moves[s]):
            self.copy(move).wait_recv()
            index, lanes, mask, bit, slot = move
            spot = self.group.at(mask)

            def add(at):
                value = self.far[slot, at, lanes].astype(F32)
                if mask:
                    self.mine[spot, at, lanes] = (self.mine[spot, at, lanes].astype(F32) + value).astype(BF)
                else:
                    self.total[at, lanes] += value

            each_rows(self.rows, add)
            if (n + 1) % per == 0 and s + 1 < len(self.moves):
                self.start(s + 1, n // per)

    def end(self):
        for n in range(len(self.masks)):
            self.mate(n).wait_send()
        for row in self.moves:
            for move in row:
                self.copy(move).wait_send()


def each_rows(rows, body):
    def run(r, held):
        body(pl.ds(pl.multiple_of(r * 16, 16), 16))
        return held

    lax.fori_loop(0, rows // 16, run, 0)


N_FOLD = 10
N_SPREAD = 5


def middle_forward(n_lo, n_cx, part, inputs, gain, hidden, second_all, mate_buf, *scratch):
    fold_s, rest = scratch[:N_FOLD], scratch[N_FOLD:]
    spread_s, (second,) = rest[:N_SPREAD], rest[N_SPREAD:]
    cube = Group(n_lo, n_cx, True)
    plane = Group(n_lo, n_cx, False)
    meet(cube.partners() + [sibling()])
    fold = Fold(plane, part, mate_buf, fold_s)
    fold.begin()
    fold.pairs()
    for s in range(len(plane.bits)):
        fold.take(s)

    def norm(at):
        h = inputs[at, :] + fold.total[at, :]
        hidden[at, :] = h
        r = lax.rsqrt(jnp.mean(h * h, axis=-1, keepdims=True) + 1e-06)
        second[at, :] = (h * r * gain[...]).astype(BF)

    each_rows(fold.rows, norm)
    rows = Spread(cube, second, second_all, spread_s)
    rows.begin()
    for s in range(len(cube.bits)):
        rows.step(s)
    fold.end()
    rows.end()


def norm_back(values, gain, grad, base, out, gain_grad, at):
    v = values[at, :]
    g = grad[at, :]
    r = lax.rsqrt(jnp.mean(v * v, axis=-1, keepdims=True) + 1e-06)
    q = g * gain[...]
    back = base[at, :] + r * q - r * r * r * v * jnp.mean(q * v, axis=-1, keepdims=True)
    out[at, :] = back
    term = g * v * r
    gain_grad[...] += term[0:8, :] + term[8:16, :]
    return back


def middle_backward(n_lo, n_cx, part, hidden, out_grad, gain, hidden_grad, gain_grad, branch_all, mate_buf, *scratch):
    fold_s, rest = scratch[:N_FOLD], scratch[N_FOLD:]
    spread_s, (branch,) = rest[:N_SPREAD], rest[N_SPREAD:]
    cube = Group(n_lo, n_cx, True)
    plane = Group(n_lo, n_cx, False)
    meet(cube.partners() + [sibling()])
    fold = Fold(cube, part, mate_buf, fold_s)
    fold.begin()
    fold.pairs()
    for s in range(len(cube.bits)):
        fold.take(s)
    gain_grad[...] = jnp.zeros_like(gain_grad)

    def norm(at):
        branch[at, :] = norm_back(hidden, gain, fold.total, out_grad, hidden_grad, gain_grad, at).astype(BF)

    each_rows(fold.rows, norm)
    rows = Spread(plane, branch, branch_all, spread_s)
    rows.begin()
    for s in range(len(plane.bits)):
        rows.step(s)
    fold.end()
    rows.end()


class Chain:
    def __init__(self, z, count, part, blocks, came, sems, along):
        self.z, self.count, self.part, self.blocks, self.came, self.along = z, count, part, blocks, came, along
        self.load_sems, self.out_sems, self.in_sems = sems

    @staticmethod
    def scratch(parts, count, rows, cols):
        hops = 2 * (count - 1)
        return [pltpu.VMEM((count, rows, cols), BF), pltpu.VMEM((hops, rows, cols), BF)] + dma_sems(
            parts * count, hops, hops
        )

    def loads(self, d):
        first = 0
        for i, part in enumerate(self.part):
            cols = part.shape[2]
            dst = self.blocks.at[d, :, pl.ds(first, cols)] if len(self.part) > 1 else self.blocks.at[d]
            yield pltpu.make_async_copy(part.at[d], dst, self.load_sems.at[len(self.part) * d + i])
            first += cols

    def begin(self):
        for d in range(self.count):
            for copy in self.loads(d):
                copy.start()

    def ready(self):
        for d in range(self.count):
            for copy in self.loads(d):
                copy.wait()

    def sides(self, k):
        last = self.count - 1
        z = self.z
        yield 0, 1, jnp.logical_and(z <= k, z < last), jnp.logical_and(z >= 1, z <= k + 1)
        yield 1, -1, jnp.logical_and(z >= last - k, z > 0), jnp.logical_and(z <= last - 1, z >= last - 1 - k)

    def copy(self, side, way, k):
        at = side * (self.count - 1) + k
        block = self.blocks.at[self.z + way * (self.count - 1 - k)]
        return send(block, self.came.at[at], self.out_sems.at[at], self.in_sems.at[at], self.along(self.z + way))

    def start(self, k):
        for side, way, sends, _ in self.sides(k):
            @pl.when(sends)
            def _():
                self.copy(side, way, k).start()

    def take(self, k, total):
        final = k == self.count - 2
        for side, way, _, comes in self.sides(k):
            at = side * (self.count - 1) + k

            @pl.when(comes)
            def _():
                land = self.came.at[at]
                send(land, land, self.out_sems.at[at], self.in_sems.at[at], self.along(self.z - way)).wait_recv()

                def add(rows):
                    value = self.came[at, rows, :].astype(F32)
                    if final:
                        total[rows, :] += value
                    else:
                        spot = self.z + way * (self.count - 2 - k)
                        self.blocks[spot, rows, :] = (self.blocks[spot, rows, :].astype(F32) + value).astype(BF)

                each_rows(total.shape[0], add)

    def own(self, total):
        def put(rows):
            total[rows, :] = self.blocks[self.z, rows, :].astype(F32)

        each_rows(total.shape[0], put)

    def end(self):
        for k in range(self.count - 1):
            for side, way, sends, _ in self.sides(k):
                @pl.when(sends)
                def _():
                    self.copy(side, way, k).wait_send()


N_CHAIN = 5


def everywhere(n_hi, n_lo, n_cx):
    n_ctx = 2 * n_cx
    n_cube = n_lo * n_ctx
    number = (lax.axis_index("hi") * n_lo + lax.axis_index("lo")) * n_ctx + lax.axis_index("cxy") * 2
    number = number + lax.axis_index("core")

    def device(i):
        return {
            "hi": i // n_cube, "lo": lax.rem(i, n_cube) // n_ctx, "cxy": lax.rem(i, n_ctx) // 2, "core": lax.rem(i, 2),
        }

    return number, device, n_hi * n_cube


def meet_all(number, device, n_dev):
    barrier = pltpu.get_barrier_semaphore()

    def greet(i, held):
        other = device(lax.rem(number + i, n_dev))
        pl.semaphore_signal(barrier, inc=1, device_id=other, device_id_type=pl.DeviceIdType.MESH)
        return held

    lax.fori_loop(1, n_dev, greet, 0)
    pl.semaphore_wait(barrier, n_dev - 1)


def ff_block(u, n_lo, n_cx):
    lo, ctx = u // (2 * n_cx), u % (2 * n_cx)
    return (ctx % 2) * (n_lo * n_cx) + lo * n_cx + ctx // 2


class Exchange:
    def __init__(self, number, device, n_dev, src, came, sems, split):
        self.number, self.device, self.n_dev, self.split = number, device, n_dev, split
        self.src, self.came, (self.out_sems, self.in_sems) = src, came, sems

    def copy(self, i):
        to = lax.rem(self.number + i, self.n_dev)
        src = self.src.at[to] if self.split else self.src
        return send(src, self.came.at[self.number], self.out_sems.at[i], self.in_sems.at[i], self.device(to))

    def start(self):
        def run(i, held):
            self.copy(i).start()
            return held

        lax.fori_loop(1, self.n_dev, run, 0)

    def recv(self):
        def run(i, held):
            source = lax.rem(self.number - i + self.n_dev, self.n_dev)
            land = self.came.at[source]
            send(land, land, self.out_sems.at[i], self.in_sems.at[i], self.device(source)).wait_recv()
            return held

        lax.fori_loop(1, self.n_dev, run, 0)

    def end(self):
        def run(i, held):
            self.copy(i).wait_send()
            return held

        lax.fori_loop(1, self.n_dev, run, 0)


N_CHAIN = 5


def last_backward(n_lo, n_cx, n_hi, with_out, n_sums, part, *refs):
    sums, packed, refs = refs[:n_sums], refs[n_sums], refs[n_sums + 1 :]
    if with_out:
        (out_part, inputs, hidden_grad, gain, hidden, input_grad, gain_rows, packed_sum, summed, mate_a, output, mate_b,
         *scratch) = refs
    else:
        inputs, hidden_grad, gain, hidden, input_grad, gain_rows, packed_sum, summed, mate_a, *scratch = refs
    fold_a, rest = scratch[:N_FOLD], scratch[N_FOLD:]
    chain_s, rest = rest[:N_CHAIN], rest[N_CHAIN:]
    (pack_came, p_own, p_out, p_in), fold_b = rest[:4], rest[4:]
    cube = Group(n_lo, n_cx, True)
    plane = Group(n_lo, n_cx, False)
    n_dp = n_hi * n_lo
    z = lax.axis_index("hi") * n_lo + lax.axis_index("lo")
    along = lambda d: {"hi": d // n_lo, "lo": lax.rem(d, n_lo)}
    meet([cube.partner(b) for b in cube.near] + [sibling()] + [along(lax.rem(z + i, n_dp)) for i in range(1, n_dp)])
    first = Fold(plane, part, mate_a, fold_a)
    chain = Chain(z, n_dp, sums, chain_s[0], chain_s[1], chain_s[2:], along)
    chain.begin()
    first.begin()
    if with_out:
        outs = Fold(cube, out_part, mate_b, fold_b, "last")
        outs.begin()
    others = [lax.rem(z + i, n_dp) for i in range(1, n_dp)]
    pushes = [
        send(packed.at[d], pack_came.at[i + 1], p_out.at[i], p_in.at[i], along(d)) for i, d in enumerate(others)
    ]
    own_pack = pltpu.make_async_copy(packed.at[z], pack_came.at[0], p_own)
    own_pack.start()
    for push in pushes:
        push.start()
    hops = n_dp - 1
    chain.ready()
    chain.start(0)
    chain.own(summed)
    first.pairs()
    if with_out:
        outs.pairs()
    first.take(0)
    for k in range(hops - 1):
        chain.take(k, summed)
        chain.start(k + 1)
        if k + 1 < len(plane.bits):
            first.take(k + 1)
        if with_out and k + 1 < len(cube.bits):
            outs.take(k)
    for s in range(hops, len(plane.bits)):
        first.take(s)
    gain_rows[...] = jnp.zeros_like(gain_rows)

    def norm(at):
        norm_back(inputs, gain, first.total, hidden_grad, input_grad, gain_rows, at)

    each_rows(first.rows, norm)
    if with_out:
        for s in range(min(hops - 1, len(cube.bits) - 1), len(cube.bits)):
            outs.take(s)

        def finish(at):
            output[at, :] = hidden[at, :] + outs.total[at, :]

        each_rows(outs.rows, finish)
    own_pack.wait()
    value = pack_came[0]
    for i, push in enumerate(pushes):
        push.wait_recv()
        value = value + pack_came[i + 1]
    packed_sum[...] = value
    chain.take(hops - 1, summed)
    for push in pushes:
        push.wait_send()
    first.end()
    if with_out:
        outs.end()
    chain.end()


def comm_call(kernel, name, number, raw, args, outs, scratch, micros):
    any_spec = pl.BlockSpec(memory_space=pl.ANY)
    vmem = pl.BlockSpec(memory_space=pltpu.VMEM)
    return pl.pallas_call(
        kernel,
        in_specs=[any_spec] * len(raw) + [vmem] * len(args),
        out_specs=[vmem if inside else any_spec for _, inside in outs],
        out_shape=[shape for shape, _ in outs],
        scratch_shapes=scratch,
        compiler_params=pltpu.CompilerParams(
            collective_id=number, has_side_effects=True, vmem_limit_bytes=56 << 20
        ),
        cost_estimate=pl.CostEstimate(flops=micros * 10**9, bytes_accessed=micros * 10**6, transcendentals=0),
        name=name,
    )(*raw, *args)


def dma_sems(*counts):
    return [pltpu.SemaphoreType.DMA((n,) if n else ()) for n in counts]


def middle_forward_call(n_lo, n_cx, part, inputs, gain):
    tok, width = inputs.shape
    near = n_cx.bit_length() - 1
    far = near + n_lo - 1
    rows = jax.ShapeDtypeStruct((tok, width), F32)
    sds = lambda *shape: jax.ShapeDtypeStruct(shape, BF)
    hidden, second_all, _ = comm_call(
        functools.partial(middle_forward, n_lo, n_cx), "sum_norm_gather_forward", 1,
        (part.reshape(n_cx, 2, tok, width),), (inputs, gain),
        [(rows, True), (sds(n_lo * n_cx * 2, tok, width), False), (sds(n_cx, tok, width), False)],
        Fold.scratch(near, near, tok, width) + Spread.sems(far, far) + [pltpu.VMEM((tok, width), BF)], 1,
    )
    return hidden, second_all.reshape(-1, width)


def middle_backward_call(n_lo, n_cx, part, hidden, out_grad, gain):
    tok, width = hidden.shape
    near = n_cx.bit_length() - 1
    far = near + n_lo - 1
    rows = jax.ShapeDtypeStruct((tok, width), F32)
    sds = lambda *shape: jax.ShapeDtypeStruct(shape, BF)
    hidden_grad, gain_grad, branch_all, _ = comm_call(
        functools.partial(middle_backward, n_lo, n_cx), "sum_norm_gather_backward", 2,
        (part.reshape(n_lo * n_cx, 2, tok, width),), (hidden, out_grad, gain),
        [(rows, True), (jax.ShapeDtypeStruct((8, width), F32), True), (sds(n_cx * 2, tok, width), False),
         (sds(n_lo * n_cx, tok, width), False)],
        Fold.scratch(far, far, tok, width) + Spread.sems(near, near) + [pltpu.VMEM((tok, width), BF)], 100,
    )
    return hidden_grad, gain_grad, branch_all.reshape(-1, width)


def last_backward_call(n_hi, n_lo, n_cx, part, out_part, sums, packed, inputs, hidden_grad, gain, hidden):
    tok, width = inputs.shape
    near = n_cx.bit_length() - 1
    far = near + n_lo - 1
    n_dp = n_hi * n_lo
    with_out = n_lo * n_cx <= 8
    rows = jax.ShapeDtypeStruct((tok, width), F32)
    sds = lambda *shape: jax.ShapeDtypeStruct(shape, BF)
    full = lambda *shape: jax.ShapeDtypeStruct(shape, F32)
    if any(p.shape[1] % 128 for p in sums):
        sums = [jnp.concatenate(sums, axis=1)]
    sums = [p.reshape(n_dp, -1, p.shape[1]) for p in sums]
    summed_shape = (*sums[0].shape[1:2], sum(p.shape[2] for p in sums))
    packed = packed.reshape(n_dp, -1, packed.shape[1])
    raw = (part.reshape(n_cx, 2, tok, width), *sums, packed)
    outs = [(rows, True), (full(8, width), True), (full(*packed.shape[1:]), True), (full(*summed_shape), True),
            (sds(n_cx, tok, width), False)]
    scratch = Fold.scratch(near, near, tok, width) + Chain.scratch(len(sums), n_dp, *summed_shape)
    scratch += [pltpu.VMEM(packed.shape, F32)] + dma_sems(0, n_dp - 1, n_dp - 1)
    if with_out:
        raw += (out_part.reshape(n_lo * n_cx, 2, tok, width),)
        outs += [(rows, True), (sds(n_lo * n_cx, tok, width), False)]
        scratch += Fold.scratch(far, near, tok, width)
    got = comm_call(
        functools.partial(last_backward, n_lo, n_cx, n_hi, with_out, len(sums)), "sum_norm_backward", 3,
        raw, (inputs, hidden_grad, gain, hidden), outs, scratch, 100,
    )
    input_grad, gain_rows, packed_sum, summed = got[:4]
    if with_out:
        output = got[5]
    else:
        output = hidden + lax.psum_scatter(out_part, CUBE, scatter_dimension=0, tiled=True).astype(F32)
    return input_grad, gain_rows, packed_sum, output, summed


class Line:
    def __init__(self, n_hi, n_lo):
        self.n_lo = n_lo
        self.count = n_hi * n_lo
        self.z = lax.axis_index("hi") * n_lo + lax.axis_index("lo")

    def device(self, z):
        return {"hi": z // self.n_lo, "lo": lax.rem(z, self.n_lo)}

    def run(self, part, sems, k, action):
        out_sems, in_sems, pass_sems, mate_sems = sems
        last = self.count - 1
        z = self.z
        for side, way in ((0, 1), (1, -1)):
            if way == 1:
                sends = jnp.logical_and(z >= k, z < last)
                comes = z >= k + 1
            else:
                sends = jnp.logical_and(z <= last - k, z > 0)
                comes = z <= last - 1 - k
            at = side * last + k
            if action in ("recv", "mate_recv"):
                @pl.when(comes)
                def _():
                    if action == "recv":
                        plane = part(z - way * (k + 1), False)
                        send(plane, plane, out_sems.at[at], in_sems.at[at], self.device(z - way)).wait_recv()
                        if pass_sems is not None:
                            send(plane, plane, pass_sems.at[at], mate_sems.at[at], sibling()).start()
                    else:
                        plane = part(z - way * (k + 1), False)
                        send(plane, plane, pass_sems.at[at], mate_sems.at[at], sibling()).wait_send()
                        plane = part(z - way * (k + 1), True)
                        send(plane, plane, pass_sems.at[at], mate_sems.at[at], sibling()).wait_recv()
            else:
                @pl.when(sends)
                def _():
                    plane = part(z - way * k, False)
                    copy = send(plane, plane, out_sems.at[at], in_sems.at[at], self.device(z + way))
                    if action == "start":
                        copy.start()
                    else:
                        copy.wait_send()


def clamp_head(head, top):
    return head - head // (top + 1) * (head - top)


def window_head(c, own_ch, bw, span):
    return clamp_head(own_ch * c // bw, HEADS - span)


def chip_head(chip, own_ch, bw, span):
    return clamp_head(window_head(2 * chip, own_ch, bw, span), HEADS - span - 1)


def window_shard(head, n_dev, n_ctx, span):
    return head * ((n_dev - n_ctx) // (HEADS - span))


def gather_start(sizes, gelu_w, lin_w, proj, rgate, igate, small, down, gate_w, up_w, inputs,
                 gl_out, gu_out, pg_z, pg_win, normed_all, down_other, small_all,
                 gu_send, own_pg, own_gl, own_rest, gl_s, gl_r, mate_s, mate_r, gu_s, gu_r, win_s, win_r,
                 zp_s, zp_r, zg_s, zg_r, zm_s, zm_r, dn_s, dn_r,
                 normed, small_came, sm_own, sm_s, sm_r, *spread_s):
    n_hi, n_lo, n_cx, n_core, own_ch, bw, span = sizes
    n_ctx = n_cx * n_core
    n_cube = n_lo * n_ctx
    n_dev = n_hi * n_cube
    hi = lax.axis_index("hi")
    lo = lax.axis_index("lo")
    cx = lax.axis_index("cxy")
    core = lax.axis_index("core")
    ctx = cx * n_core + core
    spot = lo * n_ctx + ctx
    number = hi * n_cube + spot
    line = Line(n_hi, n_lo)
    z = line.z
    wide = (span + 1) * bw
    width = proj.shape[1]
    in_plane = lambda c: {"cxy": c // n_core, "core": lax.rem(c, n_core)}
    in_cube = lambda u: {"lo": u // n_ctx, **in_plane(lax.rem(u, n_ctx))}

    _, device, _ = everywhere(n_hi, n_lo, n_cx)
    meet_all(number, device, n_dev)
    vectors = Exchange(number, device, n_dev, small, small_came, (sm_s, sm_r), False)
    vectors.start()
    own_small = pltpu.make_async_copy(small, small_came.at[number], sm_own)
    own_small.start()

    pg_parts = [(proj, 0, width), (rgate, width, bw), (igate, width + bw, bw)]
    pg_own = [
        pltpu.make_async_copy(ref, pg_z.at[z, :, pl.ds(a, n)], own_pg.at[i]) for i, (ref, a, n) in enumerate(pg_parts)
    ]
    for copy in pg_own:
        copy.start()

    def columns(ref, chip):
        at = pl.multiple_of(chip_head(chip, own_ch, bw, span) * bw, bw)
        return ref.at[:, pl.ds(at, wide)]

    mine = lambda i: gl_out.at[z, cx, core, :, pl.ds(i * wide, wide)]
    gl_own = [pltpu.make_async_copy(columns(ref, cx), mine(i), own_gl.at[i]) for i, ref in enumerate((gelu_w, lin_w))]
    gl_copies = []
    for s in range(1, n_cx):
        to = lax.rem(cx + s, n_cx)
        for i, ref in enumerate((gelu_w, lin_w)):
            gl_copies.append(
                send(columns(ref, to), mine(i), gl_s.at[2 * s + i], gl_r.at[2 * s + i], {"cxy": to})
            )
            gl_copies[-1].start()
    for copy in gl_own:
        copy.start()
    pg_part = lambda plane, other: pg_z.at[plane]
    gl_part = lambda plane, other: gl_out.at[plane, :, 1 - core if other else core]
    pg_sems, gl_sems = (zp_s, zp_r, None, None), (zg_s, zg_r, zm_s, zm_r)
    steps = line.count - 1
    for copy in pg_own:
        copy.wait()
    line.run(pg_part, pg_sems, 0, "start")
    own_small.wait()
    vectors.recv()
    piece = width // n_dev
    for d in range(n_dev):
        small_all[:, d * piece : (d + 1) * piece] = small_came[d, :, 0:piece]
    gain = small_all[0:1, :].astype(F32)

    def norm(at):
        x = inputs[at, :]
        r = lax.rsqrt(jnp.mean(x * x, axis=-1, keepdims=True) + 1e-06)
        normed[at, :] = (x * r * gain).astype(BF)

    each_rows(normed.shape[0], norm)
    rows = Spread(Group(n_lo, n_cx, False), normed, normed_all, spread_s)
    rows.begin()
    for copy in gl_own:
        copy.wait()
    for s in range(1, n_cx):
        for i in range(2):
            came = gl_out.at[z, lax.rem(cx - s + n_cx, n_cx), core, :, pl.ds(i * wide, wide)]
            send(came, came, gl_s.at[2 * s + i], gl_r.at[2 * s + i], {"cxy": lax.rem(cx + s, n_cx)}).wait_recv()
    line.run(gl_part, gl_sems, 0, "start")
    own_plane = gl_part(z, False)
    own_mate = send(own_plane, own_plane, mate_s, mate_r, sibling())
    own_mate.start()

    ff_own = gate_w.shape[1] // n_cube
    ff_pad = gu_send.shape[2] // 2
    shard_rows = gate_w.shape[0]
    for u in range(n_cube):
        first = ff_block(u, n_lo, n_cx) * ff_own
        for i, ref in enumerate((gate_w, up_w)):
            gu_send[u, :, i * ff_pad : i * ff_pad + ff_own] = ref[:, first : first + ff_own]
            if ff_pad > ff_own:
                gu_send[u, :, i * ff_pad + ff_own : (i + 1) * ff_pad] = jnp.zeros((shard_rows, ff_pad - ff_own), BF)

    for k in range(1, steps):
        line.run(pg_part, pg_sems, k - 1, "recv")
        line.run(pg_part, pg_sems, k, "start")
    for s in range(len(rows.moves)):
        rows.step(s)
    line.run(pg_part, pg_sems, steps - 1, "recv")

    def window(src, dst):
        first = window_shard(window_head(dst, own_ch, bw, span), n_dev, n_ctx, span)
        turn = lax.rem(src - first + n_dev, n_ctx)
        return (first + turn) // n_ctx, turn

    shard, turn = window(ctx, ctx)
    own_window = pltpu.make_async_copy(pg_z.at[shard], pg_win.at[turn], own_rest.at[0])
    own_window.start()
    win_copies = []
    for s in range(1, n_ctx):
        to = lax.rem(ctx + s, n_ctx)
        shard, turn = window(ctx, to)
        win_copies.append(send(pg_z.at[shard], pg_win.at[turn], win_s.at[s], win_r.at[s], in_plane(to)))
        win_copies[-1].start()
    line.run(gl_part, gl_sems, 0, "recv")
    if steps > 1:
        line.run(gl_part, gl_sems, 1, "start")
    own_gu = pltpu.make_async_copy(gu_send.at[spot], gu_out.at[spot], own_rest.at[1])
    own_gu.start()
    gu_copies = []
    for s in range(1, n_cube):
        to = lax.rem(spot + s, n_cube)
        gu_copies.append(send(gu_send.at[to], gu_out.at[spot], gu_s.at[s], gu_r.at[s], in_cube(to)))
        gu_copies[-1].start()
    down_copy = send(down, down_other, dn_s, dn_r, across())
    for k in range(2, steps):
        line.run(gl_part, gl_sems, k - 1, "recv")
        line.run(gl_part, gl_sems, k, "start")
    down_copy.start()
    line.run(gl_part, gl_sems, steps - 1, "recv")
    rows.end()
    for s in range(1, n_ctx):
        _, turn = window(lax.rem(ctx - s + n_ctx, n_ctx), ctx)
        came = pg_win.at[turn]
        send(came, came, win_s.at[s], win_r.at[s], in_plane(lax.rem(ctx + s, n_ctx))).wait_recv()
    for s in range(1, n_cube):
        came = gu_out.at[lax.rem(spot - s + n_cube, n_cube)]
        send(came, came, gu_s.at[s], gu_r.at[s], in_cube(lax.rem(spot + s, n_cube))).wait_recv()
    own_window.wait()
    own_gu.wait()
    for copy in gl_copies + win_copies + gu_copies:
        copy.wait_send()
    own_mate.wait_send()
    other_plane = gl_part(z, True)
    send(other_plane, other_plane, mate_s, mate_r, sibling()).wait_recv()
    for k in range(steps):
        line.run(pg_part, pg_sems, k, "sent")
        line.run(gl_part, gl_sems, k, "sent")
        line.run(gl_part, gl_sems, k, "mate_recv")
    down_copy.wait()
    vectors.end()


def gather_start_call(sizes, gelu_w, lin_w, proj, rgate, igate, small, down, gate_w, up_w, inputs, ff_pad):
    n_hi, n_lo, n_cx, n_core, own_ch, bw, span = sizes
    n_ctx = n_cx * n_core
    n_cube = n_lo * n_ctx
    n_dp = n_hi * n_lo
    shard, width = proj.shape
    near = n_cx.bit_length() - 1
    wide = (span + 1) * bw
    sds = lambda *shape: jax.ShapeDtypeStruct(shape, BF)
    any_spec = pl.BlockSpec(memory_space=pl.ANY)
    vmem = pl.BlockSpec(memory_space=pltpu.VMEM)
    pg_width = width + 2 * bw
    hops = 2 * (n_dp - 1)
    gl_out, gu_out, _, pg_win, normed_all, down_other, small_all = pl.pallas_call(
        functools.partial(gather_start, sizes),
        in_specs=[any_spec] * 7 + [vmem] * 3,
        out_specs=[any_spec] * 6 + [vmem],
        out_shape=[
            sds(n_dp, n_cx, n_core, shard, 2 * wide), sds(n_cube, shard, 2 * ff_pad), sds(n_dp, shard, pg_width),
            sds(n_ctx, shard, pg_width), sds(n_ctx, *inputs.shape), sds(*down.shape),
            sds(small.shape[0], width),
        ],
        scratch_shapes=[pltpu.VMEM((n_cube, shard, 2 * ff_pad), BF)]
        + dma_sems(3, 2, 2, 2 * n_cx, 2 * n_cx, 0, 0, n_cube, n_cube, n_ctx, n_ctx, hops, hops, hops, hops, hops, hops, 0, 0)
        + [pltpu.VMEM(inputs.shape, BF), pltpu.VMEM((n_dp * n_ctx, *small.shape), BF)]
        + dma_sems(0, n_dp * n_ctx, n_dp * n_ctx) + Spread.sems(near, near),
        compiler_params=pltpu.CompilerParams(collective_id=4, has_side_effects=True, vmem_limit_bytes=40 << 20),
        cost_estimate=pl.CostEstimate(flops=10**11, bytes_accessed=10**8, transcendentals=0),
        name="gather_start",
    )(gelu_w, lin_w, proj, rgate, igate, small, down, gate_w, up_w, inputs)
    return gl_out.reshape(width, 2 * wide), gu_out.reshape(-1, 2 * ff_pad), pg_win.reshape(-1, pg_width), normed_all.reshape(-1, width), down_other, small_all


def swap_first(value):
    return lax.ppermute(value, DP, [(0, 1), (3, 2)]), lax.ppermute(value, DP, [(1, 2), (2, 1)])


def swap_second(to_inner, crossed):
    return lax.ppermute(to_inner, DP, [(1, 2), (2, 1)]), lax.ppermute(crossed, DP, [(1, 0), (2, 3)])


def pad_last(value, width):
    extra = width - value.shape[-1]
    return value if extra == 0 else jnp.pad(value, [(0, 0)] * (value.ndim - 1) + [(0, extra)])


def per_device(
    inputs, segment_ids, first_gain, gelu_in_w, linear_in_w, conv_weight, conv_bias, recur_gate_w, recur_gate_b,
    input_gate_w, input_gate_b, decay_param, out_proj_w, second_gain, mlp_gate_w, mlp_up_w, mlp_down_w, out_grad,
):
    n_hi, n_lo, n_cx, n_core = (lax.axis_size(a) for a in EVERY)
    hi, lo, cx, core = (lax.axis_index(a) for a in EVERY)
    n_ctx = n_cx * n_core
    n_dp = n_hi * n_lo
    n_dev = n_dp * n_ctx
    ctx = cx * n_core + core
    tok, width = inputs.shape
    tokens = segment_ids.shape[1]
    chans = linear_in_w.shape[1]
    bw = recur_gate_w.shape[1]
    hidden_units = mlp_gate_w.shape[1]
    own_ch = chans // n_ctx
    span = max((own_ch * (c + 1) - 1) // bw - own_ch * c // bw + 1 for c in range(n_ctx))
    win = span * bw
    head0 = window_head(ctx, own_ch, bw, span)
    ch0 = head0 * bw
    own_off = own_ch * ctx - ch0
    ff_own = hidden_units // (n_lo * n_ctx)
    ff_pad = -(-ff_own // 128) * 128

    piece = width // n_dev
    small = jnp.concatenate(
        [v[None] for v in (first_gain, second_gain)]
        + [conv_weight]
        + [v[None] for v in (conv_bias, recur_gate_b, input_gate_b, decay_param)],
        axis=0,
    )
    small = jnp.pad(small, ((0, 16 - small.shape[0]), (0, 128 - piece)))

    sizes = (n_hi, n_lo, n_cx, n_core, own_ch, bw, span)
    gl_w, gu_mine, pg_win, normed_all, down_other, small_all = gather_start_call(
        sizes, gelu_in_w, linear_in_w, out_proj_w, recur_gate_w, input_gate_w, small, mlp_down_w,
        mlp_gate_w, mlp_up_w, inputs, ff_pad,
    )
    small_all = small_all.astype(F32)
    gain_first = small_all[0]
    gain_second = small_all[1]
    wide = win + bw
    chip_off = (head0 - chip_head(cx, own_ch, bw, span)) * bw
    gelu_w = lax.dynamic_slice_in_dim(gl_w[:, :wide], chip_off, win, axis=1)
    lin_w = lax.dynamic_slice_in_dim(gl_w[:, wide:], chip_off, win, axis=1)
    pg_win = lax.dynamic_slice_in_dim(pg_win, ch0 - window_shard(head0, n_dev, n_ctx, span) * piece, win)
    proj_w = pg_win[:, :width]
    recur_w = pg_win[:, width : width + bw]
    input_w = pg_win[:, width + bw :]

    gu_other = lax.ppermute(gu_mine, "hi", SWAP)
    n_cube = n_lo * n_ctx
    keeps = hi == core
    down_keep = jnp.where(keeps, mlp_down_w, down_other)
    down_came = lax.ppermute(jnp.where(keeps, down_other, mlp_down_w), "core", SWAP)
    down_w = in_order(core, down_keep, down_came, 0)
    down_w = jnp.pad(down_w, ((0, ff_pad - ff_own), (0, 0)))
    cot = lax.optimization_barrier((out_grad.astype(BF), down_other))[0]
    down_grad = lax.all_gather(cot, CUBE, axis=0, tiled=True)

    ids = segment_ids[0]
    metas = [jnp.concatenate([jnp.ones((1,), F32), (ids[1:] != ids[:-1]).astype(F32)])]
    for k in range(1, CONV):
        metas.append(jnp.concatenate([jnp.zeros((k,), F32), (ids[k:] == ids[:-k]).astype(F32)]))
    meta = jnp.stack(metas, axis=1)
    vec_win = lax.dynamic_slice_in_dim(small_all[2:10], ch0, win, axis=1)
    decay_win = vec_win[7:8]
    place_in = jnp.arange(win) - own_off
    own_mask = ((place_in >= 0) & (place_in < own_ch)).astype(F32)[None]
    vecs = jnp.concatenate(
        [
            vec_win[:7],
            -8.0 * jax.nn.softplus(decay_win),
            own_mask,
            -8.0 * jax.nn.sigmoid(decay_win),
            jnp.zeros((6, win), F32),
        ],
        axis=0,
    )
    gelu_pre = dot(normed_all, gelu_w, 1, 0)
    linear_out = dot(normed_all, lin_w, 1, 0).astype(BF)
    mixed, prev, conv_out, rec, inp = forward_call(linear_out, gelu_pre, meta, vecs, recur_w, input_w)
    proj_part = dot(mixed, proj_w, 1, 0).astype(BF)
    hidden, second_all = middle_forward_call(n_lo, n_cx, proj_part, inputs, gain_second[None])
    gu_w = in_order(hi, gu_mine, gu_other, 0)

    pre = dot(second_all, gu_w, 1, 0)
    gate_pre, up_pre = pre[:, :ff_pad], pre[:, ff_pad:]
    act_grad = dot(down_grad, down_w, 1, 1)
    gel, slope = gelu_parts(gate_pre)
    activation = (gel * up_pre).astype(BF)
    gu_low = jnp.concatenate([(act_grad * up_pre * slope).astype(BF), (act_grad * gel).astype(BF)], axis=1)
    second_part = dot(gu_low, gu_w, 1, 1).astype(BF)

    def half_of(partial, which, axis, parts):
        size = partial.shape[axis] // parts
        return lax.dynamic_slice_in_dim(partial, which * size, size, axis)

    gu_stage = swap_first(dot(half_of(second_all, 1 - hi, 1, n_hi), gu_low, 0, 0).astype(BF))
    dn_stage = swap_first(dot(activation, half_of(down_grad, 1 - hi, 1, n_hi), 0, 0).astype(BF))
    hidden_grad, gain_two_rows, branch_all = middle_backward_call(
        n_lo, n_cx, second_part, hidden, out_grad, gain_second[None]
    )

    branch_all, *stages = lax.optimization_barrier((branch_all,) + gu_stage + dn_stage)
    dn_stage = swap_second(*stages[2:])
    gu_stage = swap_second(*stages[:2])
    inner = hi != lo

    late_second, late_cot = lax.optimization_barrier((second_all, down_grad, branch_all))[:2]
    own_gu = dot(half_of(late_second, hi, 1, n_hi), gu_low, 0, 0).astype(BF)
    own_dn = dot(activation, half_of(late_cot, hi, 1, n_hi), 0, 0).astype(BF)

    turns = [
        [
            (u, ((u % n_ctx // 2 + s) % 2) * n_ctx + ff_block(u, n_lo, n_cx) // 2)
            for u in range(n_cube)
        ]
        for s in range(2)
    ]

    def both_halves(partial, got):
        return (partial.astype(F32) + got.astype(F32)).astype(BF)

    def settle(both, axis):
        odd = lax.rem(cx, 2)
        return tuple(lax.ppermute(half_of(both, lax.rem(odd + s, 2), axis, n_lo), CUBE, turns[s]) for s in range(2))

    out_part = dot(activation, lax.optimization_barrier((down_w, gain_two_rows))[0], 1, 0).astype(BF)

    own_mixed = lax.dynamic_slice_in_dim(mixed, own_off, own_ch, axis=1)
    grad_proj = dot(own_mixed, branch_all, 0, 0).astype(BF).reshape(own_ch, n_ctx, width // n_ctx)
    grad_proj = grad_proj.transpose(1, 0, 2)
    mixed_grad = dot(branch_all, proj_w, 1, 1)
    mixed_grad, own_gu, own_dn, out_part, grad_proj = lax.optimization_barrier(
        (mixed_grad, own_gu, own_dn, out_part, grad_proj)
    )
    grad_proj = exchange(grad_proj, CTX).reshape(chans, width // n_ctx)
    gelu_low, linear_low, recur_wg, input_wg, sums = backward_call(
        mixed_grad, gelu_pre, conv_out, rec, inp, prev, linear_out, meta, vecs, recur_w, input_w
    )
    gelu_low, linear_low, *stages = lax.optimization_barrier((gelu_low, linear_low, *dn_stage))
    got_dn = jnp.where(inner, *stages[:2])
    own_lows = jnp.concatenate(
        [
            lax.dynamic_slice_in_dim(gelu_low, own_off, own_ch, axis=1),
            lax.dynamic_slice_in_dim(linear_low, own_off, own_ch, axis=1),
        ],
        axis=1,
    )
    grad_gl = dot(normed_all, own_lows, 0, 0).astype(BF)
    first_part = dot(
        jnp.concatenate([gelu_low, linear_low], axis=1), jnp.concatenate([gelu_w, lin_w], axis=1), 1, 1
    ).astype(BF)
    first_part, grad_gl, *gu_stage = lax.optimization_barrier((first_part, grad_gl, *gu_stage))
    got_gu = jnp.where(inner, *gu_stage)
    dn_a, dn_b = settle(both_halves(own_dn, got_dn), 1)
    gu_sum = both_halves(own_gu, got_gu)
    first_part, dn_a, dn_b, gu_sum = lax.optimization_barrier((first_part, dn_a, dn_b, gu_sum))
    gu_a, gu_b = settle(gu_sum, 0)
    packed = jnp.concatenate([recur_wg, input_wg, pad_last(sums.T, 128)], axis=1)
    packed = lax.dynamic_slice_in_dim(packed, own_off, own_ch, axis=0)
    input_grad, gain_one_rows, packed, output, grad_three = last_backward_call(
        n_hi, n_lo, n_cx, first_part, out_part, (grad_gl, grad_proj), packed, inputs, hidden_grad, gain_first[None], hidden
    )
    gain_one_rows, gu_a, gu_b = lax.optimization_barrier((gain_one_rows, gu_a, gu_b))
    routes = [(d * n_ctx + c, c * n_dp + d) for d in range(n_dp) for c in range(n_ctx)]
    packed = lax.ppermute(packed, EVERY, routes)
    grad_gl = grad_three[:, : 2 * own_ch]
    grad_proj = grad_three[:, 2 * own_ch :]
    grad_gate = in_order(lo, gu_a[:, :ff_own], gu_b[:, :ff_own], 1).astype(F32)
    grad_up = in_order(
        lo, gu_a[:, ff_pad : ff_pad + ff_own], gu_b[:, ff_pad : ff_pad + ff_own], 1
    ).astype(F32)
    grad_dn = in_order(lo, dn_a[:ff_own], dn_b[:ff_own], 0).astype(F32)

    grad_recur_w = packed[:, :bw]
    grad_input_w = packed[:, bw : 2 * bw]
    rest = packed[:, 2 * bw : 2 * bw + 8].T
    gains = jnp.stack([jnp.sum(gain_one_rows, axis=0), jnp.sum(gain_two_rows, axis=0)])
    gains = jnp.sum(exchange(gains.reshape(2, n_dev, piece).transpose(1, 0, 2), EVERY), axis=0)

    return (
        output,
        input_grad,
        gains[0],
        grad_gl[:, :own_ch],
        grad_gl[:, own_ch:],
        rest[:CONV],
        rest[4],
        grad_recur_w,
        rest[5],
        grad_input_w,
        rest[6],
        rest[7],
        grad_proj,
        gains[1],
        grad_gate,
        grad_up,
        grad_dn,
    )


def solution(mesh):
    n_dp = mesh.shape["dp"]
    n_ctx = mesh.shape["context"]
    inner = Mesh(mesh.devices.reshape(2, n_dp // 2, n_ctx // 2, 2), EVERY)
    rows = P(EVERY, None)
    vec = P(EVERY)
    return jax.shard_map(
        per_device,
        mesh=inner,
        in_specs=(
            rows, P(DP, None), vec, rows, rows, P(None, EVERY), vec, rows, vec, rows, vec, vec, rows, vec,
            rows, rows, rows, rows,
        ),
        out_specs=(
            rows, rows, vec, P(DP, CTX), P(DP, CTX), P(None, EVERY), vec, rows, vec, rows, vec, vec,
            P(DP, CTX), vec, P(DP, CTX), P(DP, CTX), P(CTX, DP),
        ),
        check_vma=False,
    )
```

```python
import functools

import jax
import jax.numpy as jnp
from jax import lax
from jax.experimental import pallas as pl
from jax.experimental.pallas import tpu as pltpu
from jax.sharding import Mesh
from jax.sharding import PartitionSpec as P

HEADS = 10
CONV = 4
CHUNK = 256
BF = jnp.bfloat16
F32 = jnp.float32
DP = ("hi", "lo")
CTX = ("cxy", "core")
CUBE = ("lo", "cxy", "core")
EVERY = ("hi", "lo", "cxy", "core")
SWAP = [(0, 1), (1, 0)]


def dot(a, b, ca, cb):
    return lax.dot_general(a, b, (((ca,), (cb,)), ((), ())), preferred_element_type=F32)


def gelu_parts(x):
    c0 = 0.7978845608028654
    c1 = 0.044715
    x2 = x * x
    th = jnp.tanh(c0 * x * (1.0 + c1 * x2))
    half = 0.5 * (1.0 + th)
    slope = half + 0.5 * x * (1.0 - th * th) * c0 * (1.0 + 3.0 * c1 * x2)
    return x * half, slope


def minus_expm1(x):
    series = 1.0 + x * (1.0 / 8.0)
    for n in range(7, 1, -1):
        series = 1.0 + x * (1.0 / n) * series
    return jnp.where(x > -0.5, -x * series, 1.0 - jnp.exp(x))


def forward_kernel(
    lin_ref, gpre_ref, meta_ref, vec_ref, rw_ref, iw_ref,
    mixed_ref, prev_ref, conv_ref, rec_ref, inp_ref,
    xbuf, dec_s, drv_s, st_s, carry,
):
    rows = lin_ref.shape[0]
    first = pl.program_id(1) == 0

    @pl.when(first)
    def _():
        xbuf[0:8, :] = jnp.zeros((8, xbuf.shape[1]), F32)
        carry[...] = jnp.zeros_like(carry)

    x = lin_ref[...].astype(F32)
    xbuf[8 : 8 + rows, :] = x
    conv = vec_ref[4:5, :] + vec_ref[0:1, :] * x
    for k in range(1, CONV):
        conv = conv + vec_ref[k : k + 1, :] * (xbuf[8 - k : 8 - k + rows, :] * meta_ref[:, k : k + 1])
    xbuf[0:8, :] = x[rows - 8 : rows, :]
    low = conv.astype(BF)
    rec = jax.nn.sigmoid(jnp.dot(low, rw_ref[...], preferred_element_type=F32) + vec_ref[5:6, :])
    inp = jax.nn.sigmoid(jnp.dot(low, iw_ref[...], preferred_element_type=F32) + vec_ref[6:7, :])
    reset = meta_ref[:, 0:1] > 0.5
    log_decay = vec_ref[7:8, :] * rec
    scale = jnp.where(reset, 1.0, jnp.sqrt(minus_expm1(2.0 * log_decay)))
    dec_s[...] = jnp.where(reset, 0.0, jnp.exp(log_decay))
    drv_s[...] = scale * inp * conv
    conv_ref[...] = conv
    rec_ref[...] = rec
    inp_ref[...] = inp
    width = carry.shape[1]
    row = lax.broadcasted_iota(jnp.int32, (8, width), 0)

    def step(i, held):
        at = pl.multiple_of(i * 8, 8)
        a = dec_s[pl.ds(at, 8), :]
        b = drv_s[pl.ds(at, 8), :]
        for s in (1, 2, 4):
            keep = row >= s
            b = a * jnp.where(keep, pltpu.roll(b, s, 0), 0.0) + b
            a = a * jnp.where(keep, pltpu.roll(a, s, 0), 1.0)
        h = a * held + b
        st_s[pl.ds(at, 8), :] = h
        prev_ref[pl.ds(at, 8), :] = jnp.where(row == 0, held, pltpu.roll(h, 1, 0))
        return jnp.broadcast_to(h[7:8, :], (8, width))

    carry[...] = lax.fori_loop(0, rows // 8, step, carry[...], unroll=4)
    gel, _ = gelu_parts(gpre_ref[...])
    mixed_ref[...] = (gel * st_s[...] * vec_ref[8:9, :]).astype(BF)


def backward_kernel(
    mg_ref, gpre_ref, conv_ref, rec_ref, inp_ref, prev_ref, lin_ref, meta_ref, vec_ref, rw_ref, iw_ref,
    glow_ref, llow_ref, rwg_ref, iwg_ref, sum_ref,
    dec_s, sg_s, lam_s, gbuf, carry,
):
    rows = lin_ref.shape[0]
    first = pl.program_id(1) == 0

    @pl.when(first)
    def _():
        carry[...] = jnp.zeros_like(carry)
        for k in range(CONV - 1):
            gbuf[k, rows : rows + 8, :] = jnp.zeros((8, gbuf.shape[2]), F32)
        rwg_ref[...] = jnp.zeros_like(rwg_ref)
        iwg_ref[...] = jnp.zeros_like(iwg_ref)
        sum_ref[...] = jnp.zeros_like(sum_ref)

    mg = mg_ref[...]
    conv = conv_ref[...]
    rec = rec_ref[...]
    inp = inp_ref[...]
    prev = prev_ref[...]
    own = vec_ref[8:9, :]
    gel, slope = gelu_parts(gpre_ref[...])
    reset = meta_ref[:, 0:1] > 0.5
    log_decay = vec_ref[7:8, :] * rec
    scale = jnp.where(reset, 1.0, jnp.sqrt(minus_expm1(2.0 * log_decay)))
    dec = jnp.where(reset, 0.0, jnp.exp(log_decay))
    gated = scale * inp
    states = dec * prev + gated * conv
    glow_ref[...] = (mg * states * slope * own).astype(BF)
    dec_s[...] = dec
    sg_s[...] = mg * gel
    width = carry.shape[1]
    row = lax.broadcasted_iota(jnp.int32, (8, width), 0)
    blocks = rows // 8

    def step(i, held):
        at = pl.multiple_of((blocks - 1 - i) * 8, 8)
        a = dec_s[pl.ds(at, 8), :]
        g = sg_s[pl.ds(at, 8), :]
        b = a * g
        for s in (1, 2, 4):
            keep = row < 8 - s
            b = a * jnp.where(keep, pltpu.roll(b, 8 - s, 0), 0.0) + b
            a = a * jnp.where(keep, pltpu.roll(a, 8 - s, 0), 1.0)
        m = a * held + b
        lam_s[pl.ds(at, 8), :] = g + jnp.where(row == 7, held, pltpu.roll(m, 7, 0))
        return jnp.broadcast_to(m[0:1, :], (8, width))

    carry[...] = lax.fori_loop(0, blocks, step, carry[...], unroll=4)
    lam = lam_s[...]
    conv_gate = lam * gated
    dinp = lam * scale * conv
    dscale = lam * inp * conv
    dlog = jnp.where(reset, 0.0, (lam * prev - dscale * dec / scale) * dec)
    recur_grad = vec_ref[7:8, :] * dlog * rec * (1.0 - rec)
    input_grad = dinp * inp * (1.0 - inp)
    rlow = recur_grad.astype(BF)
    ilow = input_grad.astype(BF)
    low = conv.astype(BF)
    rwg_ref[...] += dot(low, rlow, 0, 0)
    iwg_ref[...] += dot(low, ilow, 0, 0)
    conv_grad = conv_gate + dot(rlow, rw_ref[...], 1, 1) + dot(ilow, iw_ref[...], 1, 1)
    lin = lin_ref[...].astype(F32)
    linear_grad = vec_ref[0:1, :] * conv_grad

    def add(at, value):
        sum_ref[at : at + 1, :] += jnp.sum(value, axis=0, keepdims=True)

    add(0, conv_grad * lin)
    for k in range(1, CONV):
        masked = conv_grad * meta_ref[:, k : k + 1]
        gbuf[k - 1, 0:rows, :] = masked
        moved = gbuf[k - 1, k : k + rows, :]
        gbuf[k - 1, rows : rows + 8, :] = masked[0:8, :]
        linear_grad = linear_grad + vec_ref[k : k + 1, :] * moved
        add(k, moved * lin)
    llow_ref[...] = (linear_grad * own).astype(BF)
    add(4, conv_grad)
    add(5, recur_grad)
    add(6, input_grad)
    add(7, vec_ref[9:10, :] * rec * dlog)


def forward_call(lin, gpre, meta, vecs, rw, iw):
    tokens, win = lin.shape
    bw = rw.shape[1]
    rows = min(CHUNK, tokens)
    grid = (win // bw, tokens // rows)
    tok = pl.BlockSpec((rows, bw), lambda h, j: (j, h))
    mspec = pl.BlockSpec((rows, meta.shape[1]), lambda h, j: (j, 0))
    vspec = pl.BlockSpec((vecs.shape[0], bw), lambda h, j: (0, h))
    wspec = pl.BlockSpec((bw, bw), lambda h, j: (h, 0))
    full = jax.ShapeDtypeStruct((tokens, win), F32)
    return pl.pallas_call(
        forward_kernel,
        grid=grid,
        in_specs=[tok, tok, mspec, vspec, wspec, wspec],
        out_specs=[tok] * 5,
        out_shape=[jax.ShapeDtypeStruct((tokens, win), BF), full, full, full, full],
        scratch_shapes=[
            pltpu.VMEM((rows + 8, bw), F32),
            pltpu.VMEM((rows, bw), F32),
            pltpu.VMEM((rows, bw), F32),
            pltpu.VMEM((rows, bw), F32),
            pltpu.VMEM((8, bw), F32),
        ],
        compiler_params=pltpu.CompilerParams(vmem_limit_bytes=40 << 20),
        cost_estimate=pl.CostEstimate(
            flops=tokens * win * (4 * bw + 100), bytes_accessed=tokens * win * 24, transcendentals=tokens * win * 6
        ),
        name="recur_forward",
    )(lin, gpre, meta, vecs, rw, iw)


def backward_call(mg, gpre, conv, rec, inp, prev, lin, meta, vecs, rw, iw):
    tokens, win = lin.shape
    bw = rw.shape[1]
    rows = min(CHUNK, tokens)
    steps = tokens // rows
    grid = (win // bw, steps)
    tok = pl.BlockSpec((rows, bw), lambda h, j: (steps - 1 - j, h))
    mspec = pl.BlockSpec((rows, meta.shape[1]), lambda h, j: (steps - 1 - j, 0))
    vspec = pl.BlockSpec((vecs.shape[0], bw), lambda h, j: (0, h))
    wspec = pl.BlockSpec((bw, bw), lambda h, j: (h, 0))
    sspec = pl.BlockSpec((8, bw), lambda h, j: (0, h))
    lows = jax.ShapeDtypeStruct((tokens, win), BF)
    wgrad = jax.ShapeDtypeStruct((win, bw), F32)
    return pl.pallas_call(
        backward_kernel,
        grid=grid,
        in_specs=[tok] * 7 + [mspec, vspec, wspec, wspec],
        out_specs=[tok, tok, wspec, wspec, sspec],
        out_shape=[lows, lows, wgrad, wgrad, jax.ShapeDtypeStruct((8, win), F32)],
        scratch_shapes=[
            pltpu.VMEM((rows, bw), F32),
            pltpu.VMEM((rows, bw), F32),
            pltpu.VMEM((rows, bw), F32),
            pltpu.VMEM((CONV - 1, rows + 8, bw), F32),
            pltpu.VMEM((8, bw), F32),
        ],
        compiler_params=pltpu.CompilerParams(vmem_limit_bytes=40 << 20),
        cost_estimate=pl.CostEstimate(
            flops=tokens * win, bytes_accessed=tokens * win, transcendentals=0
        ),
        name="recur_backward",
    )(mg, gpre, conv, rec, inp, prev, lin, meta, vecs, rw, iw)


def exchange(value, axes):
    return lax.all_to_all(value, axes, split_axis=0, concat_axis=0, tiled=True)


def in_order(flag, mine, other, axis):
    return jnp.where(
        flag == 0, jnp.concatenate([mine, other], axis=axis), jnp.concatenate([other, mine], axis=axis)
    )


def send(src, dst, out_sem, in_sem, target):
    return pltpu.make_async_remote_copy(
        src_ref=src, dst_ref=dst, send_sem=out_sem, recv_sem=in_sem,
        device_id=target, device_id_type=pl.DeviceIdType.MESH,
    )


def across():
    return {"hi": 1 - lax.axis_index("hi")}


def sibling():
    return {"core": 1 - lax.axis_index("core")}


def meet(targets):
    barrier = pltpu.get_barrier_semaphore()
    for target in targets:
        pl.semaphore_signal(barrier, inc=1, device_id=target, device_id_type=pl.DeviceIdType.MESH)
    pl.semaphore_wait(barrier, len(targets))


def subsets(bits):
    out = [()]
    for b in bits:
        out += [m + (b,) for m in out]
    return out


def lane_slices(width, parts):
    tiles = width // 128
    cuts = [tiles * i // parts * 128 for i in range(parts + 1)]
    return [pl.ds(a, b - a) for a, b in zip(cuts[:-1], cuts[1:])]


class Group:
    def __init__(self, n_lo, n_cx, cube):
        self.n_cx = n_cx
        self.near = list(range(n_cx.bit_length() - 1))
        self.far = len(self.near)
        self.cube = cube and n_lo == 2
        self.bits = self.near + ([self.far] if self.cube else [])
        self.count = n_cx * (2 if self.cube else 1)
        self.lo = lax.axis_index("lo")
        self.cx = lax.axis_index("cxy")
        self.core = lax.axis_index("core")
        self.place = self.lo * n_cx + self.cx if self.cube else self.cx

    def delta(self, bit):
        stride = 1 << bit
        return stride * (1 - 2 * lax.rem(self.place // stride, 2))

    def at(self, mask):
        spot = self.place
        for bit in mask:
            spot = spot + self.delta(bit)
        return spot

    def partner(self, bit):
        if bit == self.far:
            return {"lo": 1 - self.lo}
        return {"cxy": self.cx + self.delta(bit)}

    def partners(self):
        return [self.partner(bit) for bit in self.bits]

    def orders(self, light):
        if light is None or not self.cube:
            return [self.bits[i:] + self.bits[:i] for i in range(len(self.bits))]
        near = [self.near[i:] + self.near[:i] for i in range(len(self.near))]
        return [[self.far] + o if light == "first" else o + [self.far] for o in near]


class Spread:
    def __init__(self, group, src, out, sems, light=None):
        self.group, self.src, self.out = group, src, out
        self.keep, self.out_sems, self.in_sems, self.pass_sems, self.mate_sems = sems
        self.orders = group.orders(light)
        self.lanes = lane_slices(src.shape[-1], len(self.orders))
        self.moves = []
        index = 0
        for s in range(len(group.bits)):
            row = []
            for order, lanes in zip(self.orders, self.lanes):
                for mask in subsets(order[:s]):
                    row.append((index, lanes, mask, order[s]))
                    index += 1
            self.moves.append(row)

    @staticmethod
    def sems(group_bits, parts):
        moves = parts * ((1 << group_bits) - 1)
        return [
            pltpu.SemaphoreType.DMA(()), pltpu.SemaphoreType.DMA((moves,)), pltpu.SemaphoreType.DMA((moves,)),
            pltpu.SemaphoreType.DMA((moves + 1,)), pltpu.SemaphoreType.DMA((moves + 1,)),
        ]

    def block(self, mask, core):
        return self.group.at(mask) * 2 + core

    def copy(self, move):
        index, lanes, mask, bit = move
        dst = self.out.at[self.block(mask, self.group.core), :, lanes]
        src = dst if mask else self.src.at[:, lanes]
        return send(src, dst, self.out_sems.at[index], self.in_sems.at[index], self.group.partner(bit))

    def relay(self, move, core):
        index, lanes, mask, bit = move
        ref = self.out.at[self.block(mask + (bit,), core), :, lanes]
        return send(ref, ref, self.pass_sems.at[index + 1], self.mate_sems.at[index + 1], sibling())

    def own(self):
        mine = self.out.at[self.block((), self.group.core)]
        local = pltpu.make_async_copy(self.src, mine, self.keep)
        return local, send(self.src, mine, self.pass_sems.at[0], self.mate_sems.at[0], sibling())

    def begin(self):
        self.start(0)
        for copy in self.own():
            copy.start()

    def start(self, s):
        for move in self.moves[s]:
            self.copy(move).start()

    def finish(self, s):
        for move in self.moves[s]:
            index, lanes, mask, bit = move
            came = self.out.at[self.block(mask + (bit,), self.group.core), :, lanes]
            send(came, came, self.out_sems.at[index], self.in_sems.at[index], self.group.partner(bit)).wait_recv()

    def pass_on(self, s):
        for move in self.moves[s]:
            self.relay(move, self.group.core).start()

    def step(self, s):
        self.finish(s)
        if s + 1 < len(self.moves):
            self.start(s + 1)
        self.pass_on(s)

    def end(self):
        local, mate = self.own()
        local.wait()
        mate.wait_send()
        other = self.out.at[self.block((), 1 - self.group.core)]
        send(other, other, self.pass_sems.at[0], self.mate_sems.at[0], sibling()).wait_recv()
        for row in self.moves:
            for move in row:
                self.copy(move).wait_send()
                self.relay(move, self.group.core).wait_send()
                self.relay(move, 1 - self.group.core).wait_recv()


class Fold:
    def __init__(self, group, part, mate_buf, scratch, light=None):
        self.group, self.part, self.mate_buf = group, part, mate_buf
        (self.mine, self.far, self.stage, self.total,
         self.load_sems, self.pass_sems, self.mate_sems, self.out_sems, self.in_sems, self.stage_sems) = scratch
        self.orders = group.orders(light)
        self.lanes = lane_slices(part.shape[-1], len(self.orders))
        self.rows = self.total.shape[0]
        self.moves = []
        index = slot0 = 0
        levels = len(group.bits)
        for s in range(levels):
            row = []
            for order, lanes in zip(self.orders, self.lanes):
                for n, mask in enumerate(subsets(order[s + 1 :])):
                    row.append((index, lanes, mask, order[s], slot0 + n))
                    index += 1
            self.moves.append(row)
            slot0 += 1 << (levels - s - 1)
        masks = []
        for order in self.orders:
            masks += [m for m in subsets(group.bits) if order[0] in m and m not in masks]
        masks += [m for m in subsets(group.bits) if m and m not in masks] + [()]
        self.masks = masks

    @staticmethod
    def scratch(bits, parts, tok, width):
        count = 1 << bits
        moves = parts * (count - 1)
        dma = lambda n: pltpu.SemaphoreType.DMA((n,))
        return [
            pltpu.VMEM((count, tok, width), BF), pltpu.VMEM((count - 1, tok, width), BF),
            pltpu.VMEM((2, tok, width), BF), pltpu.VMEM((tok, width), F32),
            dma(count), dma(count), dma(count), dma(moves), dma(moves), dma(2),
        ]

    def mate(self, n):
        spot = self.group.at(self.masks[n])
        return send(
            self.part.at[spot, 1 - self.group.core], self.mate_buf.at[spot],
            self.pass_sems.at[n], self.mate_sems.at[n], sibling(),
        )

    def load(self, n):
        spot = self.group.at(self.masks[n])
        return pltpu.make_async_copy(self.part.at[spot, self.group.core], self.mine.at[spot], self.load_sems.at[n])

    def fetch(self, n):
        return pltpu.make_async_copy(
            self.mate_buf.at[self.group.at(self.masks[n])], self.stage.at[n % 2], self.stage_sems.at[n % 2]
        )

    def begin(self):
        for n in range(len(self.masks)):
            self.mate(n).start()
            self.load(n).start()

    def pairs(self):
        started = [False] * len(self.orders)
        count = len(self.masks)
        self.mate(0).wait_recv()
        self.fetch(0).start()
        for n, mask in enumerate(self.masks):
            if n + 1 < count:
                self.mate(n + 1).wait_recv()
                self.fetch(n + 1).start()
            self.load(n).wait()
            self.fetch(n).wait()
            spot = self.group.at(mask)

            def add(at, spot=spot, mask=mask, n=n):
                value = self.mine[spot, at, :].astype(F32) + self.stage[n % 2, at, :].astype(F32)
                if mask:
                    self.mine[spot, at, :] = value.astype(BF)
                else:
                    self.total[at, :] = value

            each_rows(self.rows, add)
            for j, order in enumerate(self.orders):
                need = [m for m in self.masks if order[0] in m]
                if not started[j] and all(m in self.masks[: n + 1] for m in need):
                    started[j] = True
                    self.start(0, j)

    def copy(self, move):
        index, lanes, mask, bit, slot = move
        return send(
            self.mine.at[self.group.at(mask + (bit,)), :, lanes], self.far.at[slot, :, lanes],
            self.out_sems.at[index], self.in_sems.at[index], self.group.partner(bit),
        )

    def start(self, s, part=None):
        per = len(self.moves[s]) // len(self.orders)
        for n, move in enumerate(self.moves[s]):
            if part is None or n // per == part:
                self.copy(move).start()

    def take(self, s):
        per = len(self.moves[s]) // len(self.orders)
        for n, move in enumerate(self.moves[s]):
            self.copy(move).wait_recv()
            index, lanes, mask, bit, slot = move
            spot = self.group.at(mask)

            def add(at):
                value = self.far[slot, at, lanes].astype(F32)
                if mask:
                    self.mine[spot, at, lanes] = (self.mine[spot, at, lanes].astype(F32) + value).astype(BF)
                else:
                    self.total[at, lanes] += value

            each_rows(self.rows, add)
            if (n + 1) % per == 0 and s + 1 < len(self.moves):
                self.start(s + 1, n // per)

    def end(self):
        for n in range(len(self.masks)):
            self.mate(n).wait_send()
        for row in self.moves:
            for move in row:
                self.copy(move).wait_send()


def each_rows(rows, body):
    def run(r, held):
        body(pl.ds(pl.multiple_of(r * 16, 16), 16))
        return held

    lax.fori_loop(0, rows // 16, run, 0)


N_FOLD = 10
N_SPREAD = 5


def middle_forward(n_lo, n_cx, part, inputs, gain, hidden, second_all, mate_buf, *scratch):
    fold_s, rest = scratch[:N_FOLD], scratch[N_FOLD:]
    spread_s, (second,) = rest[:N_SPREAD], rest[N_SPREAD:]
    cube = Group(n_lo, n_cx, True)
    plane = Group(n_lo, n_cx, False)
    meet(cube.partners() + [sibling()])
    fold = Fold(plane, part, mate_buf, fold_s)
    fold.begin()
    fold.pairs()
    for s in range(len(plane.bits)):
        fold.take(s)

    def norm(at):
        h = inputs[at, :] + fold.total[at, :]
        hidden[at, :] = h
        r = lax.rsqrt(jnp.mean(h * h, axis=-1, keepdims=True) + 1e-06)
        second[at, :] = (h * r * gain[...]).astype(BF)

    each_rows(fold.rows, norm)
    rows = Spread(cube, second, second_all, spread_s)
    rows.begin()
    for s in range(len(cube.bits)):
        rows.step(s)
    fold.end()
    rows.end()


def norm_back(values, gain, grad, base, out, gain_grad, at):
    v = values[at, :]
    g = grad[at, :]
    r = lax.rsqrt(jnp.mean(v * v, axis=-1, keepdims=True) + 1e-06)
    q = g * gain[...]
    back = base[at, :] + r * q - r * r * r * v * jnp.mean(q * v, axis=-1, keepdims=True)
    out[at, :] = back
    term = g * v * r
    gain_grad[...] += term[0:8, :] + term[8:16, :]
    return back


def middle_backward(n_lo, n_cx, part, hidden, out_grad, gain, hidden_grad, gain_grad, branch_all, mate_buf, *scratch):
    fold_s, rest = scratch[:N_FOLD], scratch[N_FOLD:]
    spread_s, (branch,) = rest[:N_SPREAD], rest[N_SPREAD:]
    cube = Group(n_lo, n_cx, True)
    plane = Group(n_lo, n_cx, False)
    meet(cube.partners() + [sibling()])
    fold = Fold(cube, part, mate_buf, fold_s)
    fold.begin()
    fold.pairs()
    for s in range(len(cube.bits)):
        fold.take(s)
    gain_grad[...] = jnp.zeros_like(gain_grad)

    def norm(at):
        branch[at, :] = norm_back(hidden, gain, fold.total, out_grad, hidden_grad, gain_grad, at).astype(BF)

    each_rows(fold.rows, norm)
    rows = Spread(plane, branch, branch_all, spread_s)
    rows.begin()
    for s in range(len(plane.bits)):
        rows.step(s)
    fold.end()
    rows.end()


class Chain:
    def __init__(self, z, count, part, blocks, came, sems, along):
        self.z, self.count, self.part, self.blocks, self.came, self.along = z, count, part, blocks, came, along
        self.load_sems, self.out_sems, self.in_sems = sems

    @staticmethod
    def scratch(parts, count, rows, cols):
        hops = 2 * (count - 1)
        return [pltpu.VMEM((count, rows, cols), BF), pltpu.VMEM((hops, rows, cols), BF)] + dma_sems(
            parts * count, hops, hops
        )

    def loads(self, d):
        first = 0
        for i, part in enumerate(self.part):
            cols = part.shape[2]
            dst = self.blocks.at[d, :, pl.ds(first, cols)] if len(self.part) > 1 else self.blocks.at[d]
            yield pltpu.make_async_copy(part.at[d], dst, self.load_sems.at[len(self.part) * d + i])
            first += cols

    def begin(self):
        for d in range(self.count):
            for copy in self.loads(d):
                copy.start()

    def ready(self):
        for d in range(self.count):
            for copy in self.loads(d):
                copy.wait()

    def sides(self, k):
        last = self.count - 1
        z = self.z
        yield 0, 1, jnp.logical_and(z <= k, z < last), jnp.logical_and(z >= 1, z <= k + 1)
        yield 1, -1, jnp.logical_and(z >= last - k, z > 0), jnp.logical_and(z <= last - 1, z >= last - 1 - k)

    def copy(self, side, way, k):
        at = side * (self.count - 1) + k
        block = self.blocks.at[self.z + way * (self.count - 1 - k)]
        return send(block, self.came.at[at], self.out_sems.at[at], self.in_sems.at[at], self.along(self.z + way))

    def start(self, k):
        for side, way, sends, _ in self.sides(k):
            @pl.when(sends)
            def _():
                self.copy(side, way, k).start()

    def take(self, k, total):
        final = k == self.count - 2
        for side, way, _, comes in self.sides(k):
            at = side * (self.count - 1) + k

            @pl.when(comes)
            def _():
                land = self.came.at[at]
                send(land, land, self.out_sems.at[at], self.in_sems.at[at], self.along(self.z - way)).wait_recv()

                def add(rows):
                    value = self.came[at, rows, :].astype(F32)
                    if final:
                        total[rows, :] += value
                    else:
                        spot = self.z + way * (self.count - 2 - k)
                        self.blocks[spot, rows, :] = (self.blocks[spot, rows, :].astype(F32) + value).astype(BF)

                each_rows(total.shape[0], add)

    def own(self, total):
        def put(rows):
            total[rows, :] = self.blocks[self.z, rows, :].astype(F32)

        each_rows(total.shape[0], put)

    def end(self):
        for k in range(self.count - 1):
            for side, way, sends, _ in self.sides(k):
                @pl.when(sends)
                def _():
                    self.copy(side, way, k).wait_send()


N_CHAIN = 5


def everywhere(n_hi, n_lo, n_cx):
    n_ctx = 2 * n_cx
    n_cube = n_lo * n_ctx
    number = (lax.axis_index("hi") * n_lo + lax.axis_index("lo")) * n_ctx + lax.axis_index("cxy") * 2
    number = number + lax.axis_index("core")

    def device(i):
        return {
            "hi": i // n_cube, "lo": lax.rem(i, n_cube) // n_ctx, "cxy": lax.rem(i, n_ctx) // 2, "core": lax.rem(i, 2),
        }

    return number, device, n_hi * n_cube


def meet_all(number, device, n_dev):
    barrier = pltpu.get_barrier_semaphore()

    def greet(i, held):
        other = device(lax.rem(number + i, n_dev))
        pl.semaphore_signal(barrier, inc=1, device_id=other, device_id_type=pl.DeviceIdType.MESH)
        return held

    lax.fori_loop(1, n_dev, greet, 0)
    pl.semaphore_wait(barrier, n_dev - 1)


def ff_block(u, n_lo, n_cx):
    lo, ctx = u // (2 * n_cx), u % (2 * n_cx)
    return (ctx % 2) * (n_lo * n_cx) + lo * n_cx + ctx // 2


class Exchange:
    def __init__(self, number, device, n_dev, src, came, sems, split):
        self.number, self.device, self.n_dev, self.split = number, device, n_dev, split
        self.src, self.came, (self.out_sems, self.in_sems) = src, came, sems

    def copy(self, i):
        to = lax.rem(self.number + i, self.n_dev)
        src = self.src.at[to] if self.split else self.src
        return send(src, self.came.at[self.number], self.out_sems.at[i], self.in_sems.at[i], self.device(to))

    def start(self):
        def run(i, held):
            self.copy(i).start()
            return held

        lax.fori_loop(1, self.n_dev, run, 0)

    def recv(self):
        def run(i, held):
            source = lax.rem(self.number - i + self.n_dev, self.n_dev)
            land = self.came.at[source]
            send(land, land, self.out_sems.at[i], self.in_sems.at[i], self.device(source)).wait_recv()
            return held

        lax.fori_loop(1, self.n_dev, run, 0)

    def end(self):
        def run(i, held):
            self.copy(i).wait_send()
            return held

        lax.fori_loop(1, self.n_dev, run, 0)


N_CHAIN = 5


def last_backward(n_lo, n_cx, n_hi, with_out, n_sums, part, *refs):
    sums, packed, refs = refs[:n_sums], refs[n_sums], refs[n_sums + 1 :]
    if with_out:
        (out_part, inputs, hidden_grad, gain, hidden, input_grad, gain_rows, packed_sum, summed, mate_a, output, mate_b,
         *scratch) = refs
    else:
        inputs, hidden_grad, gain, hidden, input_grad, gain_rows, packed_sum, summed, mate_a, *scratch = refs
    fold_a, rest = scratch[:N_FOLD], scratch[N_FOLD:]
    chain_s, rest = rest[:N_CHAIN], rest[N_CHAIN:]
    (pack_came, p_own, p_out, p_in), fold_b = rest[:4], rest[4:]
    cube = Group(n_lo, n_cx, True)
    plane = Group(n_lo, n_cx, False)
    n_dp = n_hi * n_lo
    z = lax.axis_index("hi") * n_lo + lax.axis_index("lo")
    along = lambda d: {"hi": d // n_lo, "lo": lax.rem(d, n_lo)}
    meet([cube.partner(b) for b in cube.near] + [sibling()] + [along(lax.rem(z + i, n_dp)) for i in range(1, n_dp)])
    first = Fold(plane, part, mate_a, fold_a)
    chain = Chain(z, n_dp, sums, chain_s[0], chain_s[1], chain_s[2:], along)
    chain.begin()
    first.begin()
    if with_out:
        outs = Fold(cube, out_part, mate_b, fold_b, "last")
        outs.begin()
    others = [lax.rem(z + i, n_dp) for i in range(1, n_dp)]
    pushes = [
        send(packed.at[d], pack_came.at[i + 1], p_out.at[i], p_in.at[i], along(d)) for i, d in enumerate(others)
    ]
    own_pack = pltpu.make_async_copy(packed.at[z], pack_came.at[0], p_own)
    own_pack.start()
    for push in pushes:
        push.start()
    hops = n_dp - 1
    chain.ready()
    chain.start(0)
    chain.own(summed)
    first.pairs()
    if with_out:
        outs.pairs()
    first.take(0)
    for k in range(hops - 1):
        chain.take(k, summed)
        chain.start(k + 1)
        if k + 1 < len(plane.bits):
            first.take(k + 1)
        if with_out and k + 1 < len(cube.bits):
            outs.take(k)
    for s in range(hops, len(plane.bits)):
        first.take(s)
    gain_rows[...] = jnp.zeros_like(gain_rows)

    def norm(at):
        norm_back(inputs, gain, first.total, hidden_grad, input_grad, gain_rows, at)

    each_rows(first.rows, norm)
    if with_out:
        for s in range(min(hops - 1, len(cube.bits) - 1), len(cube.bits)):
            outs.take(s)

        def finish(at):
            output[at, :] = hidden[at, :] + outs.total[at, :]

        each_rows(outs.rows, finish)
    own_pack.wait()
    value = pack_came[0]
    for i, push in enumerate(pushes):
        push.wait_recv()
        value = value + pack_came[i + 1]
    packed_sum[...] = value
    chain.take(hops - 1, summed)
    for push in pushes:
        push.wait_send()
    first.end()
    if with_out:
        outs.end()
    chain.end()


def comm_call(kernel, name, number, raw, args, outs, scratch, micros):
    any_spec = pl.BlockSpec(memory_space=pl.ANY)
    vmem = pl.BlockSpec(memory_space=pltpu.VMEM)
    return pl.pallas_call(
        kernel,
        in_specs=[any_spec] * len(raw) + [vmem] * len(args),
        out_specs=[vmem if inside else any_spec for _, inside in outs],
        out_shape=[shape for shape, _ in outs],
        scratch_shapes=scratch,
        compiler_params=pltpu.CompilerParams(
            collective_id=number, has_side_effects=True, vmem_limit_bytes=56 << 20
        ),
        cost_estimate=pl.CostEstimate(flops=micros * 10**9, bytes_accessed=micros * 10**6, transcendentals=0),
        name=name,
    )(*raw, *args)


def dma_sems(*counts):
    return [pltpu.SemaphoreType.DMA((n,) if n else ()) for n in counts]


def middle_forward_call(n_lo, n_cx, part, inputs, gain):
    tok, width = inputs.shape
    near = n_cx.bit_length() - 1
    far = near + n_lo - 1
    rows = jax.ShapeDtypeStruct((tok, width), F32)
    sds = lambda *shape: jax.ShapeDtypeStruct(shape, BF)
    hidden, second_all, _ = comm_call(
        functools.partial(middle_forward, n_lo, n_cx), "sum_norm_gather_forward", 1,
        (part.reshape(n_cx, 2, tok, width),), (inputs, gain),
        [(rows, True), (sds(n_lo * n_cx * 2, tok, width), False), (sds(n_cx, tok, width), False)],
        Fold.scratch(near, near, tok, width) + Spread.sems(far, far) + [pltpu.VMEM((tok, width), BF)], 1,
    )
    return hidden, second_all.reshape(-1, width)


def middle_backward_call(n_lo, n_cx, part, hidden, out_grad, gain):
    tok, width = hidden.shape
    near = n_cx.bit_length() - 1
    far = near + n_lo - 1
    rows = jax.ShapeDtypeStruct((tok, width), F32)
    sds = lambda *shape: jax.ShapeDtypeStruct(shape, BF)
    hidden_grad, gain_grad, branch_all, _ = comm_call(
        functools.partial(middle_backward, n_lo, n_cx), "sum_norm_gather_backward", 2,
        (part.reshape(n_lo * n_cx, 2, tok, width),), (hidden, out_grad, gain),
        [(rows, True), (jax.ShapeDtypeStruct((8, width), F32), True), (sds(n_cx * 2, tok, width), False),
         (sds(n_lo * n_cx, tok, width), False)],
        Fold.scratch(far, far, tok, width) + Spread.sems(near, near) + [pltpu.VMEM((tok, width), BF)], 100,
    )
    return hidden_grad, gain_grad, branch_all.reshape(-1, width)


def last_backward_call(n_hi, n_lo, n_cx, part, out_part, sums, packed, inputs, hidden_grad, gain, hidden):
    tok, width = inputs.shape
    near = n_cx.bit_length() - 1
    far = near + n_lo - 1
    n_dp = n_hi * n_lo
    with_out = n_lo * n_cx <= 8
    rows = jax.ShapeDtypeStruct((tok, width), F32)
    sds = lambda *shape: jax.ShapeDtypeStruct(shape, BF)
    full = lambda *shape: jax.ShapeDtypeStruct(shape, F32)
    if any(p.shape[1] % 128 for p in sums):
        sums = [jnp.concatenate(sums, axis=1)]
    sums = [p.reshape(n_dp, -1, p.shape[1]) for p in sums]
    summed_shape = (*sums[0].shape[1:2], sum(p.shape[2] for p in sums))
    packed = packed.reshape(n_dp, -1, packed.shape[1])
    raw = (part.reshape(n_cx, 2, tok, width), *sums, packed)
    outs = [(rows, True), (full(8, width), True), (full(*packed.shape[1:]), True), (full(*summed_shape), True),
            (sds(n_cx, tok, width), False)]
    scratch = Fold.scratch(near, near, tok, width) + Chain.scratch(len(sums), n_dp, *summed_shape)
    scratch += [pltpu.VMEM(packed.shape, F32)] + dma_sems(0, n_dp - 1, n_dp - 1)
    if with_out:
        raw += (out_part.reshape(n_lo * n_cx, 2, tok, width),)
        outs += [(rows, True), (sds(n_lo * n_cx, tok, width), False)]
        scratch += Fold.scratch(far, near, tok, width)
    got = comm_call(
        functools.partial(last_backward, n_lo, n_cx, n_hi, with_out, len(sums)), "sum_norm_backward", 3,
        raw, (inputs, hidden_grad, gain, hidden), outs, scratch, 100,
    )
    input_grad, gain_rows, packed_sum, summed = got[:4]
    if with_out:
        output = got[5]
    else:
        output = hidden + lax.psum_scatter(out_part, CUBE, scatter_dimension=0, tiled=True).astype(F32)
    return input_grad, gain_rows, packed_sum, output, summed


class Swap:
    def __init__(self, own, near_tmp, far_tmp, got, sems):
        self.own, self.near_tmp, self.far_tmp, self.got = own, near_tmp, far_tmp, got
        self.s1, self.r1, self.s2, self.r2 = sems
        hi, lo = lax.axis_index("hi"), lax.axis_index("lo")
        self.inner = hi + lo == 1
        self.outer = hi + lo != 1
        self.beside = {"lo": 1 - lo}
        self.over = {"hi": 1 - hi, "lo": 1 - lo}

    @staticmethod
    def sems():
        return dma_sems(0, 2, 2, 2)

    def first(self, action):
        for cond, land, spot, target in (
            (self.outer, self.near_tmp, 0, self.beside), (self.inner, self.far_tmp, 1, self.over)
        ):
            @pl.when(cond)
            def _():
                copy = send(self.own, land, self.s1, self.r1.at[spot], target)
                copy.start() if action == "start" else copy.wait_send()

    def arrived(self):
        @pl.when(self.inner)
        def _():
            send(self.near_tmp, self.near_tmp, self.s1, self.r1.at[0], self.beside).wait_recv()
            send(self.far_tmp, self.far_tmp, self.s1, self.r1.at[1], self.over).wait_recv()

    def second(self, action):
        @pl.when(self.inner)
        def _():
            for src, spot, target in ((self.near_tmp, 0, self.over), (self.far_tmp, 1, self.beside)):
                copy = send(src, self.got, self.s2.at[spot], self.r2.at[spot], target)
                copy.start() if action == "start" else copy.wait_send()

    def done(self):
        @pl.when(self.inner)
        def _():
            send(self.got, self.got, self.s2.at[0], self.r2.at[0], self.over).wait_recv()

        @pl.when(self.outer)
        def _():
            send(self.got, self.got, self.s2.at[1], self.r2.at[1], self.beside).wait_recv()


class Line:
    def __init__(self, n_hi, n_lo):
        self.n_lo = n_lo
        self.count = n_hi * n_lo
        self.z = lax.axis_index("hi") * n_lo + lax.axis_index("lo")

    def device(self, z):
        return {"hi": z // self.n_lo, "lo": lax.rem(z, self.n_lo)}

    def run(self, part, sems, k, action):
        out_sems, in_sems, pass_sems, mate_sems = sems
        last = self.count - 1
        z = self.z
        for side, way in ((0, 1), (1, -1)):
            if way == 1:
                sends = jnp.logical_and(z >= k, z < last)
                comes = z >= k + 1
            else:
                sends = jnp.logical_and(z <= last - k, z > 0)
                comes = z <= last - 1 - k
            at = side * last + k
            if action in ("recv", "mate_recv"):
                @pl.when(comes)
                def _():
                    if action == "recv":
                        plane = part(z - way * (k + 1), False)
                        send(plane, plane, out_sems.at[at], in_sems.at[at], self.device(z - way)).wait_recv()
                        if pass_sems is not None:
                            send(plane, plane, pass_sems.at[at], mate_sems.at[at], sibling()).start()
                    else:
                        plane = part(z - way * (k + 1), False)
                        send(plane, plane, pass_sems.at[at], mate_sems.at[at], sibling()).wait_send()
                        plane = part(z - way * (k + 1), True)
                        send(plane, plane, pass_sems.at[at], mate_sems.at[at], sibling()).wait_recv()
            else:
                @pl.when(sends)
                def _():
                    plane = part(z - way * k, False)
                    copy = send(plane, plane, out_sems.at[at], in_sems.at[at], self.device(z + way))
                    if action == "start":
                        copy.start()
                    else:
                        copy.wait_send()


def clamp_head(head, top):
    return head - head // (top + 1) * (head - top)


def window_head(c, own_ch, bw, span):
    return clamp_head(own_ch * c // bw, HEADS - span)


def chip_head(chip, own_ch, bw, span):
    return clamp_head(window_head(2 * chip, own_ch, bw, span), HEADS - span - 1)


def window_shard(head, n_dev, n_ctx, span):
    return head * ((n_dev - n_ctx) // (HEADS - span))


def gather_start(sizes, gelu_w, lin_w, proj, rgate, igate, small, down, gate_w, up_w, inputs,
                 gl_out, gu_out, pg_z, pg_win, normed_all, down_other, small_all, near_tmp, far_tmp,
                 gu_send, own_pg, own_gl, own_rest, gl_s, gl_r, mate_s, mate_r, gu_s, gu_r, win_s, win_r,
                 zp_s, zp_r, zg_s, zg_r, zm_s, zm_r, d0, d1, d2, d3,
                 normed, small_came, sm_own, sm_s, sm_r, *spread_s):
    n_hi, n_lo, n_cx, n_core, own_ch, bw, span = sizes
    n_ctx = n_cx * n_core
    n_cube = n_lo * n_ctx
    n_dev = n_hi * n_cube
    hi = lax.axis_index("hi")
    lo = lax.axis_index("lo")
    cx = lax.axis_index("cxy")
    core = lax.axis_index("core")
    ctx = cx * n_core + core
    spot = lo * n_ctx + ctx
    number = hi * n_cube + spot
    line = Line(n_hi, n_lo)
    z = line.z
    wide = (span + 1) * bw
    width = proj.shape[1]
    in_plane = lambda c: {"cxy": c // n_core, "core": lax.rem(c, n_core)}
    in_cube = lambda u: {"lo": u // n_ctx, **in_plane(lax.rem(u, n_ctx))}

    _, device, _ = everywhere(n_hi, n_lo, n_cx)
    meet_all(number, device, n_dev)
    vectors = Exchange(number, device, n_dev, small, small_came, (sm_s, sm_r), False)
    vectors.start()
    own_small = pltpu.make_async_copy(small, small_came.at[number], sm_own)
    own_small.start()

    pg_parts = [(proj, 0, width), (rgate, width, bw), (igate, width + bw, bw)]
    pg_own = [
        pltpu.make_async_copy(ref, pg_z.at[z, :, pl.ds(a, n)], own_pg.at[i]) for i, (ref, a, n) in enumerate(pg_parts)
    ]
    for copy in pg_own:
        copy.start()

    def columns(ref, chip):
        at = pl.multiple_of(chip_head(chip, own_ch, bw, span) * bw, bw)
        return ref.at[:, pl.ds(at, wide)]

    mine = lambda i: gl_out.at[z, cx, core, :, pl.ds(i * wide, wide)]
    gl_own = [pltpu.make_async_copy(columns(ref, cx), mine(i), own_gl.at[i]) for i, ref in enumerate((gelu_w, lin_w))]
    gl_copies = []
    for s in range(1, n_cx):
        to = lax.rem(cx + s, n_cx)
        for i, ref in enumerate((gelu_w, lin_w)):
            gl_copies.append(
                send(columns(ref, to), mine(i), gl_s.at[2 * s + i], gl_r.at[2 * s + i], {"cxy": to})
            )
            gl_copies[-1].start()
    for copy in gl_own:
        copy.start()
    pg_part = lambda plane, other: pg_z.at[plane]
    gl_part = lambda plane, other: gl_out.at[plane, :, 1 - core if other else core]
    pg_sems, gl_sems = (zp_s, zp_r, None, None), (zg_s, zg_r, zm_s, zm_r)
    steps = line.count - 1
    for copy in pg_own:
        copy.wait()
    line.run(pg_part, pg_sems, 0, "start")
    own_small.wait()
    vectors.recv()
    piece = width // n_dev
    for d in range(n_dev):
        small_all[:, d * piece : (d + 1) * piece] = small_came[d, :, 0:piece]
    gain = small_all[0:1, :].astype(F32)

    def norm(at):
        x = inputs[at, :]
        r = lax.rsqrt(jnp.mean(x * x, axis=-1, keepdims=True) + 1e-06)
        normed[at, :] = (x * r * gain).astype(BF)

    each_rows(normed.shape[0], norm)
    rows = Spread(Group(n_lo, n_cx, False), normed, normed_all, spread_s)
    rows.begin()
    for copy in gl_own:
        copy.wait()
    for s in range(1, n_cx):
        for i in range(2):
            came = gl_out.at[z, lax.rem(cx - s + n_cx, n_cx), core, :, pl.ds(i * wide, wide)]
            send(came, came, gl_s.at[2 * s + i], gl_r.at[2 * s + i], {"cxy": lax.rem(cx + s, n_cx)}).wait_recv()
    line.run(gl_part, gl_sems, 0, "start")
    own_plane = gl_part(z, False)
    own_mate = send(own_plane, own_plane, mate_s, mate_r, sibling())
    own_mate.start()

    ff_own = gate_w.shape[1] // n_cube
    ff_pad = gu_send.shape[2] // 2
    shard_rows = gate_w.shape[0]
    for u in range(n_cube):
        first = ff_block(u, n_lo, n_cx) * ff_own
        for i, ref in enumerate((gate_w, up_w)):
            gu_send[u, :, i * ff_pad : i * ff_pad + ff_own] = ref[:, first : first + ff_own]
            if ff_pad > ff_own:
                gu_send[u, :, i * ff_pad + ff_own : (i + 1) * ff_pad] = jnp.zeros((shard_rows, ff_pad - ff_own), BF)

    for k in range(1, steps):
        line.run(pg_part, pg_sems, k - 1, "recv")
        line.run(pg_part, pg_sems, k, "start")
    for s in range(len(rows.moves)):
        rows.step(s)
    line.run(pg_part, pg_sems, steps - 1, "recv")

    def window(src, dst):
        first = window_shard(window_head(dst, own_ch, bw, span), n_dev, n_ctx, span)
        turn = lax.rem(src - first + n_dev, n_ctx)
        return (first + turn) // n_ctx, turn

    shard, turn = window(ctx, ctx)
    own_window = pltpu.make_async_copy(pg_z.at[shard], pg_win.at[turn], own_rest.at[0])
    own_window.start()
    win_copies = []
    for s in range(1, n_ctx):
        to = lax.rem(ctx + s, n_ctx)
        shard, turn = window(ctx, to)
        win_copies.append(send(pg_z.at[shard], pg_win.at[turn], win_s.at[s], win_r.at[s], in_plane(to)))
        win_copies[-1].start()
    line.run(gl_part, gl_sems, 0, "recv")
    if steps > 1:
        line.run(gl_part, gl_sems, 1, "start")
    own_gu = pltpu.make_async_copy(gu_send.at[spot], gu_out.at[spot], own_rest.at[1])
    own_gu.start()
    gu_copies = []
    for s in range(1, n_cube):
        to = lax.rem(spot + s, n_cube)
        gu_copies.append(send(gu_send.at[to], gu_out.at[spot], gu_s.at[s], gu_r.at[s], in_cube(to)))
        gu_copies[-1].start()
    swap = Swap(down, near_tmp, far_tmp, down_other, (d0, d1, d2, d3))
    swap.first("start")
    for k in range(2, steps):
        line.run(gl_part, gl_sems, k - 1, "recv")
        line.run(gl_part, gl_sems, k, "start")
    swap.arrived()
    swap.second("start")
    line.run(gl_part, gl_sems, steps - 1, "recv")
    rows.end()
    for s in range(1, n_ctx):
        _, turn = window(lax.rem(ctx - s + n_ctx, n_ctx), ctx)
        came = pg_win.at[turn]
        send(came, came, win_s.at[s], win_r.at[s], in_plane(lax.rem(ctx + s, n_ctx))).wait_recv()
    for s in range(1, n_cube):
        came = gu_out.at[lax.rem(spot - s + n_cube, n_cube)]
        send(came, came, gu_s.at[s], gu_r.at[s], in_cube(lax.rem(spot + s, n_cube))).wait_recv()
    own_window.wait()
    own_gu.wait()
    for copy in gl_copies + win_copies + gu_copies:
        copy.wait_send()
    own_mate.wait_send()
    other_plane = gl_part(z, True)
    send(other_plane, other_plane, mate_s, mate_r, sibling()).wait_recv()
    for k in range(steps):
        line.run(pg_part, pg_sems, k, "sent")
        line.run(gl_part, gl_sems, k, "sent")
        line.run(gl_part, gl_sems, k, "mate_recv")
    swap.first("wait")
    swap.second("wait")
    swap.done()
    vectors.end()


def gather_start_call(sizes, gelu_w, lin_w, proj, rgate, igate, small, down, gate_w, up_w, inputs, ff_pad):
    n_hi, n_lo, n_cx, n_core, own_ch, bw, span = sizes
    n_ctx = n_cx * n_core
    n_cube = n_lo * n_ctx
    n_dp = n_hi * n_lo
    shard, width = proj.shape
    near = n_cx.bit_length() - 1
    wide = (span + 1) * bw
    sds = lambda *shape: jax.ShapeDtypeStruct(shape, BF)
    any_spec = pl.BlockSpec(memory_space=pl.ANY)
    vmem = pl.BlockSpec(memory_space=pltpu.VMEM)
    pg_width = width + 2 * bw
    hops = 2 * (n_dp - 1)
    gl_out, gu_out, _, pg_win, normed_all, down_other, small_all, _, _ = pl.pallas_call(
        functools.partial(gather_start, sizes),
        in_specs=[any_spec] * 7 + [vmem] * 3,
        out_specs=[any_spec] * 6 + [vmem] + [any_spec] * 2,
        out_shape=[
            sds(n_dp, n_cx, n_core, shard, 2 * wide), sds(n_cube, shard, 2 * ff_pad), sds(n_dp, shard, pg_width),
            sds(n_ctx, shard, pg_width), sds(n_ctx, *inputs.shape), sds(*down.shape),
            sds(small.shape[0], width), sds(*down.shape), sds(*down.shape),
        ],
        scratch_shapes=[pltpu.VMEM((n_cube, shard, 2 * ff_pad), BF)]
        + dma_sems(3, 2, 2, 2 * n_cx, 2 * n_cx, 0, 0, n_cube, n_cube, n_ctx, n_ctx, hops, hops, hops, hops, hops, hops)
        + Swap.sems() + [pltpu.VMEM(inputs.shape, BF), pltpu.VMEM((n_dp * n_ctx, *small.shape), BF)]
        + dma_sems(0, n_dp * n_ctx, n_dp * n_ctx) + Spread.sems(near, near),
        compiler_params=pltpu.CompilerParams(collective_id=4, has_side_effects=True, vmem_limit_bytes=40 << 20),
        cost_estimate=pl.CostEstimate(flops=10**11, bytes_accessed=10**8, transcendentals=0),
        name="gather_start",
    )(gelu_w, lin_w, proj, rgate, igate, small, down, gate_w, up_w, inputs)
    return gl_out.reshape(width, 2 * wide), gu_out.reshape(-1, 2 * ff_pad), pg_win.reshape(-1, pg_width), normed_all.reshape(-1, width), down_other, small_all


def swap_first(value):
    return lax.ppermute(value, DP, [(0, 1), (3, 2)]), lax.ppermute(value, DP, [(1, 2), (2, 1)])


def swap_second(to_inner, crossed):
    return lax.ppermute(to_inner, DP, [(1, 2), (2, 1)]), lax.ppermute(crossed, DP, [(1, 0), (2, 3)])


def pad_last(value, width):
    extra = width - value.shape[-1]
    return value if extra == 0 else jnp.pad(value, [(0, 0)] * (value.ndim - 1) + [(0, extra)])


def per_device(
    inputs, segment_ids, first_gain, gelu_in_w, linear_in_w, conv_weight, conv_bias, recur_gate_w, recur_gate_b,
    input_gate_w, input_gate_b, decay_param, out_proj_w, second_gain, mlp_gate_w, mlp_up_w, mlp_down_w, out_grad,
):
    n_hi, n_lo, n_cx, n_core = (lax.axis_size(a) for a in EVERY)
    hi, lo, cx, core = (lax.axis_index(a) for a in EVERY)
    n_ctx = n_cx * n_core
    n_dp = n_hi * n_lo
    n_dev = n_dp * n_ctx
    ctx = cx * n_core + core
    tok, width = inputs.shape
    tokens = segment_ids.shape[1]
    chans = linear_in_w.shape[1]
    bw = recur_gate_w.shape[1]
    hidden_units = mlp_gate_w.shape[1]
    own_ch = chans // n_ctx
    span = max((own_ch * (c + 1) - 1) // bw - own_ch * c // bw + 1 for c in range(n_ctx))
    win = span * bw
    head0 = window_head(ctx, own_ch, bw, span)
    ch0 = head0 * bw
    own_off = own_ch * ctx - ch0
    ff_own = hidden_units // (n_lo * n_ctx)
    ff_pad = -(-ff_own // 128) * 128

    piece = width // n_dev
    small = jnp.concatenate(
        [v[None] for v in (first_gain, second_gain)]
        + [conv_weight]
        + [v[None] for v in (conv_bias, recur_gate_b, input_gate_b, decay_param)],
        axis=0,
    )
    small = jnp.pad(small, ((0, 16 - small.shape[0]), (0, 128 - piece)))

    sizes = (n_hi, n_lo, n_cx, n_core, own_ch, bw, span)
    gl_w, gu_mine, pg_win, normed_all, down_other, small_all = gather_start_call(
        sizes, gelu_in_w, linear_in_w, out_proj_w, recur_gate_w, input_gate_w, small, mlp_down_w,
        mlp_gate_w, mlp_up_w, inputs, ff_pad,
    )
    small_all = small_all.astype(F32)
    gain_first = small_all[0]
    gain_second = small_all[1]
    wide = win + bw
    chip_off = (head0 - chip_head(cx, own_ch, bw, span)) * bw
    gelu_w = lax.dynamic_slice_in_dim(gl_w[:, :wide], chip_off, win, axis=1)
    lin_w = lax.dynamic_slice_in_dim(gl_w[:, wide:], chip_off, win, axis=1)
    pg_win = lax.dynamic_slice_in_dim(pg_win, ch0 - window_shard(head0, n_dev, n_ctx, span) * piece, win)
    proj_w = pg_win[:, :width]
    recur_w = pg_win[:, width : width + bw]
    input_w = pg_win[:, width + bw :]

    gu_other = lax.ppermute(gu_mine, "hi", SWAP)
    n_cube = n_lo * n_ctx
    keeps = hi == core
    down_keep = jnp.where(keeps, mlp_down_w, down_other)
    down_came = lax.ppermute(jnp.where(keeps, down_other, mlp_down_w), "core", SWAP)
    down_w = in_order(core, down_keep, down_came, 0)
    down_w = jnp.pad(down_w, ((0, ff_pad - ff_own), (0, 0)))
    cot = lax.optimization_barrier((out_grad.astype(BF), down_other))[0]
    down_grad = lax.all_gather(cot, CUBE, axis=0, tiled=True)

    ids = segment_ids[0]
    metas = [jnp.concatenate([jnp.ones((1,), F32), (ids[1:] != ids[:-1]).astype(F32)])]
    for k in range(1, CONV):
        metas.append(jnp.concatenate([jnp.zeros((k,), F32), (ids[k:] == ids[:-k]).astype(F32)]))
    meta = jnp.stack(metas, axis=1)
    vec_win = lax.dynamic_slice_in_dim(small_all[2:10], ch0, win, axis=1)
    decay_win = vec_win[7:8]
    place_in = jnp.arange(win) - own_off
    own_mask = ((place_in >= 0) & (place_in < own_ch)).astype(F32)[None]
    vecs = jnp.concatenate(
        [
            vec_win[:7],
            -8.0 * jax.nn.softplus(decay_win),
            own_mask,
            -8.0 * jax.nn.sigmoid(decay_win),
            jnp.zeros((6, win), F32),
        ],
        axis=0,
    )
    gelu_pre = dot(normed_all, gelu_w, 1, 0)
    linear_out = dot(normed_all, lin_w, 1, 0).astype(BF)
    mixed, prev, conv_out, rec, inp = forward_call(linear_out, gelu_pre, meta, vecs, recur_w, input_w)
    proj_part = dot(mixed, proj_w, 1, 0).astype(BF)
    hidden, second_all = middle_forward_call(n_lo, n_cx, proj_part, inputs, gain_second[None])
    gu_w = in_order(hi, gu_mine, gu_other, 0)

    pre = dot(second_all, gu_w, 1, 0)
    gate_pre, up_pre = pre[:, :ff_pad], pre[:, ff_pad:]
    act_grad = dot(down_grad, down_w, 1, 1)
    gel, slope = gelu_parts(gate_pre)
    activation = (gel * up_pre).astype(BF)
    gu_low = jnp.concatenate([(act_grad * up_pre * slope).astype(BF), (act_grad * gel).astype(BF)], axis=1)
    second_part = dot(gu_low, gu_w, 1, 1).astype(BF)

    def half_of(partial, which, axis, parts):
        size = partial.shape[axis] // parts
        return lax.dynamic_slice_in_dim(partial, which * size, size, axis)

    gu_stage = swap_first(dot(half_of(second_all, 1 - hi, 1, n_hi), gu_low, 0, 0).astype(BF))
    dn_stage = swap_first(dot(activation, half_of(down_grad, 1 - hi, 1, n_hi), 0, 0).astype(BF))
    hidden_grad, gain_two_rows, branch_all = middle_backward_call(
        n_lo, n_cx, second_part, hidden, out_grad, gain_second[None]
    )

    branch_all, *stages = lax.optimization_barrier((branch_all,) + gu_stage + dn_stage)
    dn_stage = swap_second(*stages[2:])
    gu_stage = swap_second(*stages[:2])
    inner = hi != lo

    late_second, late_cot = lax.optimization_barrier((second_all, down_grad, branch_all))[:2]
    own_gu = dot(half_of(late_second, hi, 1, n_hi), gu_low, 0, 0).astype(BF)
    own_dn = dot(activation, half_of(late_cot, hi, 1, n_hi), 0, 0).astype(BF)

    turns = [
        [
            (u, ((u % n_ctx // 2 + s) % 2) * n_ctx + ff_block(u, n_lo, n_cx) // 2)
            for u in range(n_cube)
        ]
        for s in range(2)
    ]

    def both_halves(partial, got):
        return (partial.astype(F32) + got.astype(F32)).astype(BF)

    def settle(both, axis):
        odd = lax.rem(cx, 2)
        return tuple(lax.ppermute(half_of(both, lax.rem(odd + s, 2), axis, n_lo), CUBE, turns[s]) for s in range(2))

    out_part = dot(activation, lax.optimization_barrier((down_w, gain_two_rows))[0], 1, 0).astype(BF)

    own_mixed = lax.dynamic_slice_in_dim(mixed, own_off, own_ch, axis=1)
    grad_proj = dot(own_mixed, branch_all, 0, 0).astype(BF).reshape(own_ch, n_ctx, width // n_ctx)
    grad_proj = grad_proj.transpose(1, 0, 2)
    mixed_grad = dot(branch_all, proj_w, 1, 1)
    mixed_grad, own_gu, own_dn, out_part, grad_proj = lax.optimization_barrier(
        (mixed_grad, own_gu, own_dn, out_part, grad_proj)
    )
    grad_proj = exchange(grad_proj, CTX).reshape(chans, width // n_ctx)
    gelu_low, linear_low, recur_wg, input_wg, sums = backward_call(
        mixed_grad, gelu_pre, conv_out, rec, inp, prev, linear_out, meta, vecs, recur_w, input_w
    )
    gelu_low, linear_low, *stages = lax.optimization_barrier((gelu_low, linear_low, *dn_stage))
    got_dn = jnp.where(inner, *stages[:2])
    own_lows = jnp.concatenate(
        [
            lax.dynamic_slice_in_dim(gelu_low, own_off, own_ch, axis=1),
            lax.dynamic_slice_in_dim(linear_low, own_off, own_ch, axis=1),
        ],
        axis=1,
    )
    grad_gl = dot(normed_all, own_lows, 0, 0).astype(BF)
    first_part = dot(
        jnp.concatenate([gelu_low, linear_low], axis=1), jnp.concatenate([gelu_w, lin_w], axis=1), 1, 1
    ).astype(BF)
    first_part, grad_gl, *gu_stage = lax.optimization_barrier((first_part, grad_gl, *gu_stage))
    got_gu = jnp.where(inner, *gu_stage)
    dn_a, dn_b = settle(both_halves(own_dn, got_dn), 1)
    gu_sum = both_halves(own_gu, got_gu)
    first_part, dn_a, dn_b, gu_sum = lax.optimization_barrier((first_part, dn_a, dn_b, gu_sum))
    gu_a, gu_b = settle(gu_sum, 0)
    packed = jnp.concatenate([recur_wg, input_wg, pad_last(sums.T, 128)], axis=1)
    packed = lax.dynamic_slice_in_dim(packed, own_off, own_ch, axis=0)
    input_grad, gain_one_rows, packed, output, grad_three = last_backward_call(
        n_hi, n_lo, n_cx, first_part, out_part, (grad_gl, grad_proj), packed, inputs, hidden_grad, gain_first[None], hidden
    )
    gain_one_rows, gu_a, gu_b = lax.optimization_barrier((gain_one_rows, gu_a, gu_b))
    routes = [(d * n_ctx + c, c * n_dp + d) for d in range(n_dp) for c in range(n_ctx)]
    packed = lax.ppermute(packed, EVERY, routes)
    grad_gl = grad_three[:, : 2 * own_ch]
    grad_proj = grad_three[:, 2 * own_ch :]
    grad_gate = in_order(lo, gu_a[:, :ff_own], gu_b[:, :ff_own], 1).astype(F32)
    grad_up = in_order(
        lo, gu_a[:, ff_pad : ff_pad + ff_own], gu_b[:, ff_pad : ff_pad + ff_own], 1
    ).astype(F32)
    grad_dn = in_order(lo, dn_a[:ff_own], dn_b[:ff_own], 0).astype(F32)

    grad_recur_w = packed[:, :bw]
    grad_input_w = packed[:, bw : 2 * bw]
    rest = packed[:, 2 * bw : 2 * bw + 8].T
    gains = jnp.stack([jnp.sum(gain_one_rows, axis=0), jnp.sum(gain_two_rows, axis=0)])
    gains = jnp.sum(exchange(gains.reshape(2, n_dev, piece).transpose(1, 0, 2), EVERY), axis=0)

    return (
        output,
        input_grad,
        gains[0],
        grad_gl[:, :own_ch],
        grad_gl[:, own_ch:],
        rest[:CONV],
        rest[4],
        grad_recur_w,
        rest[5],
        grad_input_w,
        rest[6],
        rest[7],
        grad_proj,
        gains[1],
        grad_gate,
        grad_up,
        grad_dn,
    )


def solution(mesh):
    n_dp = mesh.shape["dp"]
    n_ctx = mesh.shape["context"]
    inner = Mesh(mesh.devices.reshape(2, n_dp // 2, n_ctx // 2, 2), EVERY)
    rows = P(EVERY, None)
    vec = P(EVERY)
    return jax.shard_map(
        per_device,
        mesh=inner,
        in_specs=(
            rows, P(DP, None), vec, rows, rows, P(None, EVERY), vec, rows, vec, rows, vec, vec, rows, vec,
            rows, rows, rows, rows,
        ),
        out_specs=(
            rows, rows, vec, P(DP, CTX), P(DP, CTX), P(None, EVERY), vec, rows, vec, rows, vec, vec,
            P(DP, CTX), vec, P(DP, CTX), P(DP, CTX), P(CTX, DP),
        ),
        check_vma=False,
    )
```
